32 devices in a mesh: dp: 32 (over z, y, x, core).
Axes of the slice: x: 2, y: 2, z: 4, core: 2. Of those that a mesh axis runs over, the one named last changes fastest.
Arguments:
- tokens: bfloat16 [32, 1024, 768], P('dp'), may hold values from -6 to 6
- memory: bfloat16 [32, 1024, 768], P('dp'), may hold values from -6 to 6
- out_grad: bfloat16 [32, 1024, 768], P('dp'), may hold values from -6 to 6
- dec_len: int32 [32], P('dp'), may hold values from 192 to 1024, as said below
- mem_len: int32 [32], P('dp'), may hold values from 512 to 1024, as said below
- group_bounds: int32 [5], replicated, may hold values from 0 to 32, as said below
- self_norm_gain: float32 [768], replicated, may hold values from 0.5 to 1.5
- self_norm_bias: float32 [768], replicated, may hold values from -1.2 to 1.2
- self_query: bfloat16 [768, 768], replicated, may hold values from -0.21875 to 0.21875
- self_query_bias: float32 [768], replicated, may hold values from -1.2 to 1.2
- self_key: bfloat16 [768, 768], replicated, may hold values from -0.21875 to 0.21875
- self_value: bfloat16 [768, 768], replicated, may hold values from -0.21875 to 0.21875
- self_value_bias: float32 [768], replicated, may hold values from -1.2 to 1.2
- self_output: bfloat16 [768, 768], replicated, may hold values from -0.875 to 0.875
- self_output_bias: float32 [768], replicated, may hold values from -1.2 to 1.2
- position_bias: float32 [12, 256], replicated, may hold values from -3 to 3
- head_scale: float32 [12], replicated, may hold values from 0.5 to 1.5
- self_post_gain: float32 [768], replicated, may hold values from 0.5 to 1.5
- self_post_bias: float32 [768], replicated, may hold values from -1.2 to 1.2
- cross_norm_gain: float32 [768], replicated, may hold values from 0.5 to 1.5
- cross_norm_bias: float32 [768], replicated, may hold values from -1.2 to 1.2
- cross_query: bfloat16 [768, 768], replicated, may hold values from -0.21875 to 0.21875
- cross_query_bias: float32 [768], replicated, may hold values from -1.2 to 1.2
- cross_key: bfloat16 [768, 768], replicated, may hold values from -0.21875 to 0.21875
- cross_value: bfloat16 [768, 768], replicated, may hold values from -0.21875 to 0.21875
- cross_value_bias: float32 [768], replicated, may hold values from -1.2 to 1.2
- cross_output: bfloat16 [768, 768], replicated, may hold values from -0.875 to 0.875
- cross_output_bias: float32 [768], replicated, may hold values from -1.2 to 1.2
- cross_post_gain: float32 [768], replicated, may hold values from 0.5 to 1.5
- cross_post_bias: float32 [768], replicated, may hold values from -1.2 to 1.2
- feed_norm_gain: float32 [768], replicated, may hold values from 0.5 to 1.5
- feed_norm_bias: float32 [768], replicated, may hold values from -1.2 to 1.2
- feed_inner: bfloat16 [768, 3072], replicated, may hold values from -0.21875 to 0.21875
- feed_inner_bias: float32 [3072], replicated, may hold values from -3 to 3
- feed_mid_gain: float32 [3072], replicated, may hold values from 0.5 to 1.5
- feed_mid_bias: float32 [3072], replicated, may hold values from -1.2 to 1.2
- feed_outer: bfloat16 [3072, 768], replicated, may hold values from -0.109375 to 0.109375
- feed_outer_bias: float32 [768], replicated, may hold values from -1.2 to 1.2
Outputs:
- layer_out: bfloat16 [32, 1024, 768], P('dp')
- grad_tokens: float32 [32, 1024, 768], P('dp')
- grad_memory: float32 [32, 1024, 768], P('dp')
- grad_self_norm_gain: float32 [768], P('dp')
- grad_self_norm_bias: float32 [768], P('dp')
- grad_self_query: float32 [768, 768], P('dp')
- grad_self_query_bias: float32 [768], P('dp')
- grad_self_key: float32 [768, 768], P('dp')
- grad_self_value: float32 [768, 768], P('dp')
- grad_self_value_bias: float32 [768], P('dp')
- grad_self_output: float32 [768, 768], P('dp')
- grad_self_output_bias: float32 [768], P('dp')
- grad_position_bias: float32 [12, 256], P(None, 'dp')
- grad_head_scale: float32 [12], replicated
- grad_self_post_gain: float32 [768], P('dp')
- grad_self_post_bias: float32 [768], P('dp')
- grad_cross_norm_gain: float32 [768], P('dp')
- grad_cross_norm_bias: float32 [768], P('dp')
- grad_cross_query: float32 [768, 768], P('dp')
- grad_cross_query_bias: float32 [768], P('dp')
- grad_cross_key: float32 [768, 768], P('dp')
- grad_cross_value: float32 [768, 768], P('dp')
- grad_cross_value_bias: float32 [768], P('dp')
- grad_cross_output: float32 [768, 768], P('dp')
- grad_cross_output_bias: float32 [768], P('dp')
- grad_cross_post_gain: float32 [768], P('dp')
- grad_cross_post_bias: float32 [768], P('dp')
- grad_feed_norm_gain: float32 [768], P('dp')
- grad_feed_norm_bias: float32 [768], P('dp')
- grad_feed_inner: float32 [768, 3072], P('dp')
- grad_feed_inner_bias: float32 [3072], P('dp')
- grad_feed_mid_gain: float32 [3072], P('dp')
- grad_feed_mid_bias: float32 [3072], P('dp')
- grad_feed_outer: float32 [3072, 768], P('dp')
- grad_feed_outer_bias: float32 [768], P('dp')
The draws below stay inside these ranges and needn't reach their ends.
Inputs may be any that keep to these rules, and one draw needn't show every extreme that they name: `group_bounds`: Increasing; entry 0 is 0 and the last entry is the number of devices; every task group holds one device or more, group k the devices from entry k to entry k + 1 minus one. `dec_len`: the rows beyond an item's length are padding. `mem_len`: the rows beyond an item's length are padding.
All inputs are finite; a program needn't handle non-finite values.
Results may differ from the reference program's by a relative error of at most 0.028.
Values sent between devices are 32-bit elements; how exact they have to be, the bound alone decides.
No kernel may reach another device: no remote copies, remote signals or barrier semaphores. Data moves between devices by JAX's collectives and lax.ppermute only.
A program may use at most 448 MiB of HBM per device.

```python
import jax
import jax.numpy as jnp
from jax import lax

D = 768
HEADS = 12
HD = 64
FF = 3072
NB = 256
TASKS = 4
DEC = 1024
MEM = 1024
ITEMS_DEV = 1
ITEMS = 32
N_DP = 32


def group_cuts(key):
    device_total = ITEMS // ITEMS_DEV
    chosen = jax.random.permutation(jax.random.fold_in(key, 11), device_total - 1)[:TASKS - 1] + 1
    middle_cuts = jnp.sort(chosen).astype(jnp.int32)
    return jnp.concatenate([jnp.zeros((1,), jnp.int32), middle_cuts, jnp.full((1,), device_total, jnp.int32)])


def draw_group_bounds(key, part):
    return group_cuts(key)


def draw_dec_len(key, part):
    bounds = group_cuts(key)
    device_of = jnp.arange(ITEMS, dtype=jnp.int32) // ITEMS_DEV
    task_of = jnp.sum((device_of[:, None] >= bounds[None, 1:TASKS]).astype(jnp.int32), axis=1)
    upper_limit = DEC * (task_of + 1) // TASKS
    slack_rows = jax.random.randint(jax.random.fold_in(key, 12), (ITEMS,), 0, upper_limit // 4 + 1)
    lengths = (upper_limit - slack_rows).at[ITEMS - 1].set(DEC)
    return lengths.astype(jnp.int32)


def draw_mem_len(key, part):
    lengths = jax.random.randint(jax.random.fold_in(key, 13), (ITEMS,), MEM // 2, MEM + 1)
    return lengths.at[0].set(MEM).astype(jnp.int32)


def block_levels(stream_key, extent, shards, least, top_value):
    loudness = 1.0
    for position, blocks in shards:
        steps = jax.random.uniform(jax.random.fold_in(jax.random.fold_in(stream_key, 6), position), (blocks,), jnp.float32, least / len(shards), top_value / len(shards))
        loudness = loudness * jnp.repeat(jnp.exp(steps), extent[position] // blocks).reshape((-1,) + (1,) * (len(extent) - 1 - position))
    return loudness


def gaussian(key, shape, deviation, reach, shards=(), held_as=jnp.bfloat16):
    level = block_levels(key, shape, shards, -0.22, 0.18) if shards else 1.0
    drawn = jax.random.normal(key, shape, jnp.float32) * deviation * level
    return jnp.minimum(jnp.maximum(drawn, -reach), reach).astype(held_as)


def setup_inputs(seed: int = 0) -> dict:
    streams_of = jax.random.split(jax.random.key(seed), 39)
    return {
        "tokens": gaussian(streams_of[0], (ITEMS, DEC, D), 1.0, 6.0, ((0, 32),)),
        "memory": gaussian(streams_of[1], (ITEMS, MEM, D), 1.0, 6.0, ((0, 32),)),
        "out_grad": gaussian(streams_of[2], (ITEMS, DEC, D), 1.0, 6.0, ((0, 32),)),
        "dec_len": draw_dec_len(jax.random.fold_in(streams_of[38], 71), 0),
        "mem_len": draw_mem_len(jax.random.fold_in(streams_of[38], 71), 0),
        "group_bounds": draw_group_bounds(jax.random.fold_in(streams_of[38], 71), 0),
        "self_norm_gain": jnp.clip(1.0 + 0.1 * jax.random.normal(streams_of[6], (D,), jnp.float32), 0.5, 1.5),
        "self_norm_bias": gaussian(streams_of[7], (D,), 0.2, 1.2, (), jnp.float32),
        "self_query": gaussian(streams_of[8], (D, D), D ** -0.5, 0.21875),
        "self_query_bias": gaussian(streams_of[9], (D,), 0.2, 1.2, (), jnp.float32),
        "self_key": gaussian(streams_of[10], (D, D), D ** -0.5, 0.21875),
        "self_value": gaussian(streams_of[11], (D, D), D ** -0.5, 0.21875),
        "self_value_bias": gaussian(streams_of[12], (D,), 0.2, 1.2, (), jnp.float32),
        "self_output": gaussian(streams_of[13], (D, D), (D // 16) ** -0.5, 0.875),
        "self_output_bias": gaussian(streams_of[14], (D,), 0.2, 1.2, (), jnp.float32),
        "position_bias": gaussian(streams_of[15], (HEADS, NB), 0.5, 3.0, (), jnp.float32),
        "head_scale": jnp.clip(jax.random.uniform(streams_of[16], (HEADS,), jnp.float32, 0.5, 1.5), 0.5, 1.5),
        "self_post_gain": jnp.clip(1.0 + 0.1 * jax.random.normal(streams_of[17], (D,), jnp.float32), 0.5, 1.5),
        "self_post_bias": gaussian(streams_of[18], (D,), 0.2, 1.2, (), jnp.float32),
        "cross_norm_gain": jnp.clip(1.0 + 0.1 * jax.random.normal(streams_of[19], (D,), jnp.float32), 0.5, 1.5),
        "cross_norm_bias": gaussian(streams_of[20], (D,), 0.2, 1.2, (), jnp.float32),
        "cross_query": gaussian(streams_of[21], (D, D), D ** -0.5, 0.21875),
        "cross_query_bias": gaussian(streams_of[22], (D,), 0.2, 1.2, (), jnp.float32),
        "cross_key": gaussian(streams_of[23], (D, D), D ** -0.5, 0.21875),
        "cross_value": gaussian(streams_of[24], (D, D), D ** -0.5, 0.21875),
        "cross_value_bias": gaussian(streams_of[25], (D,), 0.2, 1.2, (), jnp.float32),
        "cross_output": gaussian(streams_of[26], (D, D), (D // 16) ** -0.5, 0.875),
        "cross_output_bias": gaussian(streams_of[27], (D,), 0.2, 1.2, (), jnp.float32),
        "cross_post_gain": jnp.clip(1.0 + 0.1 * jax.random.normal(streams_of[28], (D,), jnp.float32), 0.5, 1.5),
        "cross_post_bias": gaussian(streams_of[29], (D,), 0.2, 1.2, (), jnp.float32),
        "feed_norm_gain": jnp.clip(1.0 + 0.1 * jax.random.normal(streams_of[30], (D,), jnp.float32), 0.5, 1.5),
        "feed_norm_bias": gaussian(streams_of[31], (D,), 0.2, 1.2, (), jnp.float32),
        "feed_inner": gaussian(streams_of[32], (D, FF), D ** -0.5, 0.21875),
        "feed_inner_bias": gaussian(streams_of[33], (FF,), 0.5, 3.0, (), jnp.float32),
        "feed_mid_gain": jnp.clip(1.0 + 0.1 * jax.random.normal(streams_of[34], (FF,), jnp.float32), 0.5, 1.5),
        "feed_mid_bias": gaussian(streams_of[35], (FF,), 0.2, 1.2, (), jnp.float32),
        "feed_outer": gaussian(streams_of[36], (FF, D), FF ** -0.5, 0.109375),
        "feed_outer_bias": gaussian(streams_of[37], (D,), 0.2, 1.2, (), jnp.float32),
    }


EPSILON = 1e-05
HIGHEST = lax.Precision.HIGHEST
MASKED_SCORE = -1e+30
PARAM_NAMES = ('self_norm_gain', 'self_norm_bias', 'self_query', 'self_query_bias', 'self_key', 'self_value', 'self_value_bias', 'self_output', 'self_output_bias', 'position_bias', 'head_scale', 'self_post_gain', 'self_post_bias', 'cross_norm_gain', 'cross_norm_bias', 'cross_query', 'cross_query_bias', 'cross_key', 'cross_value', 'cross_value_bias', 'cross_output', 'cross_output_bias', 'cross_post_gain', 'cross_post_bias', 'feed_norm_gain', 'feed_norm_bias', 'feed_inner', 'feed_inner_bias', 'feed_mid_gain', 'feed_mid_bias', 'feed_outer', 'feed_outer_bias')

@jax.custom_vjp
def low(v):
    return lax.optimization_barrier(v.astype(jnp.bfloat16)).astype(jnp.float32)

@jax.custom_vjp
def low_back(v):
    return v

def low_keep(v):
    return (low(v), None)

def low_pass(kept, grad):
    return (grad,)

def back_keep(v):
    return (v, None)

def back_low(kept, grad):
    return (low(grad),)
low.defvjp(low_keep, low_pass)
low_back.defvjp(back_keep, back_low)

def matmul(left_side, right_side):
    return jnp.dot(left_side, right_side, precision=HIGHEST)

def layer_norm(values_in, norm_gain, norm_bias):
    center = values_in - lax.optimization_barrier(jnp.mean(values_in, axis=-1, keepdims=True))
    spread = lax.optimization_barrier(jnp.mean(center * center, axis=-1, keepdims=True))
    return center * lax.rsqrt(spread + EPSILON) * norm_gain + norm_bias

def split_heads(values_in):
    return values_in.reshape(values_in.shape[0], HEADS, HD)

def attend(queries, keys_in, values_in, extra_bias, allowed):
    scores = low_back(jnp.einsum('qhd,khd->hqk', split_heads(queries), split_heads(keys_in), precision=HIGHEST) + extra_bias)
    scores = jnp.where(allowed[None], scores, MASKED_SCORE)
    shifted = scores - lax.optimization_barrier(jnp.max(scores, axis=-1, keepdims=True))
    exponent = jnp.exp(shifted)
    probability = exponent / lax.optimization_barrier(jnp.sum(exponent, axis=-1, keepdims=True))
    mixed_heads = jnp.einsum('hqk,khd->qhd', low(probability), split_heads(values_in), precision=HIGHEST)
    return low_back(mixed_heads)

def layer_forward(weights, token_rows, memory_rows, limit_dec, limit_mem):
    positions = jnp.arange(DEC, dtype=jnp.int32)
    distance = positions[:, None] - positions[None, :]
    self_allowed = (distance >= 0) & (positions[None, :] < limit_dec)
    cross_allowed = jnp.broadcast_to(jnp.arange(MEM, dtype=jnp.int32)[None, :] < limit_mem, (DEC, MEM))
    extra_bias = weights['position_bias'][:, jnp.clip(distance, 0, NB - 1)]
    normed = low(layer_norm(token_rows, weights['self_norm_gain'], weights['self_norm_bias']))
    queries = low(low_back((matmul(normed, weights['self_query']) + weights['self_query_bias']) * 0.125))
    keys_self = low(low_back(matmul(normed, weights['self_key'])))
    values_self = low(low_back(matmul(normed, weights['self_value']) + weights['self_value_bias']))
    mixed_heads = attend(queries, keys_self, values_self, extra_bias, self_allowed)
    scaled = low((mixed_heads * weights['head_scale'][None, :, None]).reshape(DEC, D))
    branch = low_back(matmul(scaled, weights['self_output']) + weights['self_output_bias'])
    first_sum = token_rows + layer_norm(branch, weights['self_post_gain'], weights['self_post_bias'])
    normed = low(layer_norm(first_sum, weights['cross_norm_gain'], weights['cross_norm_bias']))
    queries = low(low_back((matmul(normed, weights['cross_query']) + weights['cross_query_bias']) * 0.125))
    keys_cross = low(low_back(matmul(memory_rows, weights['cross_key'])))
    values_cross = low(low_back(matmul(memory_rows, weights['cross_value']) + weights['cross_value_bias']))
    mixed_heads = attend(queries, keys_cross, values_cross, 0.0, cross_allowed)
    branch = low_back(matmul(low(mixed_heads.reshape(DEC, D)), weights['cross_output']) + weights['cross_output_bias'])
    second = first_sum + layer_norm(branch, weights['cross_post_gain'], weights['cross_post_bias'])
    normed = low(layer_norm(second, weights['feed_norm_gain'], weights['feed_norm_bias']))
    hidden = low_back(matmul(normed, weights['feed_inner']) + weights['feed_inner_bias'])
    middle = low(layer_norm(jax.nn.gelu(hidden, approximate=False), weights['feed_mid_gain'], weights['feed_mid_bias']))
    branch = low_back(matmul(middle, weights['feed_outer']) + weights['feed_outer_bias'])
    return second + branch

def reference(tokens, memory, out_grad, dec_len, mem_len, group_bounds, self_norm_gain, self_norm_bias, self_query, self_query_bias, self_key, self_value, self_value_bias, self_output, self_output_bias, position_bias, head_scale, self_post_gain, self_post_bias, cross_norm_gain, cross_norm_bias, cross_query, cross_query_bias, cross_key, cross_value, cross_value_bias, cross_output, cross_output_bias, cross_post_gain, cross_post_bias, feed_norm_gain, feed_norm_bias, feed_inner, feed_inner_bias, feed_mid_gain, feed_mid_bias, feed_outer, feed_outer_bias):
    weights = dict(zip(PARAM_NAMES, [tensor.astype(jnp.float32) for tensor in (self_norm_gain, self_norm_bias, self_query, self_query_bias, self_key, self_value, self_value_bias, self_output, self_output_bias, position_bias, head_scale, self_post_gain, self_post_bias, cross_norm_gain, cross_norm_bias, cross_query, cross_query_bias, cross_key, cross_value, cross_value_bias, cross_output, cross_output_bias, cross_post_gain, cross_post_bias, feed_norm_gain, feed_norm_bias, feed_inner, feed_inner_bias, feed_mid_gain, feed_mid_bias, feed_outer, feed_outer_bias)]))
    device_of = jnp.arange(ITEMS, dtype=jnp.int32) // ITEMS_DEV
    task_of = lax.optimization_barrier(jnp.sum((device_of[:, None] >= group_bounds[None, 1:TASKS]).astype(jnp.int32), axis=1))
    task_onehot = (task_of[:, None] == jnp.arange(TASKS, dtype=jnp.int32)[None, :]).astype(jnp.float32)
    counts = lax.optimization_barrier(jnp.sum(task_onehot * dec_len.astype(jnp.float32)[:, None], axis=0))
    factor_of = N_DP / lax.optimization_barrier(jnp.sum(task_onehot * counts[None, :], axis=1))
    zeros_tree = jax.tree.map(jnp.zeros_like, weights)

    def one_item(running, inputs):
        token_rows, memory_rows, grad_rows, limit_dec, limit_mem, factor = inputs

        def forward_only(weight_tree, token_values, memory_values):
            return layer_forward(weight_tree, token_values, memory_values, limit_dec, limit_mem)
        result, pullback = jax.vjp(forward_only, weights, token_rows.astype(jnp.float32), memory_rows.astype(jnp.float32))
        valid_rows = (jnp.arange(DEC, dtype=jnp.int32) < limit_dec)[:, None]
        weight_grads, token_grad, memory_grad = pullback(jnp.where(valid_rows, grad_rows.astype(jnp.float32), 0.0))
        running = jax.tree.map(lambda summed, update: summed + factor * update, running, weight_grads)
        return (running, (jnp.where(valid_rows, result, 0.0).astype(jnp.bfloat16), token_grad, memory_grad))
    totals, (layer_out, grad_tokens, grad_memory) = lax.scan(one_item, zeros_tree, (tokens, memory, out_grad, dec_len, mem_len, factor_of))
    return (layer_out, grad_tokens, grad_memory, totals['self_norm_gain'], totals['self_norm_bias'], totals['self_query'], totals['self_query_bias'], totals['self_key'], totals['self_value'], totals['self_value_bias'], totals['self_output'], totals['self_output_bias'], totals['position_bias'], totals['head_scale'], totals['self_post_gain'], totals['self_post_bias'], totals['cross_norm_gain'], totals['cross_norm_bias'], totals['cross_query'], totals['cross_query_bias'], totals['cross_key'], totals['cross_value'], totals['cross_value_bias'], totals['cross_output'], totals['cross_output_bias'], totals['cross_post_gain'], totals['cross_post_bias'], totals['feed_norm_gain'], totals['feed_norm_bias'], totals['feed_inner'], totals['feed_inner_bias'], totals['feed_mid_gain'], totals['feed_mid_bias'], totals['feed_outer'], totals['feed_outer_bias'])
```

```python
import functools
import jax, jax.numpy as jnp
from jax import lax
from jax.experimental import pallas as pl
from jax.experimental.pallas import tpu as pltpu
from jax.sharding import PartitionSpec as P
F32=jnp.float32; BF=jnp.bfloat16
LOG2E=1.4426950408889634
NEG=-1e30
TILE=256
SMEM=pl.BlockSpec(memory_space=pltpu.SMEM)
def cost(flops,nbytes,trans=0):
    return pl.CostEstimate(flops=int(flops)*200,bytes_accessed=int(nbytes)*200,transcendentals=int(trans))
def nt(a,b): return lax.dot_general(a,b,(((1,),(1,)),((),())),preferred_element_type=F32)
def nn(a,b): return lax.dot_general(a,b,(((1,),(0,)),((),())),preferred_element_type=F32)
def tn(a,b): return lax.dot_general(a,b,(((0,),(0,)),((),())),preferred_element_type=F32)
def params(n, mb=56, sem=None):
    return pltpu.CompilerParams(dimension_semantics=("arbitrary",)*n, vmem_limit_bytes=mb<<20)

def head_lanes(rows, h):
    lane=lax.broadcasted_iota(jnp.int32,(rows,128),1)
    return (lane<64) if h==0 else (lane>=64)

def mask_keys(k, limit, h):
    rows=k.shape[0]
    lane=lax.broadcasted_iota(jnp.int32,(rows,128),1)
    row=lax.broadcasted_iota(jnp.int32,(rows,128),0)
    spare=64 if h==0 else 0
    pen=jnp.where((lane==spare)&(row>=limit), NEG, 0.0)
    own=head_lanes(rows,h)
    return jnp.where(own,k.astype(F32),pen).astype(BF)
def mask_queries(q, h):
    rows=q.shape[0]
    lane=lax.broadcasted_iota(jnp.int32,(rows,128),1)
    spare=64 if h==0 else 0
    one=jnp.where(lane==spare,1.0,0.0)
    return jnp.where(head_lanes(rows,h),q.astype(F32),one).astype(BF)

def toeplitz(bias_row):
    r=jnp.concatenate([bias_row-bias_row[:,255:256], jnp.zeros((1,256),F32)],axis=1)
    x=jnp.broadcast_to(r,(TILE,512))
    return pltpu.roll(x,0,1,stride=1,stride_axis=0)

def fwd_kernel(causal, limit_ref, hs_ref, bias_ref, q_ref, k_ref, v_ref, o_ref, lse_ref, km, qm, vt, s_scr, p_scr, t_scr):
    S=q_ref.shape[0]; M=k_ref.shape[0]
    limit=limit_ref[0]
    vtf=v_ref[...].astype(F32).T
    ones=jnp.ones((16,M),BF)
    for h in range(2):
        km[h]=mask_keys(k_ref[...],limit,h)
        qm[h]=mask_queries(q_ref[...],h)
        vt[h,0:64]=vtf[h*64:(h+1)*64].astype(BF)
        vt[h,64:80]=ones
        if causal:
            t=toeplitz(bias_ref[pl.ds(2*pl.program_id(0)+h,1),:])
            kk=lax.broadcasted_iota(jnp.int32,(TILE,512),0)
            qq=lax.broadcasted_iota(jnp.int32,(TILE,512),1)
            t_scr[h]=jnp.where(qq>=kk,t,NEG)
    nq=S//TILE; nk=M//TILE
    for i in range(nq):
        qs=slice(i*TILE,(i+1)*TILE)
        accs=[]
        for h in range(2):
            tiles=range(i+1) if causal else range(nk)
            m=None
            for j in tiles:
                s=nt(km[h,j*TILE:(j+1)*TILE],qm[h,qs])
                if causal and j==i: s=s+t_scr[h,:,0:256]
                if causal and j==i-1: s=s+t_scr[h,:,256:512]
                s_scr[h,j*TILE:(j+1)*TILE]=s
                mj=jnp.max(s,axis=0,keepdims=True)
                m=mj if m is None else jnp.maximum(m,mj)
            m2=m*LOG2E
            n=len(tiles)*TILE
            for j in tiles:
                p_scr[h,j*TILE:(j+1)*TILE]=jnp.exp2(s_scr[h,j*TILE:(j+1)*TILE]*LOG2E-m2).astype(BF)
            acc=nn(vt[h,:,0:n],p_scr[h,0:n])
            l=acc[64:65]
            lse_ref[0,h:h+1,qs]=m2+jnp.log2(l)
            accs.append(acc[0:64]*((hs_ref[2*pl.program_id(0)+h] if causal else 1.0)/l))
        ot=jnp.concatenate(accs,axis=0)
        o_ref[qs]=ot.T.astype(BF)

def attn_fwd(causal, limit, hs, bias, q, k, v):
    S,D=q.shape; M=k.shape[0]
    pairs=D//128
    grid_spec=pltpu.PrefetchScalarGridSpec(
        num_scalar_prefetch=1, grid=(pairs,),
        in_specs=[SMEM,
                  pl.BlockSpec(bias.shape,lambda p,*_:(0,0)),
                  pl.BlockSpec((S,128),lambda p,*_:(0,p)),
                  pl.BlockSpec((M,128),lambda p,*_:(0,p)),
                  pl.BlockSpec((M,128),lambda p,*_:(0,p))],
        out_specs=[pl.BlockSpec((S,128),lambda p,*_:(0,p)),
                   pl.BlockSpec((1,2,S),lambda p,*_:(p,0,0))],
        scratch_shapes=[pltpu.VMEM((2,M,128),BF),pltpu.VMEM((2,S,128),BF),pltpu.VMEM((2,80,M),BF),
                        pltpu.VMEM((2,M,TILE),F32),pltpu.VMEM((2,M,TILE),BF),pltpu.VMEM((2,TILE,512),F32)])
    return pl.pallas_call(functools.partial(fwd_kernel,causal),grid_spec=grid_spec,
        out_shape=(jax.ShapeDtypeStruct((S,D),BF),jax.ShapeDtypeStruct((pairs,2,S),F32)),
        compiler_params=params(1),name="attn_fwd",
        cost_estimate=cost(4*S*M*D*(1 if causal else 2),8*S*D,S*M*D//128))(limit,hs,bias,q,k,v)

def bwd_kernel(causal, p0, chained, limit_ref, hs_ref, bias_ref, q_ref, k_ref, v_ref, go_ref, a_ref, lse_ref, *rest):
    if chained: rest=rest[5 if causal else 4:]
    pair=pl.program_id(0)+p0
    if causal:
        gq_ref, gk_ref, gv_ref, ds_ref, gb_ref, km, qm, q0, vm, gom, kt, p_scr, gs_scr, gqt, dl, t_scr, d_scr, far = rest
    else:
        gq_ref, gk_ref, gv_ref, ds_ref, km, qm, q0, vm, gom, kt, p_scr, gs_scr, gqt, dl = rest
    S=q_ref.shape[0]; M=k_ref.shape[0]
    nq=S//TILE; nk=M//TILE
    limit=limit_ref[0]
    kt[...]=k_ref[...].astype(F32).T.astype(BF)
    sel=jnp.concatenate([jnp.where(head_lanes(1,h),1.0,0.0) for h in range(2)]+[jnp.zeros((14,128),F32)],axis=0).astype(BF)
    x=go_ref[...].astype(F32)*a_ref[...].astype(F32)
    if causal:
        lane=lax.broadcasted_iota(jnp.int32,(1,128),1)
        x=x*(1.0/jnp.where(lane<64,jnp.full((1,128),hs_ref[2*pair],F32),jnp.full((1,128),hs_ref[2*pair+1],F32)))
    hi=x.astype(BF); lo=(x-hi.astype(F32)).astype(BF)
    dd=nt(sel,hi)+nt(sel,lo)
    dl[...]=dd[0:8]
    ds_ref[0]=jnp.broadcast_to(jnp.sum(dd[0:2],axis=1,keepdims=True),(2,128))
    zero=jnp.zeros((),F32)
    for h in range(2):
        km[h]=mask_keys(k_ref[...],limit,h)
        qm[h]=mask_queries(q_ref[...],h)
        own=head_lanes(S,h)
        q0[h]=jnp.where(own,q_ref[...].astype(F32),zero).astype(BF)
        gom[h]=jnp.where(own,go_ref[...].astype(F32),zero).astype(BF)
        vm[h]=jnp.where(head_lanes(M,h),v_ref[...].astype(F32),zero).astype(BF)
        if causal:
            t=toeplitz(bias_ref[pl.ds(2*pair+h,1),:])*LOG2E
            kk=lax.broadcasted_iota(jnp.int32,(TILE,512),0)
            qq=lax.broadcasted_iota(jnp.int32,(TILE,512),1)
            t_scr[h]=jnp.where(qq>=kk,t,NEG)
    if causal:
        d_scr[...]=jnp.zeros_like(d_scr); far[...]=jnp.zeros_like(far)
    gqt[...]=jnp.zeros_like(gqt)
    def block(j):
        js=slice(j*TILE,(j+1)*TILE)
        i0=j if causal else 0
        for h in range(2):
            for i in range(i0,nq):
                qs=slice(i*TILE,(i+1)*TILE)
                s=nt(km[h,js],qm[h,qs])*LOG2E
                if causal and i-j<2:
                    s=s+t_scr[h,:,(i-j)*TILE:(i-j+1)*TILE]
                p=jnp.exp2(s-lse_ref[0,h:h+1,qs])
                gs=p*(nt(vm[h,js],go_ref[qs])-dl[h:h+1,qs])
                p_scr[h,:,qs]=p.astype(BF)
                gs_scr[h,:,qs]=gs.astype(BF)
                if causal:
                    if i-j<2:
                        d_scr[h,:,(i-j)*TILE:(i-j+1)*TILE]+=gs
                    else:
                        far[h]+=jnp.sum(gs.reshape(TILE//8,8,TILE),axis=0)
            gqt[h*64:(h+1)*64,i0*TILE:]+=nn(kt[h*64:(h+1)*64,js],gs_scr[h,:,i0*TILE:])
        gv_ref[js]=(nn(p_scr[0,:,i0*TILE:],gom[0,i0*TILE:])+nn(p_scr[1,:,i0*TILE:],gom[1,i0*TILE:])).astype(BF)
        gk_ref[js]=(nn(gs_scr[0,:,i0*TILE:],q0[0,i0*TILE:])+nn(gs_scr[1,:,i0*TILE:],q0[1,i0*TILE:])).astype(BF)
    for j in range(nk):
        if causal:
            block(j)
        else:
            @pl.when(j*TILE<limit)
            def _(): block(j)
            @pl.when(j*TILE>=limit)
            def _():
                gv_ref[j*TILE:(j+1)*TILE]=jnp.zeros((TILE,128),BF)
                gk_ref[j*TILE:(j+1)*TILE]=jnp.zeros((TILE,128),BF)
    gq_ref[...]=gqt[...].T.astype(BF)
    if causal:
        for h in range(2):
            acc=jnp.zeros((8,512),F32)
            for g in range(TILE//8):
                acc=acc+pltpu.roll(d_scr[h,8*g:8*g+8],(512-8*g)%512,1)
            near=jnp.zeros((1,512),F32)
            for r in range(8):
                near=near+pltpu.roll(acc[r:r+1],(512-r)%512,1)
            lane=lax.broadcasted_iota(jnp.int32,(1,512),1)
            tail=jnp.sum(jnp.where(lane>=255,near,0.0),axis=1,keepdims=True)+jnp.sum(jnp.sum(far[h],axis=0,keepdims=True),axis=1,keepdims=True)
            gb_ref[0,h:h+1,:]=jnp.where(lane[:,:256]==255,tail,near[:,:256])

def attn_bwd(causal, limit, hs, bias, q, k, v, go, a, lse, p0, count, before=None):
    S,D=q.shape; M=k.shape[0]
    pairs=D//128
    col=pl.BlockSpec((S,128),lambda p,*_:(0,p+p0))
    colm=pl.BlockSpec((M,128),lambda p,*_:(0,p+p0))
    outs=[col,colm,colm,pl.BlockSpec((1,2,128),lambda p,*_:(p+p0,0,0))]
    shapes=[jax.ShapeDtypeStruct((S,D),BF),jax.ShapeDtypeStruct((M,D),BF),jax.ShapeDtypeStruct((M,D),BF),jax.ShapeDtypeStruct((pairs,2,128),F32)]
    scr=[pltpu.VMEM((2,M,128),BF),pltpu.VMEM((2,S,128),BF),pltpu.VMEM((2,S,128),BF),pltpu.VMEM((2,M,128),BF),pltpu.VMEM((2,S,128),BF),
         pltpu.VMEM((128,M),BF),pltpu.VMEM((2,TILE,S),BF),pltpu.VMEM((2,TILE,S),BF),pltpu.VMEM((128,S),F32),pltpu.VMEM((8,S),F32)]
    if causal:
        outs.append(pl.BlockSpec((1,2,256),lambda p,*_:(p+p0,0,0))); shapes.append(jax.ShapeDtypeStruct((pairs,2,256),F32))
        scr+=[pltpu.VMEM((2,TILE,512),F32),pltpu.VMEM((2,TILE,512),F32),pltpu.VMEM((2,8,TILE),F32)]
    extra=() if before is None else tuple(before)
    grid_spec=pltpu.PrefetchScalarGridSpec(
        num_scalar_prefetch=1, grid=(count,),
        in_specs=[SMEM,pl.BlockSpec(bias.shape,lambda p,*_:(0,0)),
                  col,colm,colm,col,col,pl.BlockSpec((1,2,S),lambda p,*_:(p+p0,0,0))]+[pl.BlockSpec(memory_space=pl.ANY)]*len(extra),
        out_specs=outs, scratch_shapes=scr)
    return pl.pallas_call(functools.partial(bwd_kernel,causal,p0,before is not None),grid_spec=grid_spec,out_shape=tuple(shapes),
        input_output_aliases={9+i:i for i in range(len(extra))},
        cost_estimate=cost(10*S*M*D*(1 if causal else 2)*count//pairs,16*S*D*count//pairs,S*M*D//128),
        compiler_params=params(1),name="attn_bwd")(limit,hs,bias,q,k,v,go,a,lse,*extra)
EPS=1e-5
TASKS=4
def norm_rows(v):
    c=v-jnp.mean(v,axis=-1,keepdims=True)
    inv=lax.rsqrt(jnp.mean(c*c,axis=-1,keepdims=True)+EPS)
    return c*inv,inv
def norm_back(e,n,inv,g):
    s=e*g
    return (s-jnp.mean(s,axis=-1,keepdims=True)-n*jnp.mean(s*n,axis=-1,keepdims=True))*inv
def col_sum(v): return jnp.sum(v,axis=0,keepdims=True)

def vec(ref):
    return ref[...].reshape(1,-1)
def whole(shape):
    return pl.BlockSpec(shape,lambda *_:(0,)*len(shape),pipeline_mode=pl.Buffered(1))
def rows_of(rows,cols):
    return pl.BlockSpec((rows,cols),lambda i,*_:(i,0))

def pre_kernel(x_ref,m_ref,g_ref,b_ref,wq,qb,wk,wv,vb,ck,cv,cvb,q_o,k_o,v_o,k2_o,v2_o):
    n,_=norm_rows(x_ref[...].astype(F32))
    h=(n*vec(g_ref)+vec(b_ref)).astype(BF)
    q_o[...]=((nn(h,wq[...])+vec(qb))*0.125).astype(BF)
    k_o[...]=nn(h,wk[...]).astype(BF)
    v_o[...]=(nn(h,wv[...])+vec(vb)).astype(BF)
    m=m_ref[...]
    k2_o[...]=nn(m,ck[...]).astype(BF)
    v2_o[...]=(nn(m,cv[...])+vec(cvb)).astype(BF)

def pre(x,m,g,b,wq,qb,wk,wv,vb,ck,cv,cvb,T=256):
    S,D=x.shape
    r=rows_of(T,D); w=whole((D,D)); u=whole((D,))
    o=jax.ShapeDtypeStruct((S,D),BF)
    return pl.pallas_call(pre_kernel,grid=(S//T,),in_specs=[r,r,u,u,w,u,w,w,u,w,w,u],out_specs=[r]*5,out_shape=[o]*5,
        compiler_params=params(1),name="pre",cost_estimate=cost(10*S*D*D,10*D*D+14*S*D))(x,m,g,b,wq,qb,wk,wv,vb,ck,cv,cvb)

def post_kernel(a_ref,x_ref,wo,bo,pg,pb,ng,nb,wq,qb,x1_o,q2_o,n_o,inv_o):
    n,inv=norm_rows(nn(a_ref[...],wo[...])+vec(bo))
    n_o[...]=n.astype(BF); inv_o[...]=inv
    x1=x_ref[...].astype(F32)+(n*vec(pg)+vec(pb))
    x1_o[...]=x1
    n2,_=norm_rows(x1)
    h=(n2*vec(ng)+vec(nb)).astype(BF)
    q2_o[...]=((nn(h,wq[...])+vec(qb))*0.125).astype(BF)

def post(a,x,wo,bo,pg,pb,ng,nb,wq,qb,T=256):
    S,D=x.shape
    r=rows_of(T,D); w=whole((D,D)); u=whole((D,))
    o=jax.ShapeDtypeStruct((S,D),BF)
    return pl.pallas_call(post_kernel,grid=(S//T,),in_specs=[r,r,w,u,u,u,u,u,w,u],
        out_specs=[r,r,r,rows_of(T,1)],out_shape=[jax.ShapeDtypeStruct((S,D),F32),o,o,jax.ShapeDtypeStruct((S,1),F32)],
        compiler_params=params(1),name="post",cost_estimate=cost(4*S*D*D,4*D*D+12*S*D))(a,x,wo,bo,pg,pb,ng,nb,wq,qb)

SQH=0.7071067811865476
ERFC=(-1.26551223,1.00002368,0.37409196,0.09678418,-0.18628806,0.27886807,-1.13520398,1.48851587,-0.82215223,0.17087277)
def gelu_parts(f):
    z=jnp.abs(f)*SQH
    t=1.0/(1.0+0.5*z)
    poly=jnp.full_like(t,ERFC[9]*LOG2E)
    for c in ERFC[8::-1]:
        poly=poly*t+c*LOG2E
    zz=z*z*LOG2E
    half=0.5*t*jnp.exp2(poly-zz)
    phi=jnp.where(f<0.0,half,1.0-half)
    dens=jnp.exp2(-zz)*0.3989422804014327
    return f*phi, phi+f*dens

CH=256
def mid_kernel(n,dec_ref,gb_ref,idx_ref,all_ref,a2_ref,x1_ref,og_ref,cwo,wi,wout,cbo,cpg,cpb,fng,fnb,bi,mg,mb,bo,
               lo_o,gx2_o,go2_o,u_o,gf_o,h3_o,g3_o,gb2_o,v1_o,v3_o,fac_o,ge,dg,gus):
    T,D=a2_ref.shape; FF=wi.shape[1]
    bi_v=vec(bi); mg_v=vec(mg); mb_v=vec(mb)
    step=pl.program_id(0)
    row=step*T+lax.broadcasted_iota(jnp.int32,(T,1),0)
    valid=row<dec_ref[0]
    n_b,inv_b=norm_rows(nn(a2_ref[...],cwo[...])+vec(cbo))
    x2=x1_ref[...]+(n_b*vec(cpg)+vec(cpb))
    n_x,inv_x=norm_rows(x2)
    h3=(n_x*vec(fng)+vec(fnb)).astype(BF)
    h3_o[...]=h3
    part=jnp.zeros((T,128),F32)
    for c in range(0,FF,CH):
        f=nn(h3,wi[:,c:c+CH])+bi_v[:,c:c+CH]
        a,d=gelu_parts(f)
        ge[:,c:c+CH]=a
        dg[:,c:c+CH]=d
        for l in range(0,CH,128): part=part+a[:,l:l+128]
    mean=jnp.sum(part,axis=1,keepdims=True)*(1.0/FF)
    part=jnp.zeros((T,128),F32)
    for c in range(0,FF,CH):
        e=ge[:,c:c+CH]-mean
        e=e*e
        for l in range(0,CH,128): part=part+e[:,l:l+128]
    inv=lax.rsqrt(jnp.sum(part,axis=1,keepdims=True)*(1.0/FF)+EPS)
    g3=jnp.where(valid,og_ref[...].astype(F32),0.0)
    g3b=g3.astype(BF)
    g3_o[...]=g3b
    s1=jnp.zeros((T,128),F32); s2=jnp.zeros((T,128),F32)
    @pl.when(step==0)
    def _():
        v1_o[...]=jnp.zeros_like(v1_o); v3_o[...]=jnp.zeros_like(v3_o)
        owner=lax.broadcasted_iota(jnp.int32,(n,8,128),0)
        task=sum((owner>=gb_ref[k]).astype(jnp.int32) for k in range(1,TASKS))
        mine=sum((idx_ref[0]>=gb_ref[k]).astype(jnp.int32) for k in range(1,TASKS))
        fac_o[...]=n/jnp.sum(jnp.where(task==mine,all_ref[...],0.0),axis=0)
    for c in range(0,FF,CH):
        cs=slice(c,c+CH)
        n=(ge[:,cs]-mean)*inv
        ge[:,cs]=n
        u_o[:,cs]=(n*mg_v[:,cs]+mb_v[:,cs]).astype(BF)
        gu=nt(g3b,wout[cs,:])
        en=gu*n
        v3_o[0:1,cs]+=col_sum(en)
        v3_o[1:2,cs]+=col_sum(gu)
        eg=gu*mg_v[:,cs]
        gus[:,cs]=eg
        egn=eg*n
        for l in range(0,CH,128):
            s1=s1+eg[:,l:l+128]; s2=s2+egn[:,l:l+128]
    m1=jnp.sum(s1,axis=1,keepdims=True)*(1.0/FF); m2=jnp.sum(s2,axis=1,keepdims=True)*(1.0/FF)
    out=x2+(nn(u_o[...],wout[...])+vec(bo))
    lo_o[...]=jnp.where(valid,out,0.0).astype(BF)
    for c in range(0,FF,CH):
        cs=slice(c,c+CH)
        gf=((gus[:,cs]-m1-ge[:,cs]*m2)*inv*dg[:,cs]).astype(BF)
        gf_o[:,cs]=gf
        v3_o[2:3,cs]+=col_sum(gf.astype(F32))
    gh=nt(gf_o[...],wi[...])
    v1_o[0:1]+=col_sum(gh*n_x); v1_o[1:2]+=col_sum(gh)
    gx2=g3+norm_back(gh,n_x,inv_x,vec(fng))
    gx2_o[...]=gx2
    v1_o[2:3]+=col_sum(g3)
    v1_o[3:4]+=col_sum(gx2*n_b); v1_o[4:5]+=col_sum(gx2)
    gb2=norm_back(gx2,n_b,inv_b,vec(cpg)).astype(BF)
    gb2_o[...]=gb2
    v1_o[5:6]+=col_sum(gb2.astype(F32))
    go2_o[...]=nt(gb2,cwo[...]).astype(BF)

def mid(n,dec,gb,idx,all_dec,a2,x1,og,cwo,wi,wout,cbo,cpg,cpb,fng,fnb,bi,mg,mb,bo,T=256):
    S,D=x1.shape; FF=wi.shape[1]
    r=rows_of(T,D); rf=rows_of(T,FF); u=whole((D,)); uf=whole((FF,))
    sd=jax.ShapeDtypeStruct
    acc=lambda s: pl.BlockSpec(s,lambda *_:(0,0))
    return pl.pallas_call(functools.partial(mid_kernel,n),grid=(S//T,),
        in_specs=[SMEM,SMEM,SMEM,whole((n,8,128)),r,r,r,whole((D,D)),whole((D,FF)),whole((FF,D)),u,u,u,u,u,uf,uf,uf,u],
        out_specs=[r,r,r,rf,rf,r,r,r,acc((8,D)),acc((8,FF)),acc((8,128))],
        out_shape=[sd((S,D),BF),sd((S,D),F32),sd((S,D),BF),sd((S,FF),BF),sd((S,FF),BF),sd((S,D),BF),sd((S,D),BF),sd((S,D),BF),sd((8,D),F32),sd((8,FF),F32),sd((8,128),F32)],
        scratch_shapes=[pltpu.VMEM((T,FF),F32)]*3,
        compiler_params=params(1,58),name="mid",
        cost_estimate=cost(8*S*D*FF+4*S*D*D,4*D*FF+2*D*D+S*D*20+4*S*FF,S*FF*3))(dec,gb,idx,all_dec,a2,x1,og,cwo,wi,wout,cbo,cpg,cpb,fng,fnb,bi,mg,mb,bo)

def head_row(hs_ref,D,H):
    lane=lax.broadcasted_iota(jnp.int32,(1,D),1)//(D//H)
    v=jnp.zeros((1,D),F32)
    for h in range(H): v=jnp.where(lane==h,hs_ref[h],v)
    return v
def cross_back_kernel(hs_ref,gq_ref,x1_ref,gx2_ref,n_ref,inv_ref,gv_ref,cwq,wo,cng,cnb,spg,
                      gx1_o,go1_o,h2_o,gqs_o,gb1_o,v_o):
    @pl.when(pl.program_id(0)==0)
    def _(): v_o[...]=jnp.zeros_like(v_o)
    gq=gq_ref[...]*jnp.asarray(0.125,BF)
    gqs_o[...]=gq
    n,inv=norm_rows(x1_ref[...])
    h2_o[...]=(n*vec(cng)+vec(cnb)).astype(BF)
    gh=nt(gq,cwq[...])
    v_o[0:1]+=col_sum(gh*n); v_o[1:2]+=col_sum(gh)
    v_o[2:3]+=col_sum(gq.astype(F32)); v_o[3:4]+=col_sum(gv_ref[...].astype(F32))
    gx1=gx2_ref[...]+norm_back(gh,n,inv,vec(cng))
    gx1_o[...]=gx1
    nb=n_ref[...].astype(F32)
    v_o[4:5]+=col_sum(gx1*nb); v_o[5:6]+=col_sum(gx1)
    gb1=norm_back(gx1,nb,inv_ref[...],vec(spg)).astype(BF)
    gb1_o[...]=gb1
    v_o[6:7]+=col_sum(gb1.astype(F32))
    go1_o[...]=(nt(gb1,wo[...])*head_row(hs_ref,gb1.shape[1],hs_ref.shape[0])).astype(BF)

def cross_back(hs,gq,x1,gx2,n,inv,gv,cwq,wo,cng,cnb,spg,T=256):
    S,D=x1.shape
    r=rows_of(T,D); w=whole((D,D)); u=whole((D,))
    sd=jax.ShapeDtypeStruct
    return pl.pallas_call(cross_back_kernel,grid=(S//T,),in_specs=[SMEM,r,r,r,r,rows_of(T,1),r,w,w,u,u,u],
        out_specs=[r,r,r,r,r,pl.BlockSpec((8,D),lambda *_:(0,0))],
        out_shape=[sd((S,D),F32)]+[sd((S,D),BF)]*4+[sd((8,D),F32)],
        compiler_params=params(1),name="cross_back",cost_estimate=cost(4*S*D*D,4*D*D+28*S*D))(hs,gq,x1,gx2,n,inv,gv,cwq,wo,cng,cnb,spg)

def self_norm_kernel(x_ref,gq_ref,gv_ref,g_ref,b_ref,h_o,gqs_o,v_o):
    @pl.when(pl.program_id(0)==0)
    def _(): v_o[...]=jnp.zeros_like(v_o)
    n,_=norm_rows(x_ref[...].astype(F32))
    h_o[...]=(n*vec(g_ref)+vec(b_ref)).astype(BF)
    gq=gq_ref[...]*jnp.asarray(0.125,BF)
    gqs_o[...]=gq
    v_o[0:1]+=col_sum(gq.astype(F32)); v_o[1:2]+=col_sum(gv_ref[...].astype(F32))
def self_norm(x,gq,gv,g,b,T=256):
    S,D=x.shape
    r=rows_of(T,D); u=whole((D,)); sd=jax.ShapeDtypeStruct
    return pl.pallas_call(self_norm_kernel,grid=(S//T,),in_specs=[r,r,r,u,u],out_specs=[r,r,pl.BlockSpec((8,D),lambda *_:(0,0))],
        out_shape=[sd((S,D),BF)]*2+[sd((8,D),F32)],compiler_params=params(1),name="self_norm",cost_estimate=cost(S*D*20,S*D*10))(x,gq,gv,g,b)

def tail_kernel(fac_ref,hs_ref,x_ref,gx1_ref,gq_ref,gk_ref,gv_ref,wq,wk,wv,g_ref,va,vb,vc,vf,gb,ds,gt_o,v_o):
    D=x_ref.shape[1]; H=hs_ref.shape[0]
    fac=fac_ref[0:1,0:1]
    @pl.when(pl.program_id(0)==0)
    def _():
        v_o[...]=jnp.zeros_like(v_o)
        v_o[0:8]=va[...]*fac
        v_o[8:16]=vb[...]*fac
        v_o[16:18]=vc[0:2]*fac
        for k in range(3):
            for c in range(vf.shape[1]//D):
                v_o[24+4*k+c:25+4*k+c]=vf[k:k+1,c*D:(c+1)*D]*fac
        for h in range(H):
            v_o[36+h:37+h,0:256]=gb[h//2,h%2:h%2+1,:]*fac
            v_o[36+h:37+h,256:384]=ds[h//2,h%2:h%2+1,:]*fac*(1.0/jnp.full((1,1),hs_ref[h],F32))
    n,inv=norm_rows(x_ref[...].astype(F32))
    gh=nt(gq_ref[...],wq[...])+nt(gk_ref[...],wk[...])+nt(gv_ref[...],wv[...])
    v_o[18:19]+=col_sum(gh*n)*fac; v_o[19:20]+=col_sum(gh)*fac
    gt_o[...]=gx1_ref[...]+norm_back(gh,n,inv,vec(g_ref))
def tail(fac,hs,x,gx1,gq,gk,gv,wq,wk,wv,g,va,vb,vc,vf,gb,ds,T=256):
    S,D=x.shape
    r=rows_of(T,D); w=whole((D,D)); u=whole((D,)); sd=jax.ShapeDtypeStruct
    return pl.pallas_call(tail_kernel,grid=(S//T,),in_specs=[whole((8,128)),SMEM]+[r]*5+[w]*3+[u]+[whole(v.shape) for v in (va,vb,vc,vf,gb,ds)],
        out_specs=[r,pl.BlockSpec((48,D),lambda *_:(0,0))],
        out_shape=[sd((S,D),F32)]+[sd((48,D),F32)],compiler_params=params(1),name="tail",cost_estimate=cost(10*S*D*D,10*D*D+S*D*24))(fac,hs,x,gx1,gq,gk,gv,wq,wk,wv,g,va,vb,vc,vf,gb,ds)

def memory_kernel(k_ref,v_ref,ck,cv,o):
    o[...]=nt(k_ref[...],ck[...])+nt(v_ref[...],cv[...])
def memory_grad(gk,gv,ck,cv,T=256):
    S,D=gk.shape
    r=rows_of(T,D); w=whole((D,D))
    return pl.pallas_call(memory_kernel,grid=(S//T,),in_specs=[r,r,w,w],out_specs=r,out_shape=jax.ShapeDtypeStruct((S,D),F32),
        compiler_params=params(1),name="memory",cost_estimate=cost(4*S*D*D,4*D*D+S*D*8))(gk,gv,ck,cv)

ROWS=(18,19,16,17,14,12,13,8,9,10,11,5,3,4,0,1,2)
def pick_kernel(n,idx_ref,v,*outs):
    D=v.shape[1]; w=D//n; idx=idx_ref[0]
    x=pltpu.roll(v[0:24],lax.rem(D-w*idx,D),1)
    for r,o in zip(ROWS,outs): o[...]=x[r:r+1,:w].reshape(w)
    each=n//4; wide=4*D//n
    shift=lax.rem(D-wide*lax.rem(idx,each),D)
    for k in range(3):
        y=pltpu.roll(v[pl.ds(24+4*k+idx//each,1),:],shift,1)
        outs[17+k][...]=y[:,:wide].reshape(wide)
    H=outs[20].shape[0]; b=256//n
    z=pltpu.roll(v[36:36+H,0:256],lax.rem(256-b*idx,256),1)
    outs[20][...]=z[:,:b]
    eye=lax.broadcasted_iota(jnp.int32,(H,128),0)==lax.broadcasted_iota(jnp.int32,(H,128),1)
    outs[21][...]=col_sum(jnp.where(eye,v[36:36+H,256:384],0.0))[:,:H].reshape(H)
def pick(n,idx,v,H):
    D=v.shape[1]; sd=jax.ShapeDtypeStruct
    shapes=[sd((D//n,),F32)]*17+[sd((4*D//n,),F32)]*3+[sd((H,256//n),F32),sd((H,),F32)]
    return pl.pallas_call(functools.partial(pick_kernel,n),in_specs=[SMEM,pl.BlockSpec(v.shape)],out_shape=shapes,
        compiler_params=params(0),name="pick")(idx,v)

def part_rows(scr,core,keep_o,send_o):
    groups,r=keep_o.shape[:2]
    for t in range(groups):
        if r%8==0:
            keep_o[t]=scr[pl.ds((2*t+core)*r,r),:]
            send_o[t]=scr[pl.ds((2*t+1-core)*r,r),:]
        else:
            even=scr[2*t*r:(2*t+1)*r,:]
            odd=scr[(2*t+1)*r:(2*t+2)*r,:]
            keep_o[t]=jnp.where(core==0,even,odd)
            send_o[t]=jnp.where(core==0,odd,even)
def wrow_kernel(core_ref,fac_ref,l_ref,r_ref,keep_o,send_o,scr):
    scr[...]=tn(l_ref[...],r_ref[...])*fac_ref[0:1,0:1]
    part_rows(scr,core_ref[0],keep_o,send_o)
def wgrad_rows(core,fac,lhs,rhs,n,B=768):
    S,M=lhs.shape; N=rhs.shape[1]; r=M//n; steps=M//B; groups=B//r//2
    o=pl.BlockSpec((groups,r,N),lambda i:(i,0,0)); sh=jax.ShapeDtypeStruct((n//2,r,N),F32)
    return pl.pallas_call(wrow_kernel,grid=(steps,),
        in_specs=[SMEM,whole((8,128)),pl.BlockSpec((S,B),lambda i:(0,i)),whole((S,N))],
        out_specs=[o,o],scratch_shapes=[pltpu.VMEM((B,N),F32)],out_shape=[sh,sh],compiler_params=params(1),name="wgrad",
        cost_estimate=cost(4*S*M*N,2*S*(M+N)+4*M*N))(core,fac,lhs,rhs)
def wcol_kernel(plan,core_ref,fac_ref,*refs):
    ins=refs[:-3]; keep_o,send_o,scr=refs[-3:]
    step=pl.program_id(0)
    for l,r,first,last in plan:
        @pl.when((step>=first)&(step<last))
        def _(): scr[...]=tn(ins[l][...],ins[r][...])*fac_ref[0:1,0:1]
    part_rows(scr,core_ref[0],keep_o,send_o)
def wgrad_cols(core,fac,pairs,n,B=768):
    ins=[]; specs=[]; plan=[]; at=0; seen={}
    S,M=pairs[0][0].shape
    for lhs,rhs in pairs:
        if id(lhs) not in seen:
            seen[id(lhs)]=len(ins); ins.append(lhs); specs.append(whole((S,M)))
        steps=rhs.shape[1]//B
        plan.append((seen[id(lhs)],len(ins),at,at+steps))
        ins.append(rhs)
        specs.append(pl.BlockSpec((S,B),functools.partial(lambda at,steps,i:(0,jnp.clip(i-at,0,steps-1)),at,steps)))
        at+=steps
    N=at*B; r=M//n
    o=pl.BlockSpec((n//2,r,B),lambda i:(0,0,i)); sh=jax.ShapeDtypeStruct((n//2,r,N),F32)
    return pl.pallas_call(functools.partial(wcol_kernel,plan),grid=(at,),in_specs=[SMEM,whole((8,128))]+specs,
        out_specs=[o,o],scratch_shapes=[pltpu.VMEM((M,B),F32)],out_shape=[sh,sh],compiler_params=params(1),name="wgrad",
        cost_estimate=cost(4*S*M*N,2*S*M*len(ins)+4*M*N))(core,fac,*ins)

def halve_kernel(bit_ref,km,ko,gm,go,keep_o,send_o):
    send_o[...]=ko[:,0]+go[:,0]
    keep_o[...]=km[:,0]+gm[:,0]
def halve(bit,keep,got,part=0,parts=1):
    A,_,B,r,C=keep.shape
    C=C//parts
    K=max(1,A//4)
    mine=pl.BlockSpec((K,1,B,r,C),lambda i,b:(i,b[0],0,0,part)); other=pl.BlockSpec((K,1,B,r,C),lambda i,b:(i,1-b[0],0,0,part))
    o=pl.BlockSpec((K,B,r,C),lambda i,b:(i,0,0,0)); sh=jax.ShapeDtypeStruct((A,B,r,C),F32)
    gs=pltpu.PrefetchScalarGridSpec(num_scalar_prefetch=1,grid=(A//K,),in_specs=[mine,other,mine,other],out_specs=[o,o])
    return pl.pallas_call(halve_kernel,grid_spec=gs,out_shape=[sh,sh],compiler_params=params(1),name="halve",
        cost_estimate=cost(1000,1000))(bit,keep,keep,got,got)

def deal_kernel(z_ref,k0,k1,k2,k3,g0,g1,g2,g3,o0,o1,o2,o3):
    for k,g,o in ((k0,g0,o0),(k1,g1,o1),(k2,g2,o2),(k3,g3,o3)):
        o[...]=k[0]+g[0]
def deal(z,keep,got):
    _,r,C=keep.shape
    spec=lambda m: pl.BlockSpec((1,r,C),lambda i,z,m=m:(z[0]^m,0,0))
    o=pl.BlockSpec((r,C),lambda i,z:(0,0)); sh=jax.ShapeDtypeStruct((r,C),F32)
    gs=pltpu.PrefetchScalarGridSpec(num_scalar_prefetch=1,grid=(1,),in_specs=[spec(m) for m in range(4)]*2,out_specs=[o]*4)
    return pl.pallas_call(deal_kernel,grid_spec=gs,out_shape=[sh]*4,compiler_params=params(1),name="deal",
        cost_estimate=cost(1000,1000))(z,*([keep]*4),*([got]*4))

def finish_kernel(plan,*refs):
    ins=refs[:-len(plan)]; outs=refs[-len(plan):]
    for o,pieces in zip(outs,plan):
        at=0
        for c,lo,hi in pieces:
            o[:,at:at+hi-lo]=(ins[4*c][:,lo:hi]+ins[4*c+1][:,lo:hi])+(ins[4*c+2][:,lo:hi]+ins[4*c+3][:,lo:hi])
            at+=hi-lo
def finish(chains,plan):
    ins=[v for c in chains for v in c.last]
    shapes=[jax.ShapeDtypeStruct((ins[4*p[0][0]].shape[0],sum(hi-lo for _,lo,hi in p)),F32) for p in plan]
    return pl.pallas_call(functools.partial(finish_kernel,plan),in_specs=[pl.BlockSpec(v.shape) for v in ins],out_shape=shapes,
        compiler_params=params(0),name="finish",cost_estimate=cost(1000,1000))(*ins)

def swap(x,n,bit):
    return lax.ppermute(x,"dp",[(j,j^(1<<bit)) for j in range(n)])
def after(token,*vals):
    return lax.optimization_barrier(tuple(vals)+tuple(token))[:len(vals)]
class Halving:
    def __init__(self,n,index,keep,send,order):
        self.n,self.index,self.order=n,index,list(order)
        self.live=list(range(n.bit_length()-2,0,-1))
        self.keep=keep; self.got=swap(send,n,0); self.part=(0,1)
    def split(self,orders):
        chains=[]
        for k,order in enumerate(orders):
            h=object.__new__(Halving)
            h.n,h.index,h.order,h.live=self.n,self.index,list(order),list(self.live)
            h.keep,h.got,h.part=self.keep,self.got,(k,len(orders))
            chains.append(h)
        return chains
    def step(self,token):
        keep,got=after(token,self.keep,self.got)
        b=self.order.pop(0)
        axis=self.live.index(b)
        self.live.remove(b)
        shape=(2**axis,2,2**(len(self.live)-axis))+keep.shape[-2:]
        bit=((self.index>>b)&1).reshape(1).astype(jnp.int32)
        self.keep,send=halve(bit,keep.reshape(shape),got.reshape(shape),*self.part)
        self.part=(0,1)
        self.got=swap(send,self.n,b)
        return send

    def last_step(self,token,zs):
        keep,got=after(token,self.keep,self.got)
        z=((self.index>>zs[0])&3).reshape(1).astype(jnp.int32)
        shape=(4,)+keep.shape[-2:]
        own,*sends=deal(z,keep.reshape(shape),got.reshape(shape))
        n=self.n
        self.last=[own]+[lax.ppermute(s,"dp",[(j,j^((m+1)<<zs[0])) for j in range(n)]) for m,s in enumerate(sends)]
        return own

def shards(n,tokens,memory,out_grad,dec_len,mem_len,group_bounds,
           self_norm_gain,self_norm_bias,self_query,self_query_bias,self_key,self_value,self_value_bias,self_output,self_output_bias,
           position_bias,head_scale,self_post_gain,self_post_bias,cross_norm_gain,cross_norm_bias,cross_query,cross_query_bias,
           cross_key,cross_value,cross_value_bias,cross_output,cross_output_bias,cross_post_gain,cross_post_bias,
           feed_norm_gain,feed_norm_bias,feed_inner,feed_inner_bias,feed_mid_gain,feed_mid_bias,feed_outer,feed_outer_bias):
    bits=n.bit_length()-1
    xs,ys,zs=([1],[2],[3,4]) if bits==5 else ([1,2],[3,4],list(range(5,bits)))
    order_a=xs+ys; order_b=ys+xs
    index=lax.axis_index("dp")
    idx=index.reshape(1).astype(jnp.int32)
    core=idx&1
    x=tokens[0]; m=memory[0]; og=out_grad[0]
    S,D=x.shape
    H=head_scale.shape[0]; pairs=H//2
    all_dec=lax.all_to_all(jnp.broadcast_to(dec_len.astype(F32).reshape(1,1,1),(n,8,128)),"dp",0,0,tiled=True)
    q1,k1,v1,k2,v2=pre(x,m,self_norm_gain,self_norm_bias,self_query,self_query_bias,self_key,self_value,self_value_bias,cross_key,cross_value,cross_value_bias)
    a1,lse1=attn_fwd(True,dec_len,head_scale,position_bias,q1,k1,v1)
    x1,q2,nb1,ib1=post(a1,x,self_output,self_output_bias,self_post_gain,self_post_bias,cross_norm_gain,cross_norm_bias,cross_query,cross_query_bias)
    a2,lse2=attn_fwd(False,mem_len,head_scale,position_bias,q2,k2,v2)
    lo,gx2,go2,u,gf,h3,g3,gb2,va,vf,fac=mid(n,dec_len,group_bounds,idx,all_dec,a2,x1,og,cross_output,feed_inner,feed_outer,cross_output_bias,cross_post_gain,cross_post_bias,feed_norm_gain,feed_norm_bias,feed_inner_bias,feed_mid_gain,feed_mid_bias,feed_outer_bias)
    keep,send=wgrad_cols(core,fac,[(h3,gf),(a2,gb2)],n)
    fi=Halving(n,index,keep,send,order_b)
    u,=after([send],u)
    keep,send=wgrad_rows(core,fac,u,g3,n)
    fo=Halving(n,index,keep,send,order_a)
    t=[fi.step([send])]
    t=[fo.step(t)]
    go2,=after(t,go2)
    back=attn_bwd(False,mem_len,head_scale,position_bias,q2,k2,v2,go2,a2,lse2,0,pairs)
    gq2,gk2,gv2,_=back
    gx1,go1,h2,gqs2,gb1,vb=cross_back(head_scale,gq2,x1,gx2,nb1,ib1,gv2,cross_query,self_output,cross_norm_gain,cross_norm_bias,self_post_gain)
    t=[fo.step([vb])]
    h2,=after(t,h2)
    keep,send=wgrad_cols(core,fac,[(h2,gqs2),(m,gv2),(m,gk2),(a1,gb1)],n)
    g2=Halving(n,index,keep,send,[])
    t=[fi.step([send])]
    go1,=after(t,go1)
    half=pairs//2
    back=attn_bwd(True,dec_len,head_scale,position_bias,q1,k1,v1,go1,a1,lse1,0,half)
    while fo.order: t=[fo.step([back[3]])]
    t=[fo.last_step([back[3]],zs)]
    ga,gb_=g2.split([order_a,order_b])
    t=[ga.step(t)]
    t=[gb_.step(t)]
    go1,=after(t,go1)
    gq1,gk1,gv1,ds,gb=attn_bwd(True,dec_len,head_scale,position_bias,q1,k1,v1,go1,a1,lse1,half,pairs-half,back)
    h1,gqs1,vc=self_norm(x,gq1,gv1,self_norm_gain,self_norm_bias)
    while fi.order: t=[fi.step([vc])]
    t=[fi.last_step([vc],zs)]
    h1,=after(t+fo.last[1:]+[ga.got,gb_.got],h1)
    t=[ga.step([vc,h1])]
    t=[gb_.step(t)]
    h1,=after(t,h1)
    keep,send=wgrad_cols(core,fac,[(h1,gqs1),(h1,gv1),(h1,gk1)],n)
    g3_=Halving(n,index,keep,send,[])
    gx1,=after([send],gx1)
    gt,packed=tail(fac,head_scale,x,gx1,gqs1,gk1,gv1,self_query,self_key,self_value,self_norm_gain,va,vb,vc,vf,gb,ds)
    sa,sb=g3_.split([order_a,order_b])
    t=[sa.step([packed])]
    t=[sb.step(t)]
    gk2,=after(t+fi.last[1:],gk2)
    bit=0
    other=swap(packed,n,bit)
    gm=memory_grad(gk2,gv2,cross_key,cross_value)
    t=[gm]
    def add_up(t,packed,other,bit):
        packed,other=after(t,packed,other)
        packed=packed+other
        bit+=1
        if (1<<bit)<n: other=swap(packed,n,bit)
        return packed,other,bit
    packed,other,bit=add_up(t,packed,other,bit)
    t=[packed]
    for c in (ga,gb_):
        while c.order: t=[c.step(t)]
        t=[c.last_step(t,zs)]
    packed,other,bit=add_up(t,packed,other,bit)
    t=[packed]
    while sa.order or sb.order:
        for c in (sa,sb): t=[c.step(t)]
        if (1<<bit)<n:
            packed,other,bit=add_up(t,packed,other,bit)
            t=[packed]
    for c in (sa,sb): t=[c.last_step(t,zs)]
    while (1<<bit)<n:
        packed,other,bit=add_up(t,packed,other,bit)
        t=[packed]
    small=pick(n,idx,packed,H)
    FF=feed_inner.shape[1]; M=D+D//2
    g_fo,g_fi,g_co,g_cq,g_cv,g_ck,g_so,g_sq,g_sv,g_sk=finish([fo,fi,ga,gb_,sa,sb],[
        [(0,0,D)],[(1,0,FF)],[(1,FF,FF+D)],[(2,0,D)],[(2,D,2*D)],[(3,0,D)],[(3,D,2*D)],
        [(4,0,D)],[(4,D,M),(5,0,D//2)],[(5,D//2,M)]])
    (sng,snb,sqb,svb,sob,spg,spb,cng,cnb,cqb,cvb,cob,cpg,cpb,fng,fnb,fob,fmg,fmb,fib,gpos,ghs)=small
    fo_b=fob
    return (lo[None],gt[None],gm[None],
        sng,snb,g_sq,sqb,g_sk,g_sv,svb,g_so,sob,gpos,ghs,spg,spb,cng,cnb,g_cq,cqb,g_ck,g_cv,cvb,g_co,cob,cpg,cpb,
        fng,fnb,g_fi,fib,fmg,fmb,g_fo,fo_b)

def solution(mesh):
    n=mesh.shape["dp"]
    vec=P("dp"); mat=P("dp",None); cube=P("dp",None,None)
    return jax.shard_map(functools.partial(shards,n),mesh=mesh,in_specs=(cube,cube,cube,vec,vec)+(P(),)*33,
        out_specs=(cube,cube,cube,vec,vec,mat,vec,mat,mat,vec,mat,vec,P(None,"dp"),P(),vec,vec,vec,vec,mat,vec,
                   mat,mat,vec,mat,vec,vec,vec,vec,vec,mat,vec,vec,vec,mat,vec),check_vma=False)
```

```python
import functools
import jax, jax.numpy as jnp
from jax import lax
from jax.experimental import pallas as pl
from jax.experimental.pallas import tpu as pltpu
from jax.sharding import PartitionSpec as P
F32=jnp.float32; BF=jnp.bfloat16
LOG2E=1.4426950408889634
NEG=-1e30
TILE=256
SMEM=pl.BlockSpec(memory_space=pltpu.SMEM)
def cost(flops,nbytes,trans=0):
    return pl.CostEstimate(flops=int(flops)*200,bytes_accessed=int(nbytes)*200,transcendentals=int(trans))
def nt(a,b): return lax.dot_general(a,b,(((1,),(1,)),((),())),preferred_element_type=F32)
def nn(a,b): return lax.dot_general(a,b,(((1,),(0,)),((),())),preferred_element_type=F32)
def tn(a,b): return lax.dot_general(a,b,(((0,),(0,)),((),())),preferred_element_type=F32)
def params(n, mb=56, sem=None):
    return pltpu.CompilerParams(dimension_semantics=("arbitrary",)*n, vmem_limit_bytes=mb<<20)

def head_lanes(rows, h):
    lane=lax.broadcasted_iota(jnp.int32,(rows,128),1)
    return (lane<64) if h==0 else (lane>=64)

def mask_keys(k, limit, h):
    rows=k.shape[0]
    lane=lax.broadcasted_iota(jnp.int32,(rows,128),1)
    row=lax.broadcasted_iota(jnp.int32,(rows,128),0)
    spare=64 if h==0 else 0
    pen=jnp.where((lane==spare)&(row>=limit), NEG, 0.0)
    own=head_lanes(rows,h)
    return jnp.where(own,k.astype(F32),pen).astype(BF)
def mask_queries(q, h):
    rows=q.shape[0]
    lane=lax.broadcasted_iota(jnp.int32,(rows,128),1)
    spare=64 if h==0 else 0
    one=jnp.where(lane==spare,1.0,0.0)
    return jnp.where(head_lanes(rows,h),q.astype(F32),one).astype(BF)

def toeplitz(bias_row):
    r=jnp.concatenate([bias_row-bias_row[:,255:256], jnp.zeros((1,256),F32)],axis=1)
    x=jnp.broadcast_to(r,(TILE,512))
    return pltpu.roll(x,0,1,stride=1,stride_axis=0)

def fwd_kernel(causal, limit_ref, hs_ref, bias_ref, q_ref, k_ref, v_ref, o_ref, lse_ref, km, qm, vt, s_scr, p_scr, t_scr):
    S=q_ref.shape[0]; M=k_ref.shape[0]
    limit=limit_ref[0]
    vtf=v_ref[...].astype(F32).T
    ones=jnp.ones((16,M),BF)
    for h in range(2):
        km[h]=mask_keys(k_ref[...],limit,h)
        qm[h]=mask_queries(q_ref[...],h)
        vt[h,0:64]=vtf[h*64:(h+1)*64].astype(BF)
        vt[h,64:80]=ones
        if causal:
            t=toeplitz(bias_ref[pl.ds(2*pl.program_id(0)+h,1),:])
            kk=lax.broadcasted_iota(jnp.int32,(TILE,512),0)
            qq=lax.broadcasted_iota(jnp.int32,(TILE,512),1)
            t_scr[h]=jnp.where(qq>=kk,t,NEG)
    nq=S//TILE; nk=M//TILE
    def soft(i,h):
        b=i%2
        qs=slice(i*TILE,(i+1)*TILE)
        tiles=range(i+1) if causal else range(nk)
        m=None
        for j in tiles:
            s=nt(km[h,j*TILE:(j+1)*TILE],qm[h,qs])
            if causal and j==i: s=s+t_scr[h,:,0:256]
            if causal and j==i-1: s=s+t_scr[h,:,256:512]
            s_scr[b,h,j*TILE:(j+1)*TILE]=s
            mj=jnp.max(s,axis=0,keepdims=True)
            m=mj if m is None else jnp.maximum(m,mj)
        m2=m*LOG2E
        for j in tiles:
            p_scr[b,h,j*TILE:(j+1)*TILE]=jnp.exp2(s_scr[b,h,j*TILE:(j+1)*TILE]*LOG2E-m2).astype(BF)
        return m2
    def mix(i,ms):
        b=i%2
        qs=slice(i*TILE,(i+1)*TILE)
        n=(i+1 if causal else nk)*TILE
        accs=[]
        for h in range(2):
            acc=nn(vt[h,:,0:n],p_scr[b,h,0:n])
            l=acc[64:65]
            lse_ref[0,h:h+1,qs]=ms[h]+jnp.log2(l)
            accs.append(acc[0:64]*((hs_ref[2*pl.program_id(0)+h] if causal else 1.0)/l))
        o_ref[qs]=jnp.concatenate(accs,axis=0).T.astype(BF)
    ms=None
    for i in range(nq+1):
        new=[soft(i,h) for h in range(2)] if i<nq else None
        if i>0: mix(i-1,ms)
        ms=new

def attn_fwd(causal, limit, hs, bias, q, k, v):
    S,D=q.shape; M=k.shape[0]
    pairs=D//128
    grid_spec=pltpu.PrefetchScalarGridSpec(
        num_scalar_prefetch=1, grid=(pairs,),
        in_specs=[SMEM,
                  pl.BlockSpec(bias.shape,lambda p,*_:(0,0)),
                  pl.BlockSpec((S,128),lambda p,*_:(0,p)),
                  pl.BlockSpec((M,128),lambda p,*_:(0,p)),
                  pl.BlockSpec((M,128),lambda p,*_:(0,p))],
        out_specs=[pl.BlockSpec((S,128),lambda p,*_:(0,p)),
                   pl.BlockSpec((1,2,S),lambda p,*_:(p,0,0))],
        scratch_shapes=[pltpu.VMEM((2,M,128),BF),pltpu.VMEM((2,S,128),BF),pltpu.VMEM((2,80,M),BF),
                        pltpu.VMEM((2,2,M,TILE),F32),pltpu.VMEM((2,2,M,TILE),BF),pltpu.VMEM((2,TILE,512),F32)])
    return pl.pallas_call(functools.partial(fwd_kernel,causal),grid_spec=grid_spec,
        out_shape=(jax.ShapeDtypeStruct((S,D),BF),jax.ShapeDtypeStruct((pairs,2,S),F32)),
        compiler_params=params(1),name="attn_fwd",
        cost_estimate=cost(4*S*M*D*(1 if causal else 2),8*S*D,S*M*D//128))(limit,hs,bias,q,k,v)

def bwd_kernel(causal, p0, chained, limit_ref, hs_ref, bias_ref, q_ref, k_ref, v_ref, go_ref, a_ref, lse_ref, *rest):
    if chained: rest=rest[5 if causal else 4:]
    pair=pl.program_id(0)+p0
    if causal:
        gq_ref, gk_ref, gv_ref, ds_ref, gb_ref, km, qm, q0, vm, gom, kt, p_scr, gs_scr, gqt, dl, t_scr, d_scr, far = rest
    else:
        gq_ref, gk_ref, gv_ref, ds_ref, km, qm, q0, vm, gom, kt, p_scr, gs_scr, gqt, dl = rest
    S=q_ref.shape[0]; M=k_ref.shape[0]
    nq=S//TILE; nk=M//TILE
    limit=limit_ref[0]
    kt[...]=k_ref[...].astype(F32).T.astype(BF)
    sel=jnp.concatenate([jnp.where(head_lanes(1,h),1.0,0.0) for h in range(2)]+[jnp.zeros((14,128),F32)],axis=0).astype(BF)
    x=go_ref[...].astype(F32)*a_ref[...].astype(F32)
    if causal:
        lane=lax.broadcasted_iota(jnp.int32,(1,128),1)
        x=x*(1.0/jnp.where(lane<64,jnp.full((1,128),hs_ref[2*pair],F32),jnp.full((1,128),hs_ref[2*pair+1],F32)))
    hi=x.astype(BF); lo=(x-hi.astype(F32)).astype(BF)
    dd=nt(sel,hi)+nt(sel,lo)
    dl[...]=dd[0:8]
    ds_ref[0]=jnp.broadcast_to(jnp.sum(dd[0:2],axis=1,keepdims=True),(2,128))
    zero=jnp.zeros((),F32)
    for h in range(2):
        km[h]=mask_keys(k_ref[...],limit,h)
        qm[h]=mask_queries(q_ref[...],h)
        own=head_lanes(S,h)
        q0[h]=jnp.where(own,q_ref[...].astype(F32),zero).astype(BF)
        gom[h]=jnp.where(own,go_ref[...].astype(F32),zero).astype(BF)
        vm[h]=jnp.where(head_lanes(M,h),v_ref[...].astype(F32),zero).astype(BF)
        if causal:
            t=toeplitz(bias_ref[pl.ds(2*pair+h,1),:])*LOG2E
            kk=lax.broadcasted_iota(jnp.int32,(TILE,512),0)
            qq=lax.broadcasted_iota(jnp.int32,(TILE,512),1)
            t_scr[h]=jnp.where(qq>=kk,t,NEG)
    if causal:
        d_scr[...]=jnp.zeros_like(d_scr); far[...]=jnp.zeros_like(far)
    gqt[...]=jnp.zeros_like(gqt)
    def scores(j,h):
        b=j%2
        js=slice(j*TILE,(j+1)*TILE)
        for i in range(j if causal else 0,nq):
            qs=slice(i*TILE,(i+1)*TILE)
            s=nt(km[h,js],qm[h,qs])*LOG2E
            if causal and i-j<2:
                s=s+t_scr[h,:,(i-j)*TILE:(i-j+1)*TILE]
            p=jnp.exp2(s-lse_ref[0,h:h+1,qs])
            gs=p*(nt(vm[h,js],go_ref[qs])-dl[h:h+1,qs])
            p_scr[b,h,:,qs]=p.astype(BF)
            gs_scr[b,h,:,qs]=gs.astype(BF)
            if causal:
                if i-j<2:
                    d_scr[h,:,(i-j)*TILE:(i-j+1)*TILE]+=gs
                else:
                    far[h]+=jnp.sum(gs.reshape(TILE//8,8,TILE),axis=0)
    def products(j,h):
        b=j%2
        js=slice(j*TILE,(j+1)*TILE)
        a=j*TILE if causal else 0
        if h==0:
            gv_ref[js]=(nn(p_scr[b,0,:,a:],gom[0,a:])+nn(p_scr[b,1,:,a:],gom[1,a:])).astype(BF)
            gqt[0:64,a:]+=nn(kt[0:64,js],gs_scr[b,0,:,a:])
        else:
            gk_ref[js]=(nn(gs_scr[b,0,:,a:],q0[0,a:])+nn(gs_scr[b,1,:,a:],q0[1,a:])).astype(BF)
            gqt[64:128,a:]+=nn(kt[64:128,js],gs_scr[b,1,:,a:])
    for j in range(nk+1):
        for h in range(2):
            if j<nk: scores(j,h)
            if j>0: products(j-1,h)
    gq_ref[...]=gqt[...].T.astype(BF)
    if causal:
        for h in range(2):
            acc=jnp.zeros((8,512),F32)
            for g in range(TILE//8):
                acc=acc+pltpu.roll(d_scr[h,8*g:8*g+8],(512-8*g)%512,1)
            near=jnp.zeros((1,512),F32)
            for r in range(8):
                near=near+pltpu.roll(acc[r:r+1],(512-r)%512,1)
            lane=lax.broadcasted_iota(jnp.int32,(1,512),1)
            tail=jnp.sum(jnp.where(lane>=255,near,0.0),axis=1,keepdims=True)+jnp.sum(jnp.sum(far[h],axis=0,keepdims=True),axis=1,keepdims=True)
            gb_ref[0,h:h+1,:]=jnp.where(lane[:,:256]==255,tail,near[:,:256])

def attn_bwd(causal, limit, hs, bias, q, k, v, go, a, lse, p0, count, before=None):
    S,D=q.shape; M=k.shape[0]
    pairs=D//128
    col=pl.BlockSpec((S,128),lambda p,*_:(0,p+p0))
    colm=pl.BlockSpec((M,128),lambda p,*_:(0,p+p0))
    outs=[col,colm,colm,pl.BlockSpec((1,2,128),lambda p,*_:(p+p0,0,0))]
    shapes=[jax.ShapeDtypeStruct((S,D),BF),jax.ShapeDtypeStruct((M,D),BF),jax.ShapeDtypeStruct((M,D),BF),jax.ShapeDtypeStruct((pairs,2,128),F32)]
    scr=[pltpu.VMEM((2,M,128),BF),pltpu.VMEM((2,S,128),BF),pltpu.VMEM((2,S,128),BF),pltpu.VMEM((2,M,128),BF),pltpu.VMEM((2,S,128),BF),
         pltpu.VMEM((128,M),BF),pltpu.VMEM((2,2,TILE,S),BF),pltpu.VMEM((2,2,TILE,S),BF),pltpu.VMEM((128,S),F32),pltpu.VMEM((8,S),F32)]
    if causal:
        outs.append(pl.BlockSpec((1,2,256),lambda p,*_:(p+p0,0,0))); shapes.append(jax.ShapeDtypeStruct((pairs,2,256),F32))
        scr+=[pltpu.VMEM((2,TILE,512),F32),pltpu.VMEM((2,TILE,512),F32),pltpu.VMEM((2,8,TILE),F32)]
    extra=() if before is None else tuple(before)
    grid_spec=pltpu.PrefetchScalarGridSpec(
        num_scalar_prefetch=1, grid=(count,),
        in_specs=[SMEM,pl.BlockSpec(bias.shape,lambda p,*_:(0,0)),
                  col,colm,colm,col,col,pl.BlockSpec((1,2,S),lambda p,*_:(p+p0,0,0))]+[pl.BlockSpec(memory_space=pl.ANY)]*len(extra),
        out_specs=outs, scratch_shapes=scr)
    return pl.pallas_call(functools.partial(bwd_kernel,causal,p0,before is not None),grid_spec=grid_spec,out_shape=tuple(shapes),
        input_output_aliases={9+i:i for i in range(len(extra))},
        cost_estimate=cost(10*S*M*D*(1 if causal else 2)*count//pairs,16*S*D*count//pairs,S*M*D//128),
        compiler_params=params(1),name="attn_bwd")(limit,hs,bias,q,k,v,go,a,lse,*extra)
EPS=1e-5
TASKS=4
def norm_rows(v):
    c=v-jnp.mean(v,axis=-1,keepdims=True)
    inv=lax.rsqrt(jnp.mean(c*c,axis=-1,keepdims=True)+EPS)
    return c*inv,inv
def norm_back(e,n,inv,g):
    s=e*g
    return (s-jnp.mean(s,axis=-1,keepdims=True)-n*jnp.mean(s*n,axis=-1,keepdims=True))*inv
def col_sum(v): return jnp.sum(v,axis=0,keepdims=True)

def vec(ref):
    return ref[...].reshape(1,-1)
def whole(shape):
    return pl.BlockSpec(shape,lambda *_:(0,)*len(shape),pipeline_mode=pl.Buffered(1))
def rows_of(rows,cols):
    return pl.BlockSpec((rows,cols),lambda i,*_:(i,0))

def pre_kernel(x_ref,m_ref,g_ref,b_ref,wq,qb,wk,wv,vb,ck,cv,cvb,q_o,k_o,v_o,k2_o,v2_o):
    n,_=norm_rows(x_ref[...].astype(F32))
    h=(n*vec(g_ref)+vec(b_ref)).astype(BF)
    q_o[...]=((nn(h,wq[...])+vec(qb))*0.125).astype(BF)
    k_o[...]=nn(h,wk[...]).astype(BF)
    v_o[...]=(nn(h,wv[...])+vec(vb)).astype(BF)
    m=m_ref[...]
    k2_o[...]=nn(m,ck[...]).astype(BF)
    v2_o[...]=(nn(m,cv[...])+vec(cvb)).astype(BF)

def pre(x,m,g,b,wq,qb,wk,wv,vb,ck,cv,cvb,T=256):
    S,D=x.shape
    r=rows_of(T,D); w=whole((D,D)); u=whole((D,))
    o=jax.ShapeDtypeStruct((S,D),BF)
    return pl.pallas_call(pre_kernel,grid=(S//T,),in_specs=[r,r,u,u,w,u,w,w,u,w,w,u],out_specs=[r]*5,out_shape=[o]*5,
        compiler_params=params(1),name="pre",cost_estimate=cost(10*S*D*D,10*D*D+14*S*D))(x,m,g,b,wq,qb,wk,wv,vb,ck,cv,cvb)

def post_kernel(a_ref,x_ref,wo,bo,pg,pb,ng,nb,wq,qb,x1_o,q2_o,n_o,inv_o):
    n,inv=norm_rows(nn(a_ref[...],wo[...])+vec(bo))
    n_o[...]=n.astype(BF); inv_o[...]=inv
    x1=x_ref[...].astype(F32)+(n*vec(pg)+vec(pb))
    x1_o[...]=x1
    n2,_=norm_rows(x1)
    h=(n2*vec(ng)+vec(nb)).astype(BF)
    q2_o[...]=((nn(h,wq[...])+vec(qb))*0.125).astype(BF)

def post(a,x,wo,bo,pg,pb,ng,nb,wq,qb,T=256):
    S,D=x.shape
    r=rows_of(T,D); w=whole((D,D)); u=whole((D,))
    o=jax.ShapeDtypeStruct((S,D),BF)
    return pl.pallas_call(post_kernel,grid=(S//T,),in_specs=[r,r,w,u,u,u,u,u,w,u],
        out_specs=[r,r,r,rows_of(T,1)],out_shape=[jax.ShapeDtypeStruct((S,D),F32),o,o,jax.ShapeDtypeStruct((S,1),F32)],
        compiler_params=params(1),name="post",cost_estimate=cost(4*S*D*D,4*D*D+12*S*D))(a,x,wo,bo,pg,pb,ng,nb,wq,qb)

SQH=0.7071067811865476
ERFC=(-1.26551223,1.00002368,0.37409196,0.09678418,-0.18628806,0.27886807,-1.13520398,1.48851587,-0.82215223,0.17087277)
def gelu_parts(f):
    z=jnp.abs(f)*SQH
    t=1.0/(1.0+0.5*z)
    poly=jnp.full_like(t,ERFC[9]*LOG2E)
    for c in ERFC[8::-1]:
        poly=poly*t+c*LOG2E
    zz=z*z*LOG2E
    half=0.5*t*jnp.exp2(poly-zz)
    phi=jnp.where(f<0.0,half,1.0-half)
    dens=jnp.exp2(-zz)*0.3989422804014327
    return f*phi, phi+f*dens

CH=256
def mid_kernel(n,dec_ref,gb_ref,idx_ref,all_ref,a2_ref,x1_ref,og_ref,cwo,wi,wout,cbo,cpg,cpb,fng,fnb,bi,mg,mb,bo,
               lo_o,gx2_o,go2_o,u_o,gf_o,h3_o,g3_o,gb2_o,v1_o,v3_o,fac_o,ge,dg,gus):
    T,D=a2_ref.shape; FF=wi.shape[1]
    bi_v=vec(bi); mg_v=vec(mg); mb_v=vec(mb)
    step=pl.program_id(0)
    row=step*T+lax.broadcasted_iota(jnp.int32,(T,1),0)
    valid=row<dec_ref[0]
    n_b,inv_b=norm_rows(nn(a2_ref[...],cwo[...])+vec(cbo))
    x2=x1_ref[...]+(n_b*vec(cpg)+vec(cpb))
    n_x,inv_x=norm_rows(x2)
    h3=(n_x*vec(fng)+vec(fnb)).astype(BF)
    h3_o[...]=h3
    part=jnp.zeros((T,128),F32)
    for c in range(0,FF,CH):
        f=nn(h3,wi[:,c:c+CH])+bi_v[:,c:c+CH]
        a,d=gelu_parts(f)
        ge[:,c:c+CH]=a
        dg[:,c:c+CH]=d
        for l in range(0,CH,128): part=part+a[:,l:l+128]
    mean=jnp.sum(part,axis=1,keepdims=True)*(1.0/FF)
    part=jnp.zeros((T,128),F32)
    for c in range(0,FF,CH):
        e=ge[:,c:c+CH]-mean
        e=e*e
        for l in range(0,CH,128): part=part+e[:,l:l+128]
    inv=lax.rsqrt(jnp.sum(part,axis=1,keepdims=True)*(1.0/FF)+EPS)
    g3=jnp.where(valid,og_ref[...].astype(F32),0.0)
    g3b=g3.astype(BF)
    g3_o[...]=g3b
    s1=jnp.zeros((T,128),F32); s2=jnp.zeros((T,128),F32)
    @pl.when(step==0)
    def _():
        v1_o[...]=jnp.zeros_like(v1_o); v3_o[...]=jnp.zeros_like(v3_o)
        owner=lax.broadcasted_iota(jnp.int32,(n,8,128),0)
        task=sum((owner>=gb_ref[k]).astype(jnp.int32) for k in range(1,TASKS))
        mine=sum((idx_ref[0]>=gb_ref[k]).astype(jnp.int32) for k in range(1,TASKS))
        fac_o[...]=n/jnp.sum(jnp.where(task==mine,all_ref[...],0.0),axis=0)
    for c in range(0,FF,CH):
        cs=slice(c,c+CH)
        n=(ge[:,cs]-mean)*inv
        u_o[:,cs]=(n*mg_v[:,cs]+mb_v[:,cs]).astype(BF)
        gu=nt(g3b,wout[cs,:])
        en=gu*n
        v3_o[0:1,cs]+=col_sum(en)
        v3_o[1:2,cs]+=col_sum(gu)
        eg=gu*mg_v[:,cs]
        gus[:,cs]=eg
        egn=eg*n
        for l in range(0,CH,128):
            s1=s1+eg[:,l:l+128]; s2=s2+egn[:,l:l+128]
    m1=jnp.sum(s1,axis=1,keepdims=True)*(1.0/FF); m2=jnp.sum(s2,axis=1,keepdims=True)*(1.0/FF)
    out=x2+(nn(u_o[...],wout[...])+vec(bo))
    lo_o[...]=jnp.where(valid,out,0.0).astype(BF)
    slope=inv*m2; level=m1-mean*slope
    for c in range(0,FF,CH):
        cs=slice(c,c+CH)
        gf=((gus[:,cs]-level-ge[:,cs]*slope)*inv*dg[:,cs]).astype(BF)
        gf_o[:,cs]=gf
        v3_o[2:3,cs]+=col_sum(gf.astype(F32))
    gh=nt(gf_o[...],wi[...])
    v1_o[0:1]+=col_sum(gh*n_x); v1_o[1:2]+=col_sum(gh)
    gx2=g3+norm_back(gh,n_x,inv_x,vec(fng))
    gx2_o[...]=gx2
    v1_o[2:3]+=col_sum(g3)
    v1_o[3:4]+=col_sum(gx2*n_b); v1_o[4:5]+=col_sum(gx2)
    gb2=norm_back(gx2,n_b,inv_b,vec(cpg)).astype(BF)
    gb2_o[...]=gb2
    v1_o[5:6]+=col_sum(gb2.astype(F32))
    go2_o[...]=nt(gb2,cwo[...]).astype(BF)

def mid(n,dec,gb,idx,all_dec,a2,x1,og,cwo,wi,wout,cbo,cpg,cpb,fng,fnb,bi,mg,mb,bo,T=256):
    S,D=x1.shape; FF=wi.shape[1]
    r=rows_of(T,D); rf=rows_of(T,FF); u=whole((D,)); uf=whole((FF,))
    sd=jax.ShapeDtypeStruct
    acc=lambda s: pl.BlockSpec(s,lambda *_:(0,0))
    return pl.pallas_call(functools.partial(mid_kernel,n),grid=(S//T,),
        in_specs=[SMEM,SMEM,SMEM,whole((n,8,128)),r,r,r,whole((D,D)),whole((D,FF)),whole((FF,D)),u,u,u,u,u,uf,uf,uf,u],
        out_specs=[r,r,r,rf,rf,r,r,r,acc((8,D)),acc((8,FF)),acc((8,128))],
        out_shape=[sd((S,D),BF),sd((S,D),F32),sd((S,D),BF),sd((S,FF),BF),sd((S,FF),BF),sd((S,D),BF),sd((S,D),BF),sd((S,D),BF),sd((8,D),F32),sd((8,FF),F32),sd((8,128),F32)],
        scratch_shapes=[pltpu.VMEM((T,FF),F32)]*3,
        compiler_params=params(1,58),name="mid",
        cost_estimate=cost(8*S*D*FF+4*S*D*D,4*D*FF+2*D*D+S*D*20+4*S*FF,S*FF*3))(dec,gb,idx,all_dec,a2,x1,og,cwo,wi,wout,cbo,cpg,cpb,fng,fnb,bi,mg,mb,bo)

def head_row(hs_ref,D,H):
    lane=lax.broadcasted_iota(jnp.int32,(1,D),1)//(D//H)
    v=jnp.zeros((1,D),F32)
    for h in range(H): v=jnp.where(lane==h,hs_ref[h],v)
    return v
def cross_back_kernel(hs_ref,gq_ref,x1_ref,gx2_ref,n_ref,inv_ref,gv_ref,cwq,wo,cng,cnb,spg,
                      gx1_o,go1_o,h2_o,gqs_o,gb1_o,v_o):
    @pl.when(pl.program_id(0)==0)
    def _(): v_o[...]=jnp.zeros_like(v_o)
    gq=gq_ref[...]*jnp.asarray(0.125,BF)
    gqs_o[...]=gq
    n,inv=norm_rows(x1_ref[...])
    h2_o[...]=(n*vec(cng)+vec(cnb)).astype(BF)
    gh=nt(gq,cwq[...])
    v_o[0:1]+=col_sum(gh*n); v_o[1:2]+=col_sum(gh)
    v_o[2:3]+=col_sum(gq.astype(F32)); v_o[3:4]+=col_sum(gv_ref[...].astype(F32))
    gx1=gx2_ref[...]+norm_back(gh,n,inv,vec(cng))
    gx1_o[...]=gx1
    nb=n_ref[...].astype(F32)
    v_o[4:5]+=col_sum(gx1*nb); v_o[5:6]+=col_sum(gx1)
    gb1=norm_back(gx1,nb,inv_ref[...],vec(spg)).astype(BF)
    gb1_o[...]=gb1
    v_o[6:7]+=col_sum(gb1.astype(F32))
    go1_o[...]=(nt(gb1,wo[...])*head_row(hs_ref,gb1.shape[1],hs_ref.shape[0])).astype(BF)

def cross_back(hs,gq,x1,gx2,n,inv,gv,cwq,wo,cng,cnb,spg,T=256):
    S,D=x1.shape
    r=rows_of(T,D); w=whole((D,D)); u=whole((D,))
    sd=jax.ShapeDtypeStruct
    return pl.pallas_call(cross_back_kernel,grid=(S//T,),in_specs=[SMEM,r,r,r,r,rows_of(T,1),r,w,w,u,u,u],
        out_specs=[r,r,r,r,r,pl.BlockSpec((8,D),lambda *_:(0,0))],
        out_shape=[sd((S,D),F32)]+[sd((S,D),BF)]*4+[sd((8,D),F32)],
        compiler_params=params(1),name="cross_back",cost_estimate=cost(4*S*D*D,4*D*D+28*S*D))(hs,gq,x1,gx2,n,inv,gv,cwq,wo,cng,cnb,spg)

PLACE=(15,16,13,14,12,10,11,6,7,8,9,5,3,4,0,1,2)
WIDE_ROW=17; BUCKET_LANE=32; HEAD_LANE=64
def tail_kernel(n,core_ref,fac_ref,hs_ref,x_ref,gx1_ref,gq_ref,gk_ref,gv_ref,wq,wk,wv,g_ref,b_ref,va,vb,vf,gb,ds,
                gt_o,h_o,gqs_o,keep_o,send_o,v_s,f_s,p_s,t_s):
    D=x_ref.shape[1]; H=hs_ref.shape[0]; FF=vf.shape[1]
    step=pl.program_id(0)
    @pl.when(step==0)
    def _():
        v_s[...]=jnp.zeros_like(v_s); f_s[...]=jnp.zeros_like(f_s); p_s[...]=jnp.zeros_like(p_s)
        v_s[0:6,0:D]=va[0:6]
        v_s[6:13,0:D]=vb[0:7]
        f_s[1:4,0:FF]=vf[0:3]
        for h in range(H): p_s[h:h+1]=gb[h//2,h%2:h%2+1,:]
    n_x,inv=norm_rows(x_ref[...].astype(F32))
    h_o[...]=(n_x*vec(g_ref)+vec(b_ref)).astype(BF)
    gq=gq_ref[...]*jnp.asarray(0.125,BF)
    gqs_o[...]=gq
    gh=nt(gq,wq[...])+nt(gk_ref[...],wk[...])+nt(gv_ref[...],wv[...])
    v_s[13:14,0:D]+=col_sum(gq.astype(F32)); v_s[14:15,0:D]+=col_sum(gv_ref[...].astype(F32))
    v_s[15:16,0:D]+=col_sum(gh*n_x); v_s[16:17,0:D]+=col_sum(gh)
    gt_o[...]=gx1_ref[...]+norm_back(gh,n_x,inv,vec(g_ref))
    @pl.when(step==pl.num_programs(0)-1)
    def _():
        fac=fac_ref[0:1,0:1]
        w=D//n; f=FF//n; b=256//n
        row=lax.broadcasted_iota(jnp.int32,(24,128),0); lane=lax.broadcasted_iota(jnp.int32,(24,128),1)
        heads=jnp.zeros((24,128),F32)
        for h in range(H):
            heads=jnp.where((row==h)&(lane==HEAD_LANE),ds[h//2,h%2:h%2+1,:]*(1.0/jnp.full((1,1),hs_ref[h],F32)),heads)
        def window(ref,rows,at):
            lo=at//128*128
            v=ref[0:rows,lo:lo+256]
            return v if at==lo else pltpu.roll(v,256-(at-lo),1)
        for dev in range(n):
            t=jnp.where(lane<w,window(v_s,24,w*dev)[:,:128],heads)
            p=pltpu.roll(p_s[...],(256-b*dev+BUCKET_LANE)%256,1)[:,:128]
            p=jnp.where((lane[:16]>=BUCKET_LANE)&(lane[:16]<BUCKET_LANE+b),p,t[0:16])
            u=t[16:24]+jnp.where((lane[:8]<f)&(row[:8]>0)&(row[:8]<4),window(f_s,8,f*dev)[:,:128],0.0)
            t_s[dev,0:16]=p*fac
            t_s[dev,16:24]=u*fac
        core=core_ref[0]
        for k in range(n//2):
            keep_o[k]=t_s[2*k+core]
            send_o[k]=t_s[2*k+1-core]
def tail(n,core,fac,hs,x,gx1,gq,gk,gv,wq,wk,wv,g,b,va,vb,vf,gb,ds,T=256):
    S,D=x.shape; FF=vf.shape[1]
    r=rows_of(T,D); w=whole((D,D)); u=whole((D,)); sd=jax.ShapeDtypeStruct
    tile=pl.BlockSpec((n//2,24,128),lambda *_:(0,0,0))
    return pl.pallas_call(functools.partial(tail_kernel,n),grid=(S//T,),
        in_specs=[SMEM,whole((8,128)),SMEM]+[r]*5+[w]*3+[u]*2+[whole(v.shape) for v in (va,vb,vf,gb,ds)],
        out_specs=[r,r,r,tile,tile],
        out_shape=[sd((S,D),F32),sd((S,D),BF),sd((S,D),BF),sd((n//2,24,128),F32),sd((n//2,24,128),F32)],
        scratch_shapes=[pltpu.VMEM((24,D+128),F32),pltpu.VMEM((8,FF+128),F32),pltpu.VMEM((16,256),F32),pltpu.VMEM((n,24,128),F32)],
        compiler_params=params(1),name="tail",cost_estimate=cost(6*S*D*D,6*D*D+S*D*18))(core,fac,hs,x,gx1,gq,gk,gv,wq,wk,wv,g,b,va,vb,vf,gb,ds)
def memory_kernel(k_ref,v_ref,ck,cv,o):
    o[...]=nt(k_ref[...],ck[...])+nt(v_ref[...],cv[...])
def memory_grad(gk,gv,ck,cv,T=256):
    S,D=gk.shape
    r=rows_of(T,D); w=whole((D,D))
    return pl.pallas_call(memory_kernel,grid=(S//T,),in_specs=[r,r,w,w],out_specs=r,out_shape=jax.ShapeDtypeStruct((S,D),F32),
        compiler_params=params(1),name="memory",cost_estimate=cost(1000,1000))(gk,gv,ck,cv)

def part_rows(scr,core,keep_o,send_o):
    groups,r=keep_o.shape[:2]
    for t in range(groups):
        if r%8==0:
            keep_o[t]=scr[pl.ds((2*t+core)*r,r),:]
            send_o[t]=scr[pl.ds((2*t+1-core)*r,r),:]
        else:
            even=scr[2*t*r:(2*t+1)*r,:]
            odd=scr[(2*t+1)*r:(2*t+2)*r,:]
            keep_o[t]=jnp.where(core==0,even,odd)
            send_o[t]=jnp.where(core==0,odd,even)
def wrow_kernel(core_ref,fac_ref,l_ref,r_ref,keep_o,send_o,scr):
    scr[...]=tn(l_ref[...],r_ref[...])*fac_ref[0:1,0:1]
    part_rows(scr,core_ref[0],keep_o,send_o)
def wgrad_rows(core,fac,lhs,rhs,n,B=768):
    S,M=lhs.shape; N=rhs.shape[1]; r=M//n; steps=M//B; groups=B//r//2
    o=pl.BlockSpec((groups,r,N),lambda i:(i,0,0)); sh=jax.ShapeDtypeStruct((n//2,r,N),F32)
    return pl.pallas_call(wrow_kernel,grid=(steps,),
        in_specs=[SMEM,whole((8,128)),pl.BlockSpec((S,B),lambda i:(0,i)),whole((S,N))],
        out_specs=[o,o],scratch_shapes=[pltpu.VMEM((B,N),F32)],out_shape=[sh,sh],compiler_params=params(1),name="wgrad",
        cost_estimate=cost(4*S*M*N,2*S*(M+N)+4*M*N))(core,fac,lhs,rhs)
def wcol_kernel(plan,core_ref,fac_ref,*refs):
    ins=refs[:-3]; keep_o,send_o,scr=refs[-3:]
    step=pl.program_id(0)
    for l,r,first,last in plan:
        @pl.when((step>=first)&(step<last))
        def _(): scr[...]=tn(ins[l][...],ins[r][...])*fac_ref[0:1,0:1]
    part_rows(scr,core_ref[0],keep_o,send_o)
def wgrad_cols(core,fac,pairs,n,B=768,weight=1.0):
    ins=[]; specs=[]; plan=[]; at=0; seen={}
    S,M=pairs[0][0].shape
    for lhs,rhs in pairs:
        if id(lhs) not in seen:
            seen[id(lhs)]=len(ins); ins.append(lhs); specs.append(whole((S,M)))
        steps=rhs.shape[1]//B
        plan.append((seen[id(lhs)],len(ins),at,at+steps))
        ins.append(rhs)
        specs.append(pl.BlockSpec((S,B),functools.partial(lambda at,steps,i:(0,jnp.clip(i-at,0,steps-1)),at,steps)))
        at+=steps
    N=at*B; r=M//n
    o=pl.BlockSpec((n//2,r,B),lambda i:(0,0,i)); sh=jax.ShapeDtypeStruct((n//2,r,N),F32)
    return pl.pallas_call(functools.partial(wcol_kernel,plan),grid=(at,),in_specs=[SMEM,whole((8,128))]+specs,
        out_specs=[o,o],scratch_shapes=[pltpu.VMEM((M,B),F32)],out_shape=[sh,sh],compiler_params=params(1),name="wgrad",
        cost_estimate=cost(4*S*M*N*weight,(2*S*M*len(ins)+4*M*N)*weight))(core,fac,*ins)

def halve_kernel(count,bit_ref,*refs):
    for c in range(count):
        km,ko,gm,go=refs[4*c:4*c+4]
        keep_o,send_o=refs[4*count+2*c:4*count+2*c+2]
        send_o[...]=ko[:,0]+go[:,0]
        keep_o[...]=km[:,0]+gm[:,0]
def halve(bits,chains):
    specs=[];ins=[];outs=[];shapes=[]
    size=sum(4*keep.size//parts for keep,got,part,parts in chains)
    steps=min([4 if size>8e6 else 2]+[keep.shape[0] for keep,*_ in chains])
    for c,(keep,got,part,parts) in enumerate(chains):
        A,_,B,r,C=keep.shape
        C=C//parts; K=A//steps
        for flip in (False,True,False,True):
            specs.append(pl.BlockSpec((K,1,B,r,C),functools.partial(lambda c,flip,part,i,b:(i,1-b[c] if flip else b[c],0,0,part),c,flip,part)))
        ins+=[keep,keep,got,got]
        outs+=[pl.BlockSpec((K,B,r,C),lambda i,b:(i,0,0,0))]*2
        shapes+=[jax.ShapeDtypeStruct((A,B,r,C),F32)]*2
    gs=pltpu.PrefetchScalarGridSpec(num_scalar_prefetch=1,grid=(steps,),in_specs=specs,out_specs=outs)
    return pl.pallas_call(functools.partial(halve_kernel,len(chains)),grid_spec=gs,out_shape=shapes,compiler_params=params(1),name="halve",
        cost_estimate=cost(1000,1000))(bits,*ins)

def deal_kernel(count,z_ref,*refs):
    outs=refs[8*count:]
    for m,o in enumerate(outs):
        at=0
        for c in range(count):
            k,g=refs[8*c+m],refs[8*c+4+m]
            o[:,at:at+k.shape[-1]]=k[0]+g[0]
            at+=k.shape[-1]
def deal(z,chains):
    r=chains[0][0].shape[1]; C=sum(k.shape[2] for k,_ in chains)
    specs=[];ins=[]
    for k,g in chains:
        specs+=[pl.BlockSpec((1,r,k.shape[2]),lambda i,z,m=m:(z[0]^m,0,0)) for m in range(4)]*2
        ins+=[k]*4+[g]*4
    o=pl.BlockSpec((r,C),lambda i,z:(0,0)); sh=jax.ShapeDtypeStruct((r,C),F32)
    gs=pltpu.PrefetchScalarGridSpec(num_scalar_prefetch=1,grid=(1,),in_specs=specs,out_specs=[o]*4)
    return pl.pallas_call(functools.partial(deal_kernel,len(chains)),grid_spec=gs,out_shape=[sh]*4,compiler_params=params(1),name="deal",
        cost_estimate=cost(1000,1000))(z,*ins)

def finish_kernel(n,plan,tile,*refs):
    count=len(plan)+22
    ins=refs[:-count]; outs=refs[-count:]
    total=lambda c,lo,hi: (ins[4*c][:,lo:hi]+ins[4*c+1][:,lo:hi])+(ins[4*c+2][:,lo:hi]+ins[4*c+3][:,lo:hi])
    for o,(c,lo,hi) in zip(outs,plan):
        o[...]=total(c,lo,hi)
    t=total(*tile)
    outs=outs[len(plan):]
    for r,o in zip(PLACE,outs): o[...]=t[r:r+1,:o.shape[0]].reshape(o.shape[0])
    for k in range(3):
        o=outs[17+k]
        o[...]=t[WIDE_ROW+k:WIDE_ROW+k+1,:o.shape[0]].reshape(o.shape[0])
    H,b=outs[20].shape
    outs[20][...]=pltpu.roll(t,128-BUCKET_LANE,1)[:H,:b]
    x=pltpu.roll(t,128-HEAD_LANE,1)[0:16,0:1]
    eye=lax.broadcasted_iota(jnp.int32,(16,128),0)==lax.broadcasted_iota(jnp.int32,(16,128),1)
    outs[21][...]=col_sum(jnp.where(eye,x,0.0))[:,:H].reshape(H)
def finish(n,groups,plan,tile,D,FF,H):
    ins=[v for g in groups for v in g]
    sd=jax.ShapeDtypeStruct
    shapes=[sd((ins[4*c].shape[0],hi-lo),F32) for c,lo,hi in plan]+[sd((D//n,),F32)]*17+[sd((FF//n,),F32)]*3+[sd((H,256//n),F32),sd((H,),F32)]
    return pl.pallas_call(functools.partial(finish_kernel,n,plan,tile),in_specs=[pl.BlockSpec(v.shape) for v in ins],out_shape=shapes,
        compiler_params=params(0),name="finish",cost_estimate=cost(1000,1000))(*ins)

def swap(x,n,bit):
    return lax.ppermute(x,"dp",[(j,j^(1<<bit)) for j in range(n)])
def after(token,*vals):
    return lax.optimization_barrier(tuple(vals)+tuple(token))[:len(vals)]
class Halving:
    def __init__(self,n,keep,send,order):
        self.n,self.order=n,list(order)
        self.live=list(range(n.bit_length()-2,0,-1))
        self.keep=keep; self.got=swap(send,n,0); self.part=(0,1)
    def split(self,orders):
        chains=[]
        for k,order in enumerate(orders):
            h=object.__new__(Halving)
            h.n,h.order,h.live=self.n,list(order),list(self.live)
            h.keep,h.got,h.part=self.keep,self.got,(k,len(orders))
            chains.append(h)
        return chains
def step(token,index,*chains):
    bits=[];work=[]
    flat=after(token,*[v for c in chains for v in (c.keep,c.got)])
    for k,c in enumerate(chains):
        b=c.order.pop(0)
        axis=c.live.index(b)
        c.live.remove(b)
        keep,got=flat[2*k:2*k+2]
        shape=(2**axis,2,2**(len(c.live)-axis))+keep.shape[-2:]
        bits.append((b,(index>>b)&1))
        work.append((keep.reshape(shape),got.reshape(shape))+c.part)
    outs=halve(jnp.stack([v for _,v in bits]).astype(jnp.int32),work)
    for k,c in enumerate(chains):
        c.keep,c.part=outs[2*k],(0,1)
        c.got=swap(outs[2*k+1],c.n,bits[k][0])
    return [outs[2*k+1] for k in range(len(chains))]
def last_step(token,index,zs,*chains):
    flat=after(token,*[v for c in chains for v in (c.keep,c.got)])
    z=((index>>zs[0])&3).reshape(1).astype(jnp.int32)
    cut=lambda v: v.reshape((4,)+v.shape[-2:])
    own,*sends=deal(z,[(cut(flat[2*k]),cut(flat[2*k+1])) for k in range(len(chains))])
    n=chains[0].n
    return [own]+[lax.ppermute(s,"dp",[(j,j^((m+1)<<zs[0])) for j in range(n)]) for m,s in enumerate(sends)]

def shards(n,tokens,memory,out_grad,dec_len,mem_len,group_bounds,
           self_norm_gain,self_norm_bias,self_query,self_query_bias,self_key,self_value,self_value_bias,self_output,self_output_bias,
           position_bias,head_scale,self_post_gain,self_post_bias,cross_norm_gain,cross_norm_bias,cross_query,cross_query_bias,
           cross_key,cross_value,cross_value_bias,cross_output,cross_output_bias,cross_post_gain,cross_post_bias,
           feed_norm_gain,feed_norm_bias,feed_inner,feed_inner_bias,feed_mid_gain,feed_mid_bias,feed_outer,feed_outer_bias):
    bits=n.bit_length()-1
    xs,ys,zs=([1],[2],[3,4]) if bits==5 else ([1,2],[3,4],list(range(5,bits)))
    order_a=xs+ys; order_b=ys+xs
    index=lax.axis_index("dp")
    idx=index.reshape(1).astype(jnp.int32)
    core=idx&1
    x=tokens[0]; m=memory[0]; og=out_grad[0]
    S,D=x.shape
    H=head_scale.shape[0]; pairs=H//2
    all_dec=lax.all_to_all(jnp.broadcast_to(dec_len.astype(F32).reshape(1,1,1),(n,8,128)),"dp",0,0,tiled=True)
    q1,k1,v1,k2,v2=pre(x,m,self_norm_gain,self_norm_bias,self_query,self_query_bias,self_key,self_value,self_value_bias,cross_key,cross_value,cross_value_bias)
    a1,lse1=attn_fwd(True,dec_len,head_scale,position_bias,q1,k1,v1)
    x1,q2,nb1,ib1=post(a1,x,self_output,self_output_bias,self_post_gain,self_post_bias,cross_norm_gain,cross_norm_bias,cross_query,cross_query_bias)
    a2,lse2=attn_fwd(False,mem_len,head_scale,position_bias,q2,k2,v2)
    lo,gx2,go2,u,gf,h3,g3,gb2,va,vf,fac=mid(n,dec_len,group_bounds,idx,all_dec,a2,x1,og,cross_output,feed_inner,feed_outer,cross_output_bias,cross_post_gain,cross_post_bias,feed_norm_gain,feed_norm_bias,feed_inner_bias,feed_mid_gain,feed_mid_bias,feed_outer_bias)
    keep,send=wgrad_cols(core,fac,[(h3,gf),(a2,gb2)],n)
    fi=Halving(n,keep,send,order_b)
    u,=after([send],u)
    keep,send=wgrad_rows(core,fac,u,g3,n)
    fo=Halving(n,keep,send,order_a)
    t=step([send],index,fi)
    t=step(t,index,fo)
    go2,=after(t,go2)
    gq2,gk2,gv2,_=attn_bwd(False,mem_len,head_scale,position_bias,q2,k2,v2,go2,a2,lse2,0,pairs)
    gx1,go1,h2,gqs2,gb1,vb=cross_back(head_scale,gq2,x1,gx2,nb1,ib1,gv2,cross_query,self_output,cross_norm_gain,cross_norm_bias,self_post_gain)
    t=step([vb],index,fo)
    h2,=after(t,h2)
    keep,send=wgrad_cols(core,fac,[(h2,gqs2),(m,gv2),(m,gk2),(a1,gb1)],n)
    g2=Halving(n,keep,send,[])
    t=step([send],index,fi)
    go1,=after(t,go1)
    half=pairs//2
    back=attn_bwd(True,dec_len,head_scale,position_bias,q1,k1,v1,go1,a1,lse1,0,half)
    t=[back[3]]
    while fo.order: t=step(t,index,fo)
    r_fo=last_step(t,index,zs,fo)
    ga,gb_=g2.split([order_a,order_b])
    t=step([r_fo[0]],index,ga,gb_)
    go1,=after(t,go1)
    gq1,gk1,gv1,ds,gb=attn_bwd(True,dec_len,head_scale,position_bias,q1,k1,v1,go1,a1,lse1,half,pairs-half,back)
    t=[ds]
    while fi.order: t=step(t,index,fi)
    r_fi=last_step(t,index,zs,fi)
    gx1,=after([r_fi[0]],gx1)
    gt,h1,gqs1,keep,send=tail(n,core,fac,head_scale,x,gx1,gq1,gk1,gv1,self_query,self_key,self_value,self_norm_gain,self_norm_bias,va,vb,vf,gb,ds)
    sv=Halving(n,keep,send,order_a)
    h1,=after([send]+r_fo[1:],h1)
    keep,send=wgrad_cols(core,fac,[(h1,gqs1),(h1,gv1),(h1,gk1)],n)
    g3_=Halving(n,keep,send,[])
    t=[send]
    while ga.order: t=step(t,index,ga,gb_)
    gk2,=after(t+r_fi[1:],gk2)
    gm=memory_grad(gk2,gv2,cross_key,cross_value)
    sa,sb=g3_.split([order_a,order_b])
    t=step([gm,ga.got,gb_.got],index,sa,sb,sv)
    r_g2=last_step(t,index,zs,ga,gb_)
    t=r_g2
    while sa.order: t=step(t,index,sa,sb,sv)
    FF=feed_inner.shape[1]
    if sv.keep.shape[-2]==sa.keep.shape[-2]:
        groups=[last_step(t,index,zs,sa,sb,sv)]
        tile=(3,3*D,3*D+128)
    else:
        groups=[last_step(t,index,zs,sa,sb),last_step(t,index,zs,sv)]
        tile=(4,0,128)
    g_fo,g_fi,g_co,g_cq,g_cv,g_ck,g_so,g_sq,g_sv,g_sk,*small=finish(n,[r_fo,r_fi,r_g2]+groups,[
        (0,0,D),(1,0,FF),(1,FF,FF+D),(2,0,D),(2,D,2*D),(2,2*D,3*D),(2,3*D,4*D),(3,0,D),(3,D,2*D),(3,2*D,3*D)],tile,D,FF,H)
    (sng,snb,sqb,svb,sob,spg,spb,cng,cnb,cqb,cvb,cob,cpg,cpb,fng,fnb,fob,fmg,fmb,fib,gpos,ghs)=small
    fo_b=fob
    return (lo[None],gt[None],gm[None],
        sng,snb,g_sq,sqb,g_sk,g_sv,svb,g_so,sob,gpos,ghs,spg,spb,cng,cnb,g_cq,cqb,g_ck,g_cv,cvb,g_co,cob,cpg,cpb,
        fng,fnb,g_fi,fib,fmg,fmb,g_fo,fo_b)

def solution(mesh):
    n=mesh.shape["dp"]
    vec=P("dp"); mat=P("dp",None); cube=P("dp",None,None)
    return jax.shard_map(functools.partial(shards,n),mesh=mesh,in_specs=(cube,cube,cube,vec,vec)+(P(),)*33,
        out_specs=(cube,cube,cube,vec,vec,mat,vec,mat,mat,vec,mat,vec,P(None,"dp"),P(),vec,vec,vec,vec,mat,vec,
                   mat,mat,vec,mat,vec,vec,vec,vec,vec,mat,vec,vec,vec,mat,vec),check_vma=False)
```

```python
import functools
import jax, jax.numpy as jnp
from jax import lax
from jax.experimental import pallas as pl
from jax.experimental.pallas import tpu as pltpu
from jax.sharding import PartitionSpec as P
F32=jnp.float32; BF=jnp.bfloat16
LOG2E=1.4426950408889634
NEG=-1e30
TILE=256
SMEM=pl.BlockSpec(memory_space=pltpu.SMEM)
def cost(flops,nbytes,trans=0):
    return pl.CostEstimate(flops=int(flops)*200,bytes_accessed=int(nbytes)*200,transcendentals=int(trans))
def nt(a,b): return lax.dot_general(a,b,(((1,),(1,)),((),())),preferred_element_type=F32)
def nn(a,b): return lax.dot_general(a,b,(((1,),(0,)),((),())),preferred_element_type=F32)
def tn(a,b): return lax.dot_general(a,b,(((0,),(0,)),((),())),preferred_element_type=F32)
def params(n, mb=56, sem=None):
    return pltpu.CompilerParams(dimension_semantics=("arbitrary",)*n, vmem_limit_bytes=mb<<20)

def head_lanes(rows, h):
    lane=lax.broadcasted_iota(jnp.int32,(rows,128),1)
    return (lane<64) if h==0 else (lane>=64)

def mask_keys(k, limit, h):
    rows=k.shape[0]
    lane=lax.broadcasted_iota(jnp.int32,(rows,128),1)
    row=lax.broadcasted_iota(jnp.int32,(rows,128),0)
    spare=64 if h==0 else 0
    pen=jnp.where((lane==spare)&(row>=limit), NEG, 0.0)
    own=head_lanes(rows,h)
    return jnp.where(own,k.astype(F32),pen).astype(BF)
def mask_queries(q, h):
    rows=q.shape[0]
    lane=lax.broadcasted_iota(jnp.int32,(rows,128),1)
    spare=64 if h==0 else 0
    one=jnp.where(lane==spare,1.0,0.0)
    return jnp.where(head_lanes(rows,h),q.astype(F32),one).astype(BF)

def toeplitz(bias_row):
    r=jnp.concatenate([bias_row-bias_row[:,255:256], jnp.zeros((1,256),F32)],axis=1)
    x=jnp.broadcast_to(r,(TILE,512))
    return pltpu.roll(x,0,1,stride=1,stride_axis=0)

def fwd_kernel(causal, limit_ref, hs_ref, bias_ref, q_ref, k_ref, v_ref, o_ref, lse_ref, km, qm, vt, s_scr, p_scr, t_scr):
    S=q_ref.shape[0]; M=k_ref.shape[0]
    limit=limit_ref[0]
    vtf=v_ref[...].astype(F32).T
    ones=jnp.ones((16,M),BF)
    for h in range(2):
        km[h]=mask_keys(k_ref[...],limit,h)
        qm[h]=mask_queries(q_ref[...],h)
        vt[h,0:64]=vtf[h*64:(h+1)*64].astype(BF)
        vt[h,64:80]=ones
        if causal:
            t=toeplitz(bias_ref[pl.ds(2*pl.program_id(0)+h,1),:])
            kk=lax.broadcasted_iota(jnp.int32,(TILE,512),0)
            qq=lax.broadcasted_iota(jnp.int32,(TILE,512),1)
            t_scr[h]=jnp.where(qq>=kk,t,NEG)
    nq=S//TILE; nk=M//TILE
    def soft(i,h):
        b=i%2
        qs=slice(i*TILE,(i+1)*TILE)
        tiles=range(i+1) if causal else range(nk)
        m=None
        for j in tiles:
            s=nt(km[h,j*TILE:(j+1)*TILE],qm[h,qs])
            if causal and j==i: s=s+t_scr[h,:,0:256]
            if causal and j==i-1: s=s+t_scr[h,:,256:512]
            s_scr[b,h,j*TILE:(j+1)*TILE]=s
            mj=jnp.max(s,axis=0,keepdims=True)
            m=mj if m is None else jnp.maximum(m,mj)
        m2=m*LOG2E
        for j in tiles:
            p_scr[b,h,j*TILE:(j+1)*TILE]=jnp.exp2(s_scr[b,h,j*TILE:(j+1)*TILE]*LOG2E-m2).astype(BF)
        return m2
    def mix(i,ms):
        b=i%2
        qs=slice(i*TILE,(i+1)*TILE)
        n=(i+1 if causal else nk)*TILE
        accs=[]
        for h in range(2):
            acc=nn(vt[h,:,0:n],p_scr[b,h,0:n])
            l=acc[64:65]
            lse_ref[0,h:h+1,qs]=ms[h]+jnp.log2(l)
            accs.append(acc[0:64]*((hs_ref[2*pl.program_id(0)+h] if causal else 1.0)/l))
        o_ref[qs]=jnp.concatenate(accs,axis=0).T.astype(BF)
    ms=None
    for i in range(nq+1):
        new=[soft(i,h) for h in range(2)] if i<nq else None
        if i>0: mix(i-1,ms)
        ms=new

def attn_fwd(causal, limit, hs, bias, q, k, v):
    S,D=q.shape; M=k.shape[0]
    pairs=D//128
    grid_spec=pltpu.PrefetchScalarGridSpec(
        num_scalar_prefetch=1, grid=(pairs,),
        in_specs=[SMEM,
                  pl.BlockSpec(bias.shape,lambda p,*_:(0,0)),
                  pl.BlockSpec((S,128),lambda p,*_:(0,p)),
                  pl.BlockSpec((M,128),lambda p,*_:(0,p)),
                  pl.BlockSpec((M,128),lambda p,*_:(0,p))],
        out_specs=[pl.BlockSpec((S,128),lambda p,*_:(0,p)),
                   pl.BlockSpec((1,2,S),lambda p,*_:(p,0,0))],
        scratch_shapes=[pltpu.VMEM((2,M,128),BF),pltpu.VMEM((2,S,128),BF),pltpu.VMEM((2,80,M),BF),
                        pltpu.VMEM((2,2,M,TILE),F32),pltpu.VMEM((2,2,M,TILE),BF),pltpu.VMEM((2,TILE,512),F32)])
    return pl.pallas_call(functools.partial(fwd_kernel,causal),grid_spec=grid_spec,
        out_shape=(jax.ShapeDtypeStruct((S,D),BF),jax.ShapeDtypeStruct((pairs,2,S),F32)),
        compiler_params=params(1),name="attn_fwd",
        cost_estimate=cost(4*S*M*D*(1 if causal else 2),8*S*D,S*M*D//128))(limit,hs,bias,q,k,v)

def bwd_kernel(causal, p0, chained, limit_ref, hs_ref, bias_ref, q_ref, k_ref, v_ref, go_ref, a_ref, lse_ref, *rest):
    if chained: rest=rest[5 if causal else 4:]
    pair=pl.program_id(0)+p0
    if causal:
        gq_ref, gk_ref, gv_ref, ds_ref, gb_ref, km, qm, q0, vm, gom, kt, p_scr, gs_scr, gqt, dl, t_scr, d_scr, far = rest
    else:
        gq_ref, gk_ref, gv_ref, ds_ref, km, qm, q0, vm, gom, kt, p_scr, gs_scr, gqt, dl = rest
    S=q_ref.shape[0]; M=k_ref.shape[0]
    nq=S//TILE; nk=M//TILE
    limit=limit_ref[0]
    kt[...]=k_ref[...].astype(F32).T.astype(BF)
    sel=jnp.concatenate([jnp.where(head_lanes(1,h),1.0,0.0) for h in range(2)]+[jnp.zeros((14,128),F32)],axis=0).astype(BF)
    x=go_ref[...].astype(F32)*a_ref[...].astype(F32)
    if causal:
        lane=lax.broadcasted_iota(jnp.int32,(1,128),1)
        x=x*(1.0/jnp.where(lane<64,jnp.full((1,128),hs_ref[2*pair],F32),jnp.full((1,128),hs_ref[2*pair+1],F32)))
    hi=x.astype(BF); lo=(x-hi.astype(F32)).astype(BF)
    dd=nt(sel,hi)+nt(sel,lo)
    dl[...]=dd[0:8]
    ds_ref[0]=jnp.broadcast_to(jnp.sum(dd[0:2],axis=1,keepdims=True),(2,128))
    zero=jnp.zeros((),F32)
    for h in range(2):
        km[h]=mask_keys(k_ref[...],limit,h)
        qm[h]=mask_queries(q_ref[...],h)
        own=head_lanes(S,h)
        q0[h]=jnp.where(own,q_ref[...].astype(F32),zero).astype(BF)
        gom[h]=jnp.where(own,go_ref[...].astype(F32),zero).astype(BF)
        vm[h]=jnp.where(head_lanes(M,h),v_ref[...].astype(F32),zero).astype(BF)
        if causal:
            t=toeplitz(bias_ref[pl.ds(2*pair+h,1),:])*LOG2E
            kk=lax.broadcasted_iota(jnp.int32,(TILE,512),0)
            qq=lax.broadcasted_iota(jnp.int32,(TILE,512),1)
            t_scr[h]=jnp.where(qq>=kk,t,NEG)
    if causal:
        d_scr[...]=jnp.zeros_like(d_scr); far[...]=jnp.zeros_like(far)
    gqt[...]=jnp.zeros_like(gqt)
    def scores(j,h):
        b=j%2
        js=slice(j*TILE,(j+1)*TILE)
        for i in range(j if causal else 0,nq):
            qs=slice(i*TILE,(i+1)*TILE)
            s=nt(km[h,js],qm[h,qs])*LOG2E
            if causal and i-j<2:
                s=s+t_scr[h,:,(i-j)*TILE:(i-j+1)*TILE]
            p=jnp.exp2(s-lse_ref[0,h:h+1,qs])
            gs=p*(nt(vm[h,js],go_ref[qs])-dl[h:h+1,qs])
            p_scr[b,h,:,qs]=p.astype(BF)
            gs_scr[b,h,:,qs]=gs.astype(BF)
            if causal:
                if i-j<2:
                    d_scr[h,:,(i-j)*TILE:(i-j+1)*TILE]+=gs
                else:
                    far[h]+=jnp.sum(gs.reshape(TILE//8,8,TILE),axis=0)
    def products(j,h):
        b=j%2
        js=slice(j*TILE,(j+1)*TILE)
        a=j*TILE if causal else 0
        if h==0:
            gv_ref[js]=(nn(p_scr[b,0,:,a:],gom[0,a:])+nn(p_scr[b,1,:,a:],gom[1,a:])).astype(BF)
            gqt[0:64,a:]+=nn(kt[0:64,js],gs_scr[b,0,:,a:])
        else:
            gk_ref[js]=(nn(gs_scr[b,0,:,a:],q0[0,a:])+nn(gs_scr[b,1,:,a:],q0[1,a:])).astype(BF)
            gqt[64:128,a:]+=nn(kt[64:128,js],gs_scr[b,1,:,a:])
    for j in range(nk+1):
        for h in range(2):
            if j<nk: scores(j,h)
            if j>0: products(j-1,h)
    gq_ref[...]=gqt[...].T.astype(BF)
    if causal:
        for h in range(2):
            acc=jnp.zeros((8,512),F32)
            for g in range(TILE//8):
                acc=acc+pltpu.roll(d_scr[h,8*g:8*g+8],(512-8*g)%512,1)
            near=jnp.zeros((1,512),F32)
            for r in range(8):
                near=near+pltpu.roll(acc[r:r+1],(512-r)%512,1)
            lane=lax.broadcasted_iota(jnp.int32,(1,512),1)
            tail=jnp.sum(jnp.where(lane>=255,near,0.0),axis=1,keepdims=True)+jnp.sum(jnp.sum(far[h],axis=0,keepdims=True),axis=1,keepdims=True)
            gb_ref[0,h:h+1,:]=jnp.where(lane[:,:256]==255,tail,near[:,:256])

def attn_bwd(causal, limit, hs, bias, q, k, v, go, a, lse, p0, count, before=None):
    S,D=q.shape; M=k.shape[0]
    pairs=D//128
    col=pl.BlockSpec((S,128),lambda p,*_:(0,p+p0))
    colm=pl.BlockSpec((M,128),lambda p,*_:(0,p+p0))
    outs=[col,colm,colm,pl.BlockSpec((1,2,128),lambda p,*_:(p+p0,0,0))]
    shapes=[jax.ShapeDtypeStruct((S,D),BF),jax.ShapeDtypeStruct((M,D),BF),jax.ShapeDtypeStruct((M,D),BF),jax.ShapeDtypeStruct((pairs,2,128),F32)]
    scr=[pltpu.VMEM((2,M,128),BF),pltpu.VMEM((2,S,128),BF),pltpu.VMEM((2,S,128),BF),pltpu.VMEM((2,M,128),BF),pltpu.VMEM((2,S,128),BF),
         pltpu.VMEM((128,M),BF),pltpu.VMEM((2,2,TILE,S),BF),pltpu.VMEM((2,2,TILE,S),BF),pltpu.VMEM((128,S),F32),pltpu.VMEM((8,S),F32)]
    if causal:
        outs.append(pl.BlockSpec((1,2,256),lambda p,*_:(p+p0,0,0))); shapes.append(jax.ShapeDtypeStruct((pairs,2,256),F32))
        scr+=[pltpu.VMEM((2,TILE,512),F32),pltpu.VMEM((2,TILE,512),F32),pltpu.VMEM((2,8,TILE),F32)]
    extra=() if before is None else tuple(before)
    grid_spec=pltpu.PrefetchScalarGridSpec(
        num_scalar_prefetch=1, grid=(count,),
        in_specs=[SMEM,pl.BlockSpec(bias.shape,lambda p,*_:(0,0)),
                  col,colm,colm,col,col,pl.BlockSpec((1,2,S),lambda p,*_:(p+p0,0,0))]+[pl.BlockSpec(memory_space=pl.ANY)]*len(extra),
        out_specs=outs, scratch_shapes=scr)
    return pl.pallas_call(functools.partial(bwd_kernel,causal,p0,before is not None),grid_spec=grid_spec,out_shape=tuple(shapes),
        input_output_aliases={9+i:i for i in range(len(extra))},
        cost_estimate=cost(10*S*M*D*(1 if causal else 2)*count//pairs,16*S*D*count//pairs,S*M*D//128),
        compiler_params=params(1),name="attn_bwd")(limit,hs,bias,q,k,v,go,a,lse,*extra)
EPS=1e-5
TASKS=4
def norm_rows(v):
    c=v-jnp.mean(v,axis=-1,keepdims=True)
    inv=lax.rsqrt(jnp.mean(c*c,axis=-1,keepdims=True)+EPS)
    return c*inv,inv
def norm_back(e,n,inv,g):
    s=e*g
    return (s-jnp.mean(s,axis=-1,keepdims=True)-n*jnp.mean(s*n,axis=-1,keepdims=True))*inv
def col_sum(v): return jnp.sum(v,axis=0,keepdims=True)

def vec(ref):
    return ref[...].reshape(1,-1)
def whole(shape):
    return pl.BlockSpec(shape,lambda *_:(0,)*len(shape),pipeline_mode=pl.Buffered(1))
def rows_of(rows,cols):
    return pl.BlockSpec((rows,cols),lambda i,*_:(i,0))

def pre_kernel(x_ref,m_ref,g_ref,b_ref,wq,qb,wk,wv,vb,ck,cv,cvb,q_o,k_o,v_o,k2_o,v2_o):
    n,_=norm_rows(x_ref[...].astype(F32))
    h=(n*vec(g_ref)+vec(b_ref)).astype(BF)
    q_o[...]=((nn(h,wq[...])+vec(qb))*0.125).astype(BF)
    k_o[...]=nn(h,wk[...]).astype(BF)
    v_o[...]=(nn(h,wv[...])+vec(vb)).astype(BF)
    m=m_ref[...]
    k2_o[...]=nn(m,ck[...]).astype(BF)
    v2_o[...]=(nn(m,cv[...])+vec(cvb)).astype(BF)

def pre(x,m,g,b,wq,qb,wk,wv,vb,ck,cv,cvb,T=256):
    S,D=x.shape
    r=rows_of(T,D); w=whole((D,D)); u=whole((D,))
    o=jax.ShapeDtypeStruct((S,D),BF)
    return pl.pallas_call(pre_kernel,grid=(S//T,),in_specs=[r,r,u,u,w,u,w,w,u,w,w,u],out_specs=[r]*5,out_shape=[o]*5,
        compiler_params=params(1),name="pre",cost_estimate=cost(10*S*D*D,10*D*D+14*S*D))(x,m,g,b,wq,qb,wk,wv,vb,ck,cv,cvb)

def post_kernel(a_ref,x_ref,wo,bo,pg,pb,ng,nb,wq,qb,x1_o,q2_o,n_o,inv_o):
    n,inv=norm_rows(nn(a_ref[...],wo[...])+vec(bo))
    n_o[...]=n.astype(BF); inv_o[...]=inv
    x1=x_ref[...].astype(F32)+(n*vec(pg)+vec(pb))
    x1_o[...]=x1
    n2,_=norm_rows(x1)
    h=(n2*vec(ng)+vec(nb)).astype(BF)
    q2_o[...]=((nn(h,wq[...])+vec(qb))*0.125).astype(BF)

def post(a,x,wo,bo,pg,pb,ng,nb,wq,qb,T=256):
    S,D=x.shape
    r=rows_of(T,D); w=whole((D,D)); u=whole((D,))
    o=jax.ShapeDtypeStruct((S,D),BF)
    return pl.pallas_call(post_kernel,grid=(S//T,),in_specs=[r,r,w,u,u,u,u,u,w,u],
        out_specs=[r,r,r,rows_of(T,1)],out_shape=[jax.ShapeDtypeStruct((S,D),F32),o,o,jax.ShapeDtypeStruct((S,1),F32)],
        compiler_params=params(1),name="post",cost_estimate=cost(4*S*D*D,4*D*D+12*S*D))(a,x,wo,bo,pg,pb,ng,nb,wq,qb)

SQH=0.7071067811865476
ERFC=(-1.26551223,1.00002368,0.37409196,0.09678418,-0.18628806,0.27886807,-1.13520398,1.48851587,-0.82215223,0.17087277)
def gelu_parts(f):
    z=jnp.abs(f)*SQH
    t=1.0/(1.0+0.5*z)
    poly=jnp.full_like(t,ERFC[9]*LOG2E)
    for c in ERFC[8::-1]:
        poly=poly*t+c*LOG2E
    zz=z*z*LOG2E
    half=0.5*t*jnp.exp2(poly-zz)
    phi=jnp.where(f<0.0,half,1.0-half)
    dens=jnp.exp2(-zz)*0.3989422804014327
    return f*phi, phi+f*dens

CH=256
def mid_kernel(n,dec_ref,gb_ref,idx_ref,all_ref,a2_ref,x1_ref,og_ref,cwo,wi,wout,cbo,cpg,cpb,fng,fnb,bi,mg,mb,bo,
               lo_o,gx2_o,go2_o,u_o,gf_o,h3_o,g3_o,gb2_o,v1_o,v3_o,fac_o,ge,dg,gus):
    T,D=a2_ref.shape; FF=wi.shape[1]
    bi_v=vec(bi); mg_v=vec(mg); mb_v=vec(mb)
    step=pl.program_id(0)
    row=step*T+lax.broadcasted_iota(jnp.int32,(T,1),0)
    valid=row<dec_ref[0]
    n_b,inv_b=norm_rows(nn(a2_ref[...],cwo[...])+vec(cbo))
    x2=x1_ref[...]+(n_b*vec(cpg)+vec(cpb))
    n_x,inv_x=norm_rows(x2)
    h3=(n_x*vec(fng)+vec(fnb)).astype(BF)
    h3_o[...]=h3
    part=jnp.zeros((T,128),F32)
    for c in range(0,FF,CH):
        f=nn(h3,wi[:,c:c+CH])+bi_v[:,c:c+CH]
        a,d=gelu_parts(f)
        ge[:,c:c+CH]=a
        dg[:,c:c+CH]=d
        for l in range(0,CH,128): part=part+a[:,l:l+128]
    mean=jnp.sum(part,axis=1,keepdims=True)*(1.0/FF)
    part=jnp.zeros((T,128),F32)
    for c in range(0,FF,CH):
        e=ge[:,c:c+CH]-mean
        e=e*e
        for l in range(0,CH,128): part=part+e[:,l:l+128]
    inv=lax.rsqrt(jnp.sum(part,axis=1,keepdims=True)*(1.0/FF)+EPS)
    g3=jnp.where(valid,og_ref[...].astype(F32),0.0)
    g3b=g3.astype(BF)
    g3_o[...]=g3b
    s1=jnp.zeros((T,128),F32); s2=jnp.zeros((T,128),F32)
    @pl.when(step==0)
    def _():
        v1_o[...]=jnp.zeros_like(v1_o); v3_o[...]=jnp.zeros_like(v3_o)
        owner=lax.broadcasted_iota(jnp.int32,(n,8,128),0)
        task=sum((owner>=gb_ref[k]).astype(jnp.int32) for k in range(1,TASKS))
        mine=sum((idx_ref[0]>=gb_ref[k]).astype(jnp.int32) for k in range(1,TASKS))
        fac_o[...]=n/jnp.sum(jnp.where(task==mine,all_ref[...],0.0),axis=0)
    for c in range(0,FF,CH):
        cs=slice(c,c+CH)
        n=(ge[:,cs]-mean)*inv
        u_o[:,cs]=(n*mg_v[:,cs]+mb_v[:,cs]).astype(BF)
        gu=nt(g3b,wout[cs,:])
        en=gu*n
        v3_o[0:1,cs]+=col_sum(en)
        v3_o[1:2,cs]+=col_sum(gu)
        eg=gu*mg_v[:,cs]
        gus[:,cs]=eg
        egn=eg*n
        for l in range(0,CH,128):
            s1=s1+eg[:,l:l+128]; s2=s2+egn[:,l:l+128]
    m1=jnp.sum(s1,axis=1,keepdims=True)*(1.0/FF); m2=jnp.sum(s2,axis=1,keepdims=True)*(1.0/FF)
    out=x2+(nn(u_o[...],wout[...])+vec(bo))
    lo_o[...]=jnp.where(valid,out,0.0).astype(BF)
    slope=inv*m2; level=m1-mean*slope
    for c in range(0,FF,CH):
        cs=slice(c,c+CH)
        gf=((gus[:,cs]-level-ge[:,cs]*slope)*inv*dg[:,cs]).astype(BF)
        gf_o[:,cs]=gf
        v3_o[2:3,cs]+=col_sum(gf.astype(F32))
    gh=nt(gf_o[...],wi[...])
    v1_o[0:1]+=col_sum(gh*n_x); v1_o[1:2]+=col_sum(gh)
    gx2=g3+norm_back(gh,n_x,inv_x,vec(fng))
    gx2_o[...]=gx2
    v1_o[2:3]+=col_sum(g3)
    v1_o[3:4]+=col_sum(gx2*n_b); v1_o[4:5]+=col_sum(gx2)
    gb2=norm_back(gx2,n_b,inv_b,vec(cpg)).astype(BF)
    gb2_o[...]=gb2
    v1_o[5:6]+=col_sum(gb2.astype(F32))
    go2_o[...]=nt(gb2,cwo[...]).astype(BF)

def mid(n,dec,gb,idx,all_dec,a2,x1,og,cwo,wi,wout,cbo,cpg,cpb,fng,fnb,bi,mg,mb,bo,T=256):
    S,D=x1.shape; FF=wi.shape[1]
    r=rows_of(T,D); rf=rows_of(T,FF); u=whole((D,)); uf=whole((FF,))
    sd=jax.ShapeDtypeStruct
    acc=lambda s: pl.BlockSpec(s,lambda *_:(0,0))
    return pl.pallas_call(functools.partial(mid_kernel,n),grid=(S//T,),
        in_specs=[SMEM,SMEM,SMEM,whole((n,8,128)),r,r,r,whole((D,D)),whole((D,FF)),whole((FF,D)),u,u,u,u,u,uf,uf,uf,u],
        out_specs=[r,r,r,rf,rf,r,r,r,acc((8,D)),acc((8,FF)),acc((8,128))],
        out_shape=[sd((S,D),BF),sd((S,D),F32),sd((S,D),BF),sd((S,FF),BF),sd((S,FF),BF),sd((S,D),BF),sd((S,D),BF),sd((S,D),BF),sd((8,D),F32),sd((8,FF),F32),sd((8,128),F32)],
        scratch_shapes=[pltpu.VMEM((T,FF),F32)]*3,
        compiler_params=params(1,58),name="mid",
        cost_estimate=cost(8*S*D*FF+4*S*D*D,4*D*FF+2*D*D+S*D*20+4*S*FF,S*FF*3))(dec,gb,idx,all_dec,a2,x1,og,cwo,wi,wout,cbo,cpg,cpb,fng,fnb,bi,mg,mb,bo)

def head_row(hs_ref,D,H):
    lane=lax.broadcasted_iota(jnp.int32,(1,D),1)//(D//H)
    v=jnp.zeros((1,D),F32)
    for h in range(H): v=jnp.where(lane==h,hs_ref[h],v)
    return v
def cross_back_kernel(hs_ref,gq_ref,x1_ref,gx2_ref,n_ref,inv_ref,gv_ref,cwq,wo,cng,cnb,spg,
                      gx1_o,go1_o,h2_o,gqs_o,gb1_o,v_o):
    @pl.when(pl.program_id(0)==0)
    def _(): v_o[...]=jnp.zeros_like(v_o)
    gq=gq_ref[...]*jnp.asarray(0.125,BF)
    gqs_o[...]=gq
    n,inv=norm_rows(x1_ref[...])
    h2_o[...]=(n*vec(cng)+vec(cnb)).astype(BF)
    gh=nt(gq,cwq[...])
    v_o[0:1]+=col_sum(gh*n); v_o[1:2]+=col_sum(gh)
    v_o[2:3]+=col_sum(gq.astype(F32)); v_o[3:4]+=col_sum(gv_ref[...].astype(F32))
    gx1=gx2_ref[...]+norm_back(gh,n,inv,vec(cng))
    gx1_o[...]=gx1
    nb=n_ref[...].astype(F32)
    v_o[4:5]+=col_sum(gx1*nb); v_o[5:6]+=col_sum(gx1)
    gb1=norm_back(gx1,nb,inv_ref[...],vec(spg)).astype(BF)
    gb1_o[...]=gb1
    v_o[6:7]+=col_sum(gb1.astype(F32))
    go1_o[...]=(nt(gb1,wo[...])*head_row(hs_ref,gb1.shape[1],hs_ref.shape[0])).astype(BF)

def cross_back(hs,gq,x1,gx2,n,inv,gv,cwq,wo,cng,cnb,spg,T=256):
    S,D=x1.shape
    r=rows_of(T,D); w=whole((D,D)); u=whole((D,))
    sd=jax.ShapeDtypeStruct
    return pl.pallas_call(cross_back_kernel,grid=(S//T,),in_specs=[SMEM,r,r,r,r,rows_of(T,1),r,w,w,u,u,u],
        out_specs=[r,r,r,r,r,pl.BlockSpec((8,D),lambda *_:(0,0))],
        out_shape=[sd((S,D),F32)]+[sd((S,D),BF)]*4+[sd((8,D),F32)],
        compiler_params=params(1),name="cross_back",cost_estimate=cost(4*S*D*D,4*D*D+28*S*D))(hs,gq,x1,gx2,n,inv,gv,cwq,wo,cng,cnb,spg)

PLACE=(15,16,13,14,12,10,11,6,7,8,9,5,3,4,0,1,2)
WIDE_ROW=17; BUCKET_LANE=32; HEAD_LANE=64
def tail_kernel(n,core_ref,fac_ref,hs_ref,x_ref,gx1_ref,gq_ref,gk_ref,gv_ref,wq,wk,wv,g_ref,b_ref,va,vb,vf,gb,ds,
                gt_o,h_o,gqs_o,keep_o,send_o,v_s,f_s,p_s,t_s):
    D=x_ref.shape[1]; H=hs_ref.shape[0]; FF=vf.shape[1]
    step=pl.program_id(0)
    @pl.when(step==0)
    def _():
        v_s[...]=jnp.zeros_like(v_s); f_s[...]=jnp.zeros_like(f_s); p_s[...]=jnp.zeros_like(p_s)
        v_s[0:6,0:D]=va[0:6]
        v_s[6:13,0:D]=vb[0:7]
        f_s[1:4,0:FF]=vf[0:3]
        for h in range(H): p_s[h:h+1]=gb[h//2,h%2:h%2+1,:]
    n_x,inv=norm_rows(x_ref[...].astype(F32))
    h_o[...]=(n_x*vec(g_ref)+vec(b_ref)).astype(BF)
    gq=gq_ref[...]*jnp.asarray(0.125,BF)
    gqs_o[...]=gq
    gh=nt(gq,wq[...])+nt(gk_ref[...],wk[...])+nt(gv_ref[...],wv[...])
    v_s[13:14,0:D]+=col_sum(gq.astype(F32)); v_s[14:15,0:D]+=col_sum(gv_ref[...].astype(F32))
    v_s[15:16,0:D]+=col_sum(gh*n_x); v_s[16:17,0:D]+=col_sum(gh)
    gt_o[...]=gx1_ref[...]+norm_back(gh,n_x,inv,vec(g_ref))
    @pl.when(step==pl.num_programs(0)-1)
    def _():
        fac=fac_ref[0:1,0:1]
        w=D//n; f=FF//n; b=256//n
        row=lax.broadcasted_iota(jnp.int32,(24,128),0); lane=lax.broadcasted_iota(jnp.int32,(24,128),1)
        heads=jnp.zeros((24,128),F32)
        for h in range(H):
            heads=jnp.where((row==h)&(lane==HEAD_LANE),ds[h//2,h%2:h%2+1,:]*(1.0/jnp.full((1,1),hs_ref[h],F32)),heads)
        def window(ref,rows,at):
            lo=at//128*128
            v=ref[0:rows,lo:lo+256]
            return v if at==lo else pltpu.roll(v,256-(at-lo),1)
        for dev in range(n):
            t=jnp.where(lane<w,window(v_s,24,w*dev)[:,:128],heads)
            p=pltpu.roll(p_s[...],(256-b*dev+BUCKET_LANE)%256,1)[:,:128]
            p=jnp.where((lane[:16]>=BUCKET_LANE)&(lane[:16]<BUCKET_LANE+b),p,t[0:16])
            u=t[16:24]+jnp.where((lane[:8]<f)&(row[:8]>0)&(row[:8]<4),window(f_s,8,f*dev)[:,:128],0.0)
            t_s[dev,0:16]=p*fac
            t_s[dev,16:24]=u*fac
        core=core_ref[0]
        for k in range(n//2):
            keep_o[k]=t_s[2*k+core]
            send_o[k]=t_s[2*k+1-core]
def tail(n,core,fac,hs,x,gx1,gq,gk,gv,wq,wk,wv,g,b,va,vb,vf,gb,ds,T=256):
    S,D=x.shape; FF=vf.shape[1]
    r=rows_of(T,D); w=whole((D,D)); u=whole((D,)); sd=jax.ShapeDtypeStruct
    tile=pl.BlockSpec((n//2,24,128),lambda *_:(0,0,0))
    return pl.pallas_call(functools.partial(tail_kernel,n),grid=(S//T,),
        in_specs=[SMEM,whole((8,128)),SMEM]+[r]*5+[w]*3+[u]*2+[whole(v.shape) for v in (va,vb,vf,gb,ds)],
        out_specs=[r,r,r,tile,tile],
        out_shape=[sd((S,D),F32),sd((S,D),BF),sd((S,D),BF),sd((n//2,24,128),F32),sd((n//2,24,128),F32)],
        scratch_shapes=[pltpu.VMEM((24,D+128),F32),pltpu.VMEM((8,FF+128),F32),pltpu.VMEM((16,256),F32),pltpu.VMEM((n,24,128),F32)],
        compiler_params=params(1),name="tail",cost_estimate=cost(1000,1000))(core,fac,hs,x,gx1,gq,gk,gv,wq,wk,wv,g,b,va,vb,vf,gb,ds)
def memory_kernel(k_ref,v_ref,ck,cv,o):
    o[...]=nt(k_ref[...],ck[...])+nt(v_ref[...],cv[...])
def memory_grad(gk,gv,ck,cv,T=256):
    S,D=gk.shape
    r=rows_of(T,D); w=whole((D,D))
    return pl.pallas_call(memory_kernel,grid=(S//T,),in_specs=[r,r,w,w],out_specs=r,out_shape=jax.ShapeDtypeStruct((S,D),F32),
        compiler_params=params(1),name="memory",cost_estimate=cost(4*S*D*D,4*D*D+S*D*8))(gk,gv,ck,cv)

def part_rows(scr,core,keep_o,send_o):
    groups,r=keep_o.shape[:2]
    for t in range(groups):
        if r%8==0:
            keep_o[t]=scr[pl.ds((2*t+core)*r,r),:]
            send_o[t]=scr[pl.ds((2*t+1-core)*r,r),:]
        else:
            even=scr[2*t*r:(2*t+1)*r,:]
            odd=scr[(2*t+1)*r:(2*t+2)*r,:]
            keep_o[t]=jnp.where(core==0,even,odd)
            send_o[t]=jnp.where(core==0,odd,even)
def wrow_kernel(core_ref,fac_ref,l_ref,r_ref,keep_o,send_o,scr):
    scr[...]=tn(l_ref[...],r_ref[...])*fac_ref[0:1,0:1]
    part_rows(scr,core_ref[0],keep_o,send_o)
def wgrad_rows(core,fac,lhs,rhs,n,B=768):
    S,M=lhs.shape; N=rhs.shape[1]; r=M//n; steps=M//B; groups=B//r//2
    o=pl.BlockSpec((groups,r,N),lambda i:(i,0,0)); sh=jax.ShapeDtypeStruct((n//2,r,N),F32)
    return pl.pallas_call(wrow_kernel,grid=(steps,),
        in_specs=[SMEM,whole((8,128)),pl.BlockSpec((S,B),lambda i:(0,i)),whole((S,N))],
        out_specs=[o,o],scratch_shapes=[pltpu.VMEM((B,N),F32)],out_shape=[sh,sh],compiler_params=params(1),name="wgrad",
        cost_estimate=cost(4*S*M*N,2*S*(M+N)+4*M*N))(core,fac,lhs,rhs)
def wcol_kernel(plan,core_ref,fac_ref,*refs):
    ins=refs[:-3]; keep_o,send_o,scr=refs[-3:]
    step=pl.program_id(0)
    for l,r,first,last in plan:
        @pl.when((step>=first)&(step<last))
        def _(): scr[...]=tn(ins[l][...],ins[r][...])*fac_ref[0:1,0:1]
    part_rows(scr,core_ref[0],keep_o,send_o)
def wgrad_cols(core,fac,pairs,n,B=768,weight=1.0):
    ins=[]; specs=[]; plan=[]; at=0; seen={}
    S,M=pairs[0][0].shape
    for lhs,rhs in pairs:
        if id(lhs) not in seen:
            seen[id(lhs)]=len(ins); ins.append(lhs); specs.append(whole((S,M)))
        steps=rhs.shape[1]//B
        plan.append((seen[id(lhs)],len(ins),at,at+steps))
        ins.append(rhs)
        specs.append(pl.BlockSpec((S,B),functools.partial(lambda at,steps,i:(0,jnp.clip(i-at,0,steps-1)),at,steps)))
        at+=steps
    N=at*B; r=M//n
    o=pl.BlockSpec((n//2,r,B),lambda i:(0,0,i)); sh=jax.ShapeDtypeStruct((n//2,r,N),F32)
    return pl.pallas_call(functools.partial(wcol_kernel,plan),grid=(at,),in_specs=[SMEM,whole((8,128))]+specs,
        out_specs=[o,o],scratch_shapes=[pltpu.VMEM((M,B),F32)],out_shape=[sh,sh],compiler_params=params(1),name="wgrad",
        cost_estimate=cost(4*S*M*N*weight,(2*S*M*len(ins)+4*M*N)*weight))(core,fac,*ins)

def halve_kernel(count,bit_ref,*refs):
    for c in range(count):
        km,ko,gm,go=refs[4*c:4*c+4]
        keep_o,send_o=refs[4*count+2*c:4*count+2*c+2]
        send_o[...]=ko[:,0]+go[:,0]
        keep_o[...]=km[:,0]+gm[:,0]
def halve(bits,chains):
    specs=[];ins=[];outs=[];shapes=[]
    size=sum(4*keep.size//parts for keep,got,part,parts in chains)
    steps=min([4 if size>8e6 else 2]+[keep.shape[0] for keep,*_ in chains])
    for c,(keep,got,part,parts) in enumerate(chains):
        A,_,B,r,C=keep.shape
        C=C//parts; K=A//steps
        for flip in (False,True,False,True):
            specs.append(pl.BlockSpec((K,1,B,r,C),functools.partial(lambda c,flip,part,i,b:(i,1-b[c] if flip else b[c],0,0,part),c,flip,part)))
        ins+=[keep,keep,got,got]
        outs+=[pl.BlockSpec((K,B,r,C),lambda i,b:(i,0,0,0))]*2
        shapes+=[jax.ShapeDtypeStruct((A,B,r,C),F32)]*2
    gs=pltpu.PrefetchScalarGridSpec(num_scalar_prefetch=1,grid=(steps,),in_specs=specs,out_specs=outs)
    return pl.pallas_call(functools.partial(halve_kernel,len(chains)),grid_spec=gs,out_shape=shapes,compiler_params=params(1),name="halve",
        cost_estimate=cost(1000,1000))(bits,*ins)

def deal_kernel(count,z_ref,*refs):
    outs=refs[8*count:]
    for m,o in enumerate(outs):
        at=0
        for c in range(count):
            k,g=refs[8*c+m],refs[8*c+4+m]
            o[:,at:at+k.shape[-1]]=k[0]+g[0]
            at+=k.shape[-1]
def deal(z,chains):
    r=chains[0][0].shape[1]; C=sum(k.shape[2] for k,_ in chains)
    specs=[];ins=[]
    for k,g in chains:
        specs+=[pl.BlockSpec((1,r,k.shape[2]),lambda i,z,m=m:(z[0]^m,0,0)) for m in range(4)]*2
        ins+=[k]*4+[g]*4
    o=pl.BlockSpec((r,C),lambda i,z:(0,0)); sh=jax.ShapeDtypeStruct((r,C),F32)
    gs=pltpu.PrefetchScalarGridSpec(num_scalar_prefetch=1,grid=(1,),in_specs=specs,out_specs=[o]*4)
    return pl.pallas_call(functools.partial(deal_kernel,len(chains)),grid_spec=gs,out_shape=[sh]*4,compiler_params=params(1),name="deal",
        cost_estimate=cost(1000,1000))(z,*ins)

def finish_kernel(n,plan,tile,*refs):
    count=len(plan)+22
    ins=refs[:-count]; outs=refs[-count:]
    total=lambda c,lo,hi: (ins[4*c][:,lo:hi]+ins[4*c+1][:,lo:hi])+(ins[4*c+2][:,lo:hi]+ins[4*c+3][:,lo:hi])
    for o,(c,lo,hi) in zip(outs,plan):
        o[...]=total(c,lo,hi)
    t=total(*tile)
    outs=outs[len(plan):]
    for r,o in zip(PLACE,outs): o[...]=t[r:r+1,:o.shape[0]].reshape(o.shape[0])
    for k in range(3):
        o=outs[17+k]
        o[...]=t[WIDE_ROW+k:WIDE_ROW+k+1,:o.shape[0]].reshape(o.shape[0])
    H,b=outs[20].shape
    outs[20][...]=pltpu.roll(t,128-BUCKET_LANE,1)[:H,:b]
    x=pltpu.roll(t,128-HEAD_LANE,1)[0:16,0:1]
    eye=lax.broadcasted_iota(jnp.int32,(16,128),0)==lax.broadcasted_iota(jnp.int32,(16,128),1)
    outs[21][...]=col_sum(jnp.where(eye,x,0.0))[:,:H].reshape(H)
def finish(n,groups,plan,tile,D,FF,H):
    ins=[v for g in groups for v in g]
    sd=jax.ShapeDtypeStruct
    shapes=[sd((ins[4*c].shape[0],hi-lo),F32) for c,lo,hi in plan]+[sd((D//n,),F32)]*17+[sd((FF//n,),F32)]*3+[sd((H,256//n),F32),sd((H,),F32)]
    return pl.pallas_call(functools.partial(finish_kernel,n,plan,tile),in_specs=[pl.BlockSpec(v.shape) for v in ins],out_shape=shapes,
        compiler_params=params(0),name="finish",cost_estimate=cost(1000,1000))(*ins)

def swap(x,n,bit):
    return lax.ppermute(x,"dp",[(j,j^(1<<bit)) for j in range(n)])
def after(token,*vals):
    return lax.optimization_barrier(tuple(vals)+tuple(token))[:len(vals)]
class Halving:
    def __init__(self,n,keep,send,order):
        self.n,self.order=n,list(order)
        self.live=list(range(n.bit_length()-2,0,-1))
        self.keep=keep; self.got=swap(send,n,0); self.part=(0,1)
    def split(self,orders):
        chains=[]
        for k,order in enumerate(orders):
            h=object.__new__(Halving)
            h.n,h.order,h.live=self.n,list(order),list(self.live)
            h.keep,h.got,h.part=self.keep,self.got,(k,len(orders))
            chains.append(h)
        return chains
def step(token,index,*chains):
    bits=[];work=[]
    flat=after(token,*[v for c in chains for v in (c.keep,c.got)])
    for k,c in enumerate(chains):
        b=c.order.pop(0)
        axis=c.live.index(b)
        c.live.remove(b)
        keep,got=flat[2*k:2*k+2]
        shape=(2**axis,2,2**(len(c.live)-axis))+keep.shape[-2:]
        bits.append((b,(index>>b)&1))
        work.append((keep.reshape(shape),got.reshape(shape))+c.part)
    outs=halve(jnp.stack([v for _,v in bits]).astype(jnp.int32),work)
    for k,c in enumerate(chains):
        c.keep,c.part=outs[2*k],(0,1)
        c.got=swap(outs[2*k+1],c.n,bits[k][0])
    return [outs[2*k+1] for k in range(len(chains))]
def last_step(token,index,zs,*chains):
    flat=after(token,*[v for c in chains for v in (c.keep,c.got)])
    z=((index>>zs[0])&3).reshape(1).astype(jnp.int32)
    cut=lambda v: v.reshape((4,)+v.shape[-2:])
    own,*sends=deal(z,[(cut(flat[2*k]),cut(flat[2*k+1])) for k in range(len(chains))])
    n=chains[0].n
    return [own]+[lax.ppermute(s,"dp",[(j,j^((m+1)<<zs[0])) for j in range(n)]) for m,s in enumerate(sends)]

def shards(n,tokens,memory,out_grad,dec_len,mem_len,group_bounds,
           self_norm_gain,self_norm_bias,self_query,self_query_bias,self_key,self_value,self_value_bias,self_output,self_output_bias,
           position_bias,head_scale,self_post_gain,self_post_bias,cross_norm_gain,cross_norm_bias,cross_query,cross_query_bias,
           cross_key,cross_value,cross_value_bias,cross_output,cross_output_bias,cross_post_gain,cross_post_bias,
           feed_norm_gain,feed_norm_bias,feed_inner,feed_inner_bias,feed_mid_gain,feed_mid_bias,feed_outer,feed_outer_bias):
    bits=n.bit_length()-1
    xs,ys,zs=([1],[2],[3,4]) if bits==5 else ([1,2],[3,4],list(range(5,bits)))
    order_a=xs+ys; order_b=ys+xs
    index=lax.axis_index("dp")
    idx=index.reshape(1).astype(jnp.int32)
    core=idx&1
    x=tokens[0]; m=memory[0]; og=out_grad[0]
    S,D=x.shape
    H=head_scale.shape[0]; pairs=H//2
    all_dec=lax.all_to_all(jnp.broadcast_to(dec_len.astype(F32).reshape(1,1,1),(n,8,128)),"dp",0,0,tiled=True)
    q1,k1,v1,k2,v2=pre(x,m,self_norm_gain,self_norm_bias,self_query,self_query_bias,self_key,self_value,self_value_bias,cross_key,cross_value,cross_value_bias)
    a1,lse1=attn_fwd(True,dec_len,head_scale,position_bias,q1,k1,v1)
    x1,q2,nb1,ib1=post(a1,x,self_output,self_output_bias,self_post_gain,self_post_bias,cross_norm_gain,cross_norm_bias,cross_query,cross_query_bias)
    a2,lse2=attn_fwd(False,mem_len,head_scale,position_bias,q2,k2,v2)
    lo,gx2,go2,u,gf,h3,g3,gb2,va,vf,fac=mid(n,dec_len,group_bounds,idx,all_dec,a2,x1,og,cross_output,feed_inner,feed_outer,cross_output_bias,cross_post_gain,cross_post_bias,feed_norm_gain,feed_norm_bias,feed_inner_bias,feed_mid_gain,feed_mid_bias,feed_outer_bias)
    keep,send=wgrad_cols(core,fac,[(h3,gf),(a2,gb2)],n)
    fi=Halving(n,keep,send,order_b)
    u,=after([send],u)
    keep,send=wgrad_rows(core,fac,u,g3,n)
    fo=Halving(n,keep,send,order_a)
    t=step([send],index,fi)
    t=step(t,index,fo)
    go2,=after(t,go2)
    gq2,gk2,gv2,_=attn_bwd(False,mem_len,head_scale,position_bias,q2,k2,v2,go2,a2,lse2,0,pairs)
    gx1,go1,h2,gqs2,gb1,vb=cross_back(head_scale,gq2,x1,gx2,nb1,ib1,gv2,cross_query,self_output,cross_norm_gain,cross_norm_bias,self_post_gain)
    t=step([vb],index,fo)
    h2,=after(t,h2)
    keep,send=wgrad_cols(core,fac,[(h2,gqs2),(m,gv2),(m,gk2),(a1,gb1)],n)
    g2=Halving(n,keep,send,[])
    t=step([send],index,fi)
    go1,=after(t,go1)
    half=pairs//2
    back=attn_bwd(True,dec_len,head_scale,position_bias,q1,k1,v1,go1,a1,lse1,0,half)
    t=[back[3]]
    while fo.order: t=step(t,index,fo)
    r_fo=last_step(t,index,zs,fo)
    ga,gb_=g2.split([order_a,order_b])
    t=step([r_fo[0]],index,ga,gb_)
    go1,=after(t,go1)
    gq1,gk1,gv1,ds,gb=attn_bwd(True,dec_len,head_scale,position_bias,q1,k1,v1,go1,a1,lse1,half,pairs-half,back)
    t=[ds]
    while fi.order: t=step(t,index,fi)
    r_fi=last_step(t,index,zs,fi)
    gx1,=after([r_fi[0]],gx1)
    gt,h1,gqs1,keep,send=tail(n,core,fac,head_scale,x,gx1,gq1,gk1,gv1,self_query,self_key,self_value,self_norm_gain,self_norm_bias,va,vb,vf,gb,ds)
    sv=Halving(n,keep,send,order_a)
    h1,=after([send,ga.got,gb_.got]+r_fo[1:],h1)
    keep,send=wgrad_cols(core,fac,[(h1,gqs1),(h1,gv1),(h1,gk1)],n)
    g3_=Halving(n,keep,send,[])
    t=[send]
    while ga.order: t=step(t,index,ga,gb_)
    sa,sb=g3_.split([order_a,order_b])
    t=step(t,index,sa,sb,sv)
    gk2,=after(t+r_fi[1:],gk2)
    gm=memory_grad(gk2,gv2,cross_key,cross_value)
    r_g2=last_step([gm],index,zs,ga,gb_)
    t=r_g2[:1]
    while sa.order: t=step(t,index,sa,sb,sv)
    t=t+r_g2[1:]
    FF=feed_inner.shape[1]
    if sv.keep.shape[-2]==sa.keep.shape[-2]:
        groups=[last_step(t,index,zs,sa,sb,sv)]
        tile=(3,3*D,3*D+128)
    else:
        groups=[last_step(t,index,zs,sa,sb),last_step(t,index,zs,sv)]
        tile=(4,0,128)
    g_fo,g_fi,g_co,g_cq,g_cv,g_ck,g_so,g_sq,g_sv,g_sk,*small=finish(n,[r_fo,r_fi,r_g2]+groups,[
        (0,0,D),(1,0,FF),(1,FF,FF+D),(2,0,D),(2,D,2*D),(2,2*D,3*D),(2,3*D,4*D),(3,0,D),(3,D,2*D),(3,2*D,3*D)],tile,D,FF,H)
    (sng,snb,sqb,svb,sob,spg,spb,cng,cnb,cqb,cvb,cob,cpg,cpb,fng,fnb,fob,fmg,fmb,fib,gpos,ghs)=small
    fo_b=fob
    return (lo[None],gt[None],gm[None],
        sng,snb,g_sq,sqb,g_sk,g_sv,svb,g_so,sob,gpos,ghs,spg,spb,cng,cnb,g_cq,cqb,g_ck,g_cv,cvb,g_co,cob,cpg,cpb,
        fng,fnb,g_fi,fib,fmg,fmb,g_fo,fo_b)

def solution(mesh):
    n=mesh.shape["dp"]
    vec=P("dp"); mat=P("dp",None); cube=P("dp",None,None)
    return jax.shard_map(functools.partial(shards,n),mesh=mesh,in_specs=(cube,cube,cube,vec,vec)+(P(),)*33,
        out_specs=(cube,cube,cube,vec,vec,mat,vec,mat,mat,vec,mat,vec,P(None,"dp"),P(),vec,vec,vec,vec,mat,vec,
                   mat,mat,vec,mat,vec,vec,vec,vec,vec,mat,vec,vec,vec,mat,vec),check_vma=False)
```

```python
import functools
import jax, jax.numpy as jnp
from jax import lax
from jax.experimental import pallas as pl
from jax.experimental.pallas import tpu as pltpu
from jax.sharding import PartitionSpec as P
F32=jnp.float32; BF=jnp.bfloat16
LOG2E=1.4426950408889634
NEG=-1e30
TILE=256
SMEM=pl.BlockSpec(memory_space=pltpu.SMEM)
def cost(flops,nbytes,trans=0):
    return pl.CostEstimate(flops=int(flops)*200,bytes_accessed=int(nbytes)*200,transcendentals=int(trans))
def nt(a,b): return lax.dot_general(a,b,(((1,),(1,)),((),())),preferred_element_type=F32)
def nn(a,b): return lax.dot_general(a,b,(((1,),(0,)),((),())),preferred_element_type=F32)
def tn(a,b): return lax.dot_general(a,b,(((0,),(0,)),((),())),preferred_element_type=F32)
def params(n, mb=56, sem=None):
    return pltpu.CompilerParams(dimension_semantics=("arbitrary",)*n, vmem_limit_bytes=mb<<20)

def head_lanes(rows, h):
    lane=lax.broadcasted_iota(jnp.int32,(rows,128),1)
    return (lane<64) if h==0 else (lane>=64)

def mask_keys(k, limit, h):
    rows=k.shape[0]
    lane=lax.broadcasted_iota(jnp.int32,(rows,128),1)
    row=lax.broadcasted_iota(jnp.int32,(rows,128),0)
    spare=64 if h==0 else 0
    pen=jnp.where((lane==spare)&(row>=limit), NEG, 0.0)
    own=head_lanes(rows,h)
    return jnp.where(own,k.astype(F32),pen).astype(BF)
def mask_queries(q, h):
    rows=q.shape[0]
    lane=lax.broadcasted_iota(jnp.int32,(rows,128),1)
    spare=64 if h==0 else 0
    one=jnp.where(lane==spare,1.0,0.0)
    return jnp.where(head_lanes(rows,h),q.astype(F32),one).astype(BF)

def toeplitz(bias_row):
    r=jnp.concatenate([bias_row-bias_row[:,255:256], jnp.zeros((1,256),F32)],axis=1)
    x=jnp.broadcast_to(r,(TILE,512))
    return pltpu.roll(x,0,1,stride=1,stride_axis=0)

def fwd_kernel(causal, limit_ref, hs_ref, bias_ref, q_ref, k_ref, v_ref, o_ref, lse_ref, km, qm, vt, s_scr, p_scr, t_scr):
    S=q_ref.shape[0]; M=k_ref.shape[0]
    limit=limit_ref[0]
    vtf=v_ref[...].astype(F32).T
    ones=jnp.ones((16,M),BF)
    for h in range(2):
        km[h]=mask_keys(k_ref[...],limit,h)
        qm[h]=mask_queries(q_ref[...],h)
        vt[h,0:64]=vtf[h*64:(h+1)*64].astype(BF)
        vt[h,64:80]=ones
        if causal:
            t=toeplitz(bias_ref[pl.ds(2*pl.program_id(0)+h,1),:])
            kk=lax.broadcasted_iota(jnp.int32,(TILE,512),0)
            qq=lax.broadcasted_iota(jnp.int32,(TILE,512),1)
            t_scr[h]=jnp.where(qq>=kk,t,NEG)
    nq=S//TILE; nk=M//TILE
    def soft(i,h):
        b=i%2
        qs=slice(i*TILE,(i+1)*TILE)
        tiles=range(i+1) if causal else range(nk)
        m=None
        for j in tiles:
            s=nt(km[h,j*TILE:(j+1)*TILE],qm[h,qs])
            if causal and j==i: s=s+t_scr[h,:,0:256]
            if causal and j==i-1: s=s+t_scr[h,:,256:512]
            s_scr[b,h,j*TILE:(j+1)*TILE]=s
            mj=jnp.max(s,axis=0,keepdims=True)
            m=mj if m is None else jnp.maximum(m,mj)
        m2=m*LOG2E
        for j in tiles:
            p_scr[b,h,j*TILE:(j+1)*TILE]=jnp.exp2(s_scr[b,h,j*TILE:(j+1)*TILE]*LOG2E-m2).astype(BF)
        return m2
    def mix(i,ms):
        b=i%2
        qs=slice(i*TILE,(i+1)*TILE)
        n=(i+1 if causal else nk)*TILE
        accs=[]
        for h in range(2):
            acc=nn(vt[h,:,0:n],p_scr[b,h,0:n])
            l=acc[64:65]
            lse_ref[0,h:h+1,qs]=ms[h]+jnp.log2(l)
            accs.append(acc[0:64]*((hs_ref[2*pl.program_id(0)+h] if causal else 1.0)/l))
        o_ref[qs]=jnp.concatenate(accs,axis=0).T.astype(BF)
    ms=None
    for i in range(nq+1):
        new=[soft(i,h) for h in range(2)] if i<nq else None
        if i>0: mix(i-1,ms)
        ms=new

def attn_fwd(causal, limit, hs, bias, q, k, v):
    S,D=q.shape; M=k.shape[0]
    pairs=D//128
    grid_spec=pltpu.PrefetchScalarGridSpec(
        num_scalar_prefetch=1, grid=(pairs,),
        in_specs=[SMEM,
                  pl.BlockSpec(bias.shape,lambda p,*_:(0,0)),
                  pl.BlockSpec((S,128),lambda p,*_:(0,p)),
                  pl.BlockSpec((M,128),lambda p,*_:(0,p)),
                  pl.BlockSpec((M,128),lambda p,*_:(0,p))],
        out_specs=[pl.BlockSpec((S,128),lambda p,*_:(0,p)),
                   pl.BlockSpec((1,2,S),lambda p,*_:(p,0,0))],
        scratch_shapes=[pltpu.VMEM((2,M,128),BF),pltpu.VMEM((2,S,128),BF),pltpu.VMEM((2,80,M),BF),
                        pltpu.VMEM((2,2,M,TILE),F32),pltpu.VMEM((2,2,M,TILE),BF),pltpu.VMEM((2,TILE,512),F32)])
    return pl.pallas_call(functools.partial(fwd_kernel,causal),grid_spec=grid_spec,
        out_shape=(jax.ShapeDtypeStruct((S,D),BF),jax.ShapeDtypeStruct((pairs,2,S),F32)),
        compiler_params=params(1),name="attn_fwd",
        cost_estimate=cost(4*S*M*D*(1 if causal else 2),8*S*D,S*M*D//128))(limit,hs,bias,q,k,v)

def bwd_kernel(causal, p0, chained, limit_ref, hs_ref, bias_ref, q_ref, k_ref, v_ref, go_ref, a_ref, lse_ref, *rest):
    if chained: rest=rest[5 if causal else 4:]
    pair=pl.program_id(0)+p0
    if causal:
        gq_ref, gk_ref, gv_ref, ds_ref, gb_ref, km, qm, q0, vm, gom, kt, p_scr, gs_scr, gqt, dl, t_scr, d_scr, far = rest
    else:
        gq_ref, gk_ref, gv_ref, ds_ref, km, qm, q0, vm, gom, kt, p_scr, gs_scr, gqt, dl = rest
    S=q_ref.shape[0]; M=k_ref.shape[0]
    nq=S//TILE; nk=M//TILE
    limit=limit_ref[0]
    kt[...]=k_ref[...].astype(F32).T.astype(BF)
    sel=jnp.concatenate([jnp.where(head_lanes(1,h),1.0,0.0) for h in range(2)]+[jnp.zeros((14,128),F32)],axis=0).astype(BF)
    x=go_ref[...].astype(F32)*a_ref[...].astype(F32)
    if causal:
        lane=lax.broadcasted_iota(jnp.int32,(1,128),1)
        x=x*(1.0/jnp.where(lane<64,jnp.full((1,128),hs_ref[2*pair],F32),jnp.full((1,128),hs_ref[2*pair+1],F32)))
    hi=x.astype(BF); lo=(x-hi.astype(F32)).astype(BF)
    dd=nt(sel,hi)+nt(sel,lo)
    dl[...]=dd[0:8]
    ds_ref[0]=jnp.broadcast_to(jnp.sum(dd[0:2],axis=1,keepdims=True),(2,128))
    zero=jnp.zeros((),F32)
    for h in range(2):
        km[h]=mask_keys(k_ref[...],limit,h)
        qm[h]=mask_queries(q_ref[...],h)
        own=head_lanes(S,h)
        q0[h]=jnp.where(own,q_ref[...].astype(F32),zero).astype(BF)
        gom[h]=jnp.where(own,go_ref[...].astype(F32),zero).astype(BF)
        vm[h]=jnp.where(head_lanes(M,h),v_ref[...].astype(F32),zero).astype(BF)
        if causal:
            t=toeplitz(bias_ref[pl.ds(2*pair+h,1),:])*LOG2E
            kk=lax.broadcasted_iota(jnp.int32,(TILE,512),0)
            qq=lax.broadcasted_iota(jnp.int32,(TILE,512),1)
            t_scr[h]=jnp.where(qq>=kk,t,NEG)
    if causal:
        d_scr[...]=jnp.zeros_like(d_scr); far[...]=jnp.zeros_like(far)
    gqt[...]=jnp.zeros_like(gqt)
    def scores(j,h):
        b=j%2
        js=slice(j*TILE,(j+1)*TILE)
        for i in range(j if causal else 0,nq):
            qs=slice(i*TILE,(i+1)*TILE)
            s=nt(km[h,js],qm[h,qs])*LOG2E
            if causal and i-j<2:
                s=s+t_scr[h,:,(i-j)*TILE:(i-j+1)*TILE]
            p=jnp.exp2(s-lse_ref[0,h:h+1,qs])
            gs=p*(nt(vm[h,js],go_ref[qs])-dl[h:h+1,qs])
            p_scr[b,h,:,qs]=p.astype(BF)
            gs_scr[b,h,:,qs]=gs.astype(BF)
            if causal:
                if i-j<2:
                    d_scr[h,:,(i-j)*TILE:(i-j+1)*TILE]+=gs
                else:
                    far[h]+=jnp.sum(gs.reshape(TILE//8,8,TILE),axis=0)
    def products(j,h):
        b=j%2
        js=slice(j*TILE,(j+1)*TILE)
        a=j*TILE if causal else 0
        if h==0:
            gv_ref[js]=(nn(p_scr[b,0,:,a:],gom[0,a:])+nn(p_scr[b,1,:,a:],gom[1,a:])).astype(BF)
            gqt[0:64,a:]+=nn(kt[0:64,js],gs_scr[b,0,:,a:])
        else:
            gk_ref[js]=(nn(gs_scr[b,0,:,a:],q0[0,a:])+nn(gs_scr[b,1,:,a:],q0[1,a:])).astype(BF)
            gqt[64:128,a:]+=nn(kt[64:128,js],gs_scr[b,1,:,a:])
    for j in range(nk+1):
        for h in range(2):
            if j<nk: scores(j,h)
            if j>0: products(j-1,h)
    gq_ref[...]=gqt[...].T.astype(BF)
    if causal:
        for h in range(2):
            acc=jnp.zeros((8,512),F32)
            for g in range(TILE//8):
                acc=acc+pltpu.roll(d_scr[h,8*g:8*g+8],(512-8*g)%512,1)
            near=jnp.zeros((1,512),F32)
            for r in range(8):
                near=near+pltpu.roll(acc[r:r+1],(512-r)%512,1)
            lane=lax.broadcasted_iota(jnp.int32,(1,512),1)
            tail=jnp.sum(jnp.where(lane>=255,near,0.0),axis=1,keepdims=True)+jnp.sum(jnp.sum(far[h],axis=0,keepdims=True),axis=1,keepdims=True)
            gb_ref[0,h:h+1,:]=jnp.where(lane[:,:256]==255,tail,near[:,:256])

def attn_bwd(causal, limit, hs, bias, q, k, v, go, a, lse, p0, count, before=None):
    S,D=q.shape; M=k.shape[0]
    pairs=D//128
    col=pl.BlockSpec((S,128),lambda p,*_:(0,p+p0))
    colm=pl.BlockSpec((M,128),lambda p,*_:(0,p+p0))
    outs=[col,colm,colm,pl.BlockSpec((1,2,128),lambda p,*_:(p+p0,0,0))]
    shapes=[jax.ShapeDtypeStruct((S,D),BF),jax.ShapeDtypeStruct((M,D),BF),jax.ShapeDtypeStruct((M,D),BF),jax.ShapeDtypeStruct((pairs,2,128),F32)]
    scr=[pltpu.VMEM((2,M,128),BF),pltpu.VMEM((2,S,128),BF),pltpu.VMEM((2,S,128),BF),pltpu.VMEM((2,M,128),BF),pltpu.VMEM((2,S,128),BF),
         pltpu.VMEM((128,M),BF),pltpu.VMEM((2,2,TILE,S),BF),pltpu.VMEM((2,2,TILE,S),BF),pltpu.VMEM((128,S),F32),pltpu.VMEM((8,S),F32)]
    if causal:
        outs.append(pl.BlockSpec((1,2,256),lambda p,*_:(p+p0,0,0))); shapes.append(jax.ShapeDtypeStruct((pairs,2,256),F32))
        scr+=[pltpu.VMEM((2,TILE,512),F32),pltpu.VMEM((2,TILE,512),F32),pltpu.VMEM((2,8,TILE),F32)]
    extra=() if before is None else tuple(before)
    grid_spec=pltpu.PrefetchScalarGridSpec(
        num_scalar_prefetch=1, grid=(count,),
        in_specs=[SMEM,pl.BlockSpec(bias.shape,lambda p,*_:(0,0)),
                  col,colm,colm,col,col,pl.BlockSpec((1,2,S),lambda p,*_:(p+p0,0,0))]+[pl.BlockSpec(memory_space=pl.ANY)]*len(extra),
        out_specs=outs, scratch_shapes=scr)
    return pl.pallas_call(functools.partial(bwd_kernel,causal,p0,before is not None),grid_spec=grid_spec,out_shape=tuple(shapes),
        input_output_aliases={9+i:i for i in range(len(extra))},
        cost_estimate=cost(10*S*M*D*(1 if causal else 2)*count//pairs,16*S*D*count//pairs,S*M*D//128),
        compiler_params=params(1),name="attn_bwd")(limit,hs,bias,q,k,v,go,a,lse,*extra)
EPS=1e-5
TASKS=4
def norm_rows(v):
    c=v-jnp.mean(v,axis=-1,keepdims=True)
    inv=lax.rsqrt(jnp.mean(c*c,axis=-1,keepdims=True)+EPS)
    return c*inv,inv
def norm_back(e,n,inv,g):
    s=e*g
    return (s-jnp.mean(s,axis=-1,keepdims=True)-n*jnp.mean(s*n,axis=-1,keepdims=True))*inv
def col_sum(v): return jnp.sum(v,axis=0,keepdims=True)

def vec(ref):
    return ref[...].reshape(1,-1)
def whole(shape):
    return pl.BlockSpec(shape,lambda *_:(0,)*len(shape),pipeline_mode=pl.Buffered(1))
def rows_of(rows,cols):
    return pl.BlockSpec((rows,cols),lambda i,*_:(i,0))

def pre_kernel(x_ref,m_ref,g_ref,b_ref,wq,qb,wk,wv,vb,ck,cv,cvb,q_o,k_o,v_o,k2_o,v2_o):
    n,_=norm_rows(x_ref[...].astype(F32))
    h=(n*vec(g_ref)+vec(b_ref)).astype(BF)
    q_o[...]=((nn(h,wq[...])+vec(qb))*0.125).astype(BF)
    k_o[...]=nn(h,wk[...]).astype(BF)
    v_o[...]=(nn(h,wv[...])+vec(vb)).astype(BF)
    m=m_ref[...]
    k2_o[...]=nn(m,ck[...]).astype(BF)
    v2_o[...]=(nn(m,cv[...])+vec(cvb)).astype(BF)

def pre(x,m,g,b,wq,qb,wk,wv,vb,ck,cv,cvb,T=256):
    S,D=x.shape
    r=rows_of(T,D); w=whole((D,D)); u=whole((D,))
    o=jax.ShapeDtypeStruct((S,D),BF)
    return pl.pallas_call(pre_kernel,grid=(S//T,),in_specs=[r,r,u,u,w,u,w,w,u,w,w,u],out_specs=[r]*5,out_shape=[o]*5,
        compiler_params=params(1),name="pre",cost_estimate=cost(10*S*D*D,10*D*D+14*S*D))(x,m,g,b,wq,qb,wk,wv,vb,ck,cv,cvb)

def post_kernel(a_ref,x_ref,wo,bo,pg,pb,ng,nb,wq,qb,x1_o,q2_o,n_o,inv_o):
    n,inv=norm_rows(nn(a_ref[...],wo[...])+vec(bo))
    n_o[...]=n.astype(BF); inv_o[...]=inv
    x1=x_ref[...].astype(F32)+(n*vec(pg)+vec(pb))
    x1_o[...]=x1
    n2,_=norm_rows(x1)
    h=(n2*vec(ng)+vec(nb)).astype(BF)
    q2_o[...]=((nn(h,wq[...])+vec(qb))*0.125).astype(BF)

def post(a,x,wo,bo,pg,pb,ng,nb,wq,qb,T=256):
    S,D=x.shape
    r=rows_of(T,D); w=whole((D,D)); u=whole((D,))
    o=jax.ShapeDtypeStruct((S,D),BF)
    return pl.pallas_call(post_kernel,grid=(S//T,),in_specs=[r,r,w,u,u,u,u,u,w,u],
        out_specs=[r,r,r,rows_of(T,1)],out_shape=[jax.ShapeDtypeStruct((S,D),F32),o,o,jax.ShapeDtypeStruct((S,1),F32)],
        compiler_params=params(1),name="post",cost_estimate=cost(4*S*D*D,4*D*D+12*S*D))(a,x,wo,bo,pg,pb,ng,nb,wq,qb)

SQH=0.7071067811865476
ERFC=(-1.26551223,1.00002368,0.37409196,0.09678418,-0.18628806,0.27886807,-1.13520398,1.48851587,-0.82215223,0.17087277)
def gelu_parts(f):
    t=1.0/(1.0+jnp.abs(f)*(0.5*SQH))
    poly=jnp.full_like(t,ERFC[9]*LOG2E)
    for c in ERFC[8:0:-1]:
        poly=poly*t+c*LOG2E
    poly=poly*t+(ERFC[0]*LOG2E-1.0)
    zz=f*f*(0.5*LOG2E)
    half=t*jnp.exp2(poly-zz)
    phi=jnp.where(f<0.0,half,1.0-half)
    dens=jnp.exp2(-1.3257480647361595-zz)
    return f*phi, phi+f*dens

CH=256
def mid_kernel(n,dec_ref,gb_ref,idx_ref,all_ref,a2_ref,x1_ref,og_ref,cwo,wi,wout,cbo,cpg,cpb,fng,fnb,bi,mg,mb,bo,
               lo_o,gx2_o,go2_o,u_o,gf_o,h3_o,g3_o,gb2_o,v1_o,v3_o,fac_o,ge,dg,gus):
    T,D=a2_ref.shape; FF=wi.shape[1]
    bi_v=vec(bi); mg_v=vec(mg); mb_v=vec(mb)
    step=pl.program_id(0)
    row=step*T+lax.broadcasted_iota(jnp.int32,(T,1),0)
    valid=row<dec_ref[0]
    n_b,inv_b=norm_rows(nn(a2_ref[...],cwo[...])+vec(cbo))
    x2=x1_ref[...]+(n_b*vec(cpg)+vec(cpb))
    n_x,inv_x=norm_rows(x2)
    h3=(n_x*vec(fng)+vec(fnb)).astype(BF)
    h3_o[...]=h3
    part=jnp.zeros((T,128),F32)
    for c in range(0,FF,CH):
        f=nn(h3,wi[:,c:c+CH])+bi_v[:,c:c+CH]
        a,d=gelu_parts(f)
        ge[:,c:c+CH]=a
        dg[:,c:c+CH]=d
        for l in range(0,CH,128): part=part+a[:,l:l+128]
    mean=jnp.sum(part,axis=1,keepdims=True)*(1.0/FF)
    part=jnp.zeros((T,128),F32)
    for c in range(0,FF,CH):
        e=ge[:,c:c+CH]-mean
        e=e*e
        for l in range(0,CH,128): part=part+e[:,l:l+128]
    inv=lax.rsqrt(jnp.sum(part,axis=1,keepdims=True)*(1.0/FF)+EPS)
    g3=jnp.where(valid,og_ref[...].astype(F32),0.0)
    g3b=g3.astype(BF)
    g3_o[...]=g3b
    s1=jnp.zeros((T,128),F32); s2=jnp.zeros((T,128),F32)
    @pl.when(step==0)
    def _():
        v1_o[...]=jnp.zeros_like(v1_o); v3_o[...]=jnp.zeros_like(v3_o)
        owner=lax.broadcasted_iota(jnp.int32,(n,8,128),0)
        task=sum((owner>=gb_ref[k]).astype(jnp.int32) for k in range(1,TASKS))
        mine=sum((idx_ref[0]>=gb_ref[k]).astype(jnp.int32) for k in range(1,TASKS))
        fac_o[...]=n/jnp.sum(jnp.where(task==mine,all_ref[...],0.0),axis=0)
    for c in range(0,FF,CH):
        cs=slice(c,c+CH)
        n=(ge[:,cs]-mean)*inv
        u_o[:,cs]=(n*mg_v[:,cs]+mb_v[:,cs]).astype(BF)
        gu=nt(g3b,wout[cs,:])
        en=gu*n
        v3_o[0:1,cs]+=col_sum(en)
        v3_o[1:2,cs]+=col_sum(gu)
        eg=gu*mg_v[:,cs]
        gus[:,cs]=eg
        egn=eg*n
        for l in range(0,CH,128):
            s1=s1+eg[:,l:l+128]; s2=s2+egn[:,l:l+128]
    m1=jnp.sum(s1,axis=1,keepdims=True)*(1.0/FF); m2=jnp.sum(s2,axis=1,keepdims=True)*(1.0/FF)
    out=x2+(nn(u_o[...],wout[...])+vec(bo))
    lo_o[...]=jnp.where(valid,out,0.0).astype(BF)
    slope=inv*m2; level=m1-mean*slope
    for c in range(0,FF,CH):
        cs=slice(c,c+CH)
        gf=((gus[:,cs]-level-ge[:,cs]*slope)*inv*dg[:,cs]).astype(BF)
        gf_o[:,cs]=gf
        v3_o[2:3,cs]+=col_sum(gf.astype(F32))
    gh=nt(gf_o[...],wi[...])
    v1_o[0:1]+=col_sum(gh*n_x); v1_o[1:2]+=col_sum(gh)
    gx2=g3+norm_back(gh,n_x,inv_x,vec(fng))
    gx2_o[...]=gx2
    v1_o[2:3]+=col_sum(g3)
    v1_o[3:4]+=col_sum(gx2*n_b); v1_o[4:5]+=col_sum(gx2)
    gb2=norm_back(gx2,n_b,inv_b,vec(cpg)).astype(BF)
    gb2_o[...]=gb2
    v1_o[5:6]+=col_sum(gb2.astype(F32))
    go2_o[...]=nt(gb2,cwo[...]).astype(BF)

def mid(n,dec,gb,idx,all_dec,a2,x1,og,cwo,wi,wout,cbo,cpg,cpb,fng,fnb,bi,mg,mb,bo,T=256):
    S,D=x1.shape; FF=wi.shape[1]
    r=rows_of(T,D); rf=rows_of(T,FF); u=whole((D,)); uf=whole((FF,))
    sd=jax.ShapeDtypeStruct
    acc=lambda s: pl.BlockSpec(s,lambda *_:(0,0))
    return pl.pallas_call(functools.partial(mid_kernel,n),grid=(S//T,),
        in_specs=[SMEM,SMEM,SMEM,whole((n,8,128)),r,r,r,whole((D,D)),whole((D,FF)),whole((FF,D)),u,u,u,u,u,uf,uf,uf,u],
        out_specs=[r,r,r,rf,rf,r,r,r,acc((8,D)),acc((8,FF)),acc((8,128))],
        out_shape=[sd((S,D),BF),sd((S,D),F32),sd((S,D),BF),sd((S,FF),BF),sd((S,FF),BF),sd((S,D),BF),sd((S,D),BF),sd((S,D),BF),sd((8,D),F32),sd((8,FF),F32),sd((8,128),F32)],
        scratch_shapes=[pltpu.VMEM((T,FF),F32)]*3,
        compiler_params=params(1,58),name="mid",
        cost_estimate=cost(8*S*D*FF+4*S*D*D,4*D*FF+2*D*D+S*D*20+4*S*FF,S*FF*3))(dec,gb,idx,all_dec,a2,x1,og,cwo,wi,wout,cbo,cpg,cpb,fng,fnb,bi,mg,mb,bo)

def head_row(hs_ref,D,H):
    lane=lax.broadcasted_iota(jnp.int32,(1,D),1)//(D//H)
    v=jnp.zeros((1,D),F32)
    for h in range(H): v=jnp.where(lane==h,hs_ref[h],v)
    return v
def cross_back_kernel(hs_ref,gq_ref,x1_ref,gx2_ref,n_ref,inv_ref,gv_ref,cwq,wo,cng,cnb,spg,
                      gx1_o,go1_o,h2_o,gqs_o,gb1_o,v_o):
    @pl.when(pl.program_id(0)==0)
    def _(): v_o[...]=jnp.zeros_like(v_o)
    gq=gq_ref[...]*jnp.asarray(0.125,BF)
    gqs_o[...]=gq
    n,inv=norm_rows(x1_ref[...])
    h2_o[...]=(n*vec(cng)+vec(cnb)).astype(BF)
    gh=nt(gq,cwq[...])
    v_o[0:1]+=col_sum(gh*n); v_o[1:2]+=col_sum(gh)
    v_o[2:3]+=col_sum(gq.astype(F32)); v_o[3:4]+=col_sum(gv_ref[...].astype(F32))
    gx1=gx2_ref[...]+norm_back(gh,n,inv,vec(cng))
    gx1_o[...]=gx1
    nb=n_ref[...].astype(F32)
    v_o[4:5]+=col_sum(gx1*nb); v_o[5:6]+=col_sum(gx1)
    gb1=norm_back(gx1,nb,inv_ref[...],vec(spg)).astype(BF)
    gb1_o[...]=gb1
    v_o[6:7]+=col_sum(gb1.astype(F32))
    go1_o[...]=(nt(gb1,wo[...])*head_row(hs_ref,gb1.shape[1],hs_ref.shape[0])).astype(BF)

def cross_back(hs,gq,x1,gx2,n,inv,gv,cwq,wo,cng,cnb,spg,T=256):
    S,D=x1.shape
    r=rows_of(T,D); w=whole((D,D)); u=whole((D,))
    sd=jax.ShapeDtypeStruct
    return pl.pallas_call(cross_back_kernel,grid=(S//T,),in_specs=[SMEM,r,r,r,r,rows_of(T,1),r,w,w,u,u,u],
        out_specs=[r,r,r,r,r,pl.BlockSpec((8,D),lambda *_:(0,0))],
        out_shape=[sd((S,D),F32)]+[sd((S,D),BF)]*4+[sd((8,D),F32)],
        compiler_params=params(1),name="cross_back",cost_estimate=cost(4*S*D*D,4*D*D+28*S*D))(hs,gq,x1,gx2,n,inv,gv,cwq,wo,cng,cnb,spg)

PLACE=(15,16,13,14,12,10,11,6,7,8,9,5,3,4,0,1,2)
WIDE_ROW=17; BUCKET_LANE=32; HEAD_LANE=64
def tail_kernel(n,core_ref,fac_ref,hs_ref,x_ref,gx1_ref,gq_ref,gk_ref,gv_ref,wq,wk,wv,g_ref,b_ref,va,vb,vf,gb,ds,
                gt_o,h_o,gqs_o,keep_o,send_o,v_s,f_s,p_s,t_s):
    D=x_ref.shape[1]; H=hs_ref.shape[0]; FF=vf.shape[1]
    step=pl.program_id(0)
    @pl.when(step==0)
    def _():
        v_s[...]=jnp.zeros_like(v_s); f_s[...]=jnp.zeros_like(f_s); p_s[...]=jnp.zeros_like(p_s)
        v_s[0:6,0:D]=va[0:6]
        v_s[6:13,0:D]=vb[0:7]
        f_s[1:4,0:FF]=vf[0:3]
        for h in range(H): p_s[h:h+1]=gb[h//2,h%2:h%2+1,:]
    n_x,inv=norm_rows(x_ref[...].astype(F32))
    h_o[...]=(n_x*vec(g_ref)+vec(b_ref)).astype(BF)
    gq=gq_ref[...]*jnp.asarray(0.125,BF)
    gqs_o[...]=gq
    gh=nt(gq,wq[...])+nt(gk_ref[...],wk[...])+nt(gv_ref[...],wv[...])
    v_s[13:14,0:D]+=col_sum(gq.astype(F32)); v_s[14:15,0:D]+=col_sum(gv_ref[...].astype(F32))
    v_s[15:16,0:D]+=col_sum(gh*n_x); v_s[16:17,0:D]+=col_sum(gh)
    gt_o[...]=gx1_ref[...]+norm_back(gh,n_x,inv,vec(g_ref))
    @pl.when(step==pl.num_programs(0)-1)
    def _():
        fac=fac_ref[0:1,0:1]
        w=D//n; f=FF//n; b=256//n
        row=lax.broadcasted_iota(jnp.int32,(24,128),0); lane=lax.broadcasted_iota(jnp.int32,(24,128),1)
        heads=jnp.zeros((24,128),F32)
        for h in range(H):
            heads=jnp.where((row==h)&(lane==HEAD_LANE),ds[h//2,h%2:h%2+1,:]*(1.0/jnp.full((1,1),hs_ref[h],F32)),heads)
        def window(ref,rows,at):
            lo=at//128*128
            v=ref[0:rows,lo:lo+256]
            return v if at==lo else pltpu.roll(v,256-(at-lo),1)
        for dev in range(n):
            t=jnp.where(lane<w,window(v_s,24,w*dev)[:,:128],heads)
            p=pltpu.roll(p_s[...],(256-b*dev+BUCKET_LANE)%256,1)[:,:128]
            p=jnp.where((lane[:16]>=BUCKET_LANE)&(lane[:16]<BUCKET_LANE+b),p,t[0:16])
            u=t[16:24]+jnp.where((lane[:8]<f)&(row[:8]>0)&(row[:8]<4),window(f_s,8,f*dev)[:,:128],0.0)
            t_s[dev,0:16]=p*fac
            t_s[dev,16:24]=u*fac
        core=core_ref[0]
        for k in range(n//2):
            keep_o[k]=t_s[2*k+core]
            send_o[k]=t_s[2*k+1-core]
def tail(n,core,fac,hs,x,gx1,gq,gk,gv,wq,wk,wv,g,b,va,vb,vf,gb,ds,T=256):
    S,D=x.shape; FF=vf.shape[1]
    r=rows_of(T,D); w=whole((D,D)); u=whole((D,)); sd=jax.ShapeDtypeStruct
    tile=pl.BlockSpec((n//2,24,128),lambda *_:(0,0,0))
    return pl.pallas_call(functools.partial(tail_kernel,n),grid=(S//T,),
        in_specs=[SMEM,whole((8,128)),SMEM]+[r]*5+[w]*3+[u]*2+[whole(v.shape) for v in (va,vb,vf,gb,ds)],
        out_specs=[r,r,r,tile,tile],
        out_shape=[sd((S,D),F32),sd((S,D),BF),sd((S,D),BF),sd((n//2,24,128),F32),sd((n//2,24,128),F32)],
        scratch_shapes=[pltpu.VMEM((24,D+128),F32),pltpu.VMEM((8,FF+128),F32),pltpu.VMEM((16,256),F32),pltpu.VMEM((n,24,128),F32)],
        compiler_params=params(1),name="tail",cost_estimate=cost(1000,1000))(core,fac,hs,x,gx1,gq,gk,gv,wq,wk,wv,g,b,va,vb,vf,gb,ds)
def memory_kernel(k_ref,v_ref,ck,cv,o):
    o[...]=nt(k_ref[...],ck[...])+nt(v_ref[...],cv[...])
def memory_grad(gk,gv,ck,cv,T=256):
    S,D=gk.shape
    r=rows_of(T,D); w=whole((D,D))
    return pl.pallas_call(memory_kernel,grid=(S//T,),in_specs=[r,r,w,w],out_specs=r,out_shape=jax.ShapeDtypeStruct((S,D),F32),
        compiler_params=params(1),name="memory",cost_estimate=cost(4*S*D*D,4*D*D+S*D*8))(gk,gv,ck,cv)

def part_rows(scr,core,keep_o,send_o):
    groups,r=keep_o.shape[:2]
    for t in range(groups):
        if r%8==0:
            keep_o[t]=scr[pl.ds((2*t+core)*r,r),:]
            send_o[t]=scr[pl.ds((2*t+1-core)*r,r),:]
        else:
            even=scr[2*t*r:(2*t+1)*r,:]
            odd=scr[(2*t+1)*r:(2*t+2)*r,:]
            keep_o[t]=jnp.where(core==0,even,odd)
            send_o[t]=jnp.where(core==0,odd,even)
def wrow_kernel(core_ref,fac_ref,l_ref,r_ref,keep_o,send_o,scr):
    scr[...]=tn(l_ref[...],r_ref[...])*fac_ref[0:1,0:1]
    part_rows(scr,core_ref[0],keep_o,send_o)
def wgrad_rows(core,fac,lhs,rhs,n,B=768):
    S,M=lhs.shape; N=rhs.shape[1]; r=M//n; steps=M//B; groups=B//r//2
    o=pl.BlockSpec((groups,r,N),lambda i:(i,0,0)); sh=jax.ShapeDtypeStruct((n//2,r,N),F32)
    return pl.pallas_call(wrow_kernel,grid=(steps,),
        in_specs=[SMEM,whole((8,128)),pl.BlockSpec((S,B),lambda i:(0,i)),whole((S,N))],
        out_specs=[o,o],scratch_shapes=[pltpu.VMEM((B,N),F32)],out_shape=[sh,sh],compiler_params=params(1),name="wgrad",
        cost_estimate=cost(4*S*M*N,2*S*(M+N)+4*M*N))(core,fac,lhs,rhs)
def wcol_kernel(plan,core_ref,fac_ref,*refs):
    ins=refs[:-3]; keep_o,send_o,scr=refs[-3:]
    step=pl.program_id(0)
    for l,r,first,last in plan:
        @pl.when((step>=first)&(step<last))
        def _(): scr[...]=tn(ins[l][...],ins[r][...])*fac_ref[0:1,0:1]
    part_rows(scr,core_ref[0],keep_o,send_o)
def wgrad_cols(core,fac,pairs,n,B=768,weight=1.0):
    ins=[]; specs=[]; plan=[]; at=0; seen={}
    S,M=pairs[0][0].shape
    for lhs,rhs in pairs:
        if id(lhs) not in seen:
            seen[id(lhs)]=len(ins); ins.append(lhs); specs.append(whole((S,M)))
        steps=rhs.shape[1]//B
        plan.append((seen[id(lhs)],len(ins),at,at+steps))
        ins.append(rhs)
        specs.append(pl.BlockSpec((S,B),functools.partial(lambda at,steps,i:(0,jnp.clip(i-at,0,steps-1)),at,steps)))
        at+=steps
    N=at*B; r=M//n
    o=pl.BlockSpec((n//2,r,B),lambda i:(0,0,i)); sh=jax.ShapeDtypeStruct((n//2,r,N),F32)
    return pl.pallas_call(functools.partial(wcol_kernel,plan),grid=(at,),in_specs=[SMEM,whole((8,128))]+specs,
        out_specs=[o,o],scratch_shapes=[pltpu.VMEM((M,B),F32)],out_shape=[sh,sh],compiler_params=params(1),name="wgrad",
        cost_estimate=cost(4*S*M*N*weight,(2*S*M*len(ins)+4*M*N)*weight))(core,fac,*ins)

def halve_kernel(count,bit_ref,*refs):
    for c in range(count):
        km,ko,gm,go=refs[4*c:4*c+4]
        keep_o,send_o=refs[4*count+2*c:4*count+2*c+2]
        send_o[...]=ko[:,0]+go[:,0]
        keep_o[...]=km[:,0]+gm[:,0]
def halve(bits,chains):
    specs=[];ins=[];outs=[];shapes=[]
    size=sum(4*keep.size//parts for keep,got,part,parts in chains)
    steps=min([4 if size>8e6 else 2 if size>3e6 else 1]+[keep.shape[0] for keep,*_ in chains])
    for c,(keep,got,part,parts) in enumerate(chains):
        A,_,B,r,C=keep.shape
        C=C//parts; K=A//steps
        for flip in (False,True,False,True):
            specs.append(pl.BlockSpec((K,1,B,r,C),functools.partial(lambda c,flip,part,i,b:(i,1-b[c] if flip else b[c],0,0,part),c,flip,part)))
        ins+=[keep,keep,got,got]
        outs+=[pl.BlockSpec((K,B,r,C),lambda i,b:(i,0,0,0))]*2
        shapes+=[jax.ShapeDtypeStruct((A,B,r,C),F32)]*2
    gs=pltpu.PrefetchScalarGridSpec(num_scalar_prefetch=1,grid=(steps,),in_specs=specs,out_specs=outs)
    return pl.pallas_call(functools.partial(halve_kernel,len(chains)),grid_spec=gs,out_shape=shapes,compiler_params=params(1),name="halve",
        cost_estimate=cost(1000,1000))(bits,*ins)

def deal_kernel(count,z_ref,*refs):
    outs=refs[8*count:]
    for m,o in enumerate(outs):
        at=0
        for c in range(count):
            k,g=refs[8*c+m],refs[8*c+4+m]
            o[:,at:at+k.shape[-1]]=k[0]+g[0]
            at+=k.shape[-1]
def deal(z,chains):
    r=chains[0][0].shape[1]; C=sum(k.shape[2] for k,_ in chains)
    specs=[];ins=[]
    for k,g in chains:
        specs+=[pl.BlockSpec((1,r,k.shape[2]),lambda i,z,m=m:(z[0]^m,0,0)) for m in range(4)]*2
        ins+=[k]*4+[g]*4
    o=pl.BlockSpec((r,C),lambda i,z:(0,0)); sh=jax.ShapeDtypeStruct((r,C),F32)
    gs=pltpu.PrefetchScalarGridSpec(num_scalar_prefetch=1,grid=(1,),in_specs=specs,out_specs=[o]*4)
    return pl.pallas_call(functools.partial(deal_kernel,len(chains)),grid_spec=gs,out_shape=[sh]*4,compiler_params=params(1),name="deal",
        cost_estimate=cost(1000,1000))(z,*ins)

def finish_kernel(n,plan,tile,*refs):
    count=len(plan)+22
    ins=refs[:-count]; outs=refs[-count:]
    total=lambda c,lo,hi: (ins[4*c][:,lo:hi]+ins[4*c+1][:,lo:hi])+(ins[4*c+2][:,lo:hi]+ins[4*c+3][:,lo:hi])
    for o,(c,lo,hi) in zip(outs,plan):
        o[...]=total(c,lo,hi)
    t=total(*tile)
    outs=outs[len(plan):]
    for r,o in zip(PLACE,outs): o[...]=t[r:r+1,:o.shape[0]].reshape(o.shape[0])
    for k in range(3):
        o=outs[17+k]
        o[...]=t[WIDE_ROW+k:WIDE_ROW+k+1,:o.shape[0]].reshape(o.shape[0])
    H,b=outs[20].shape
    outs[20][...]=pltpu.roll(t,128-BUCKET_LANE,1)[:H,:b]
    x=pltpu.roll(t,128-HEAD_LANE,1)[0:16,0:1]
    eye=lax.broadcasted_iota(jnp.int32,(16,128),0)==lax.broadcasted_iota(jnp.int32,(16,128),1)
    outs[21][...]=col_sum(jnp.where(eye,x,0.0))[:,:H].reshape(H)
def finish(n,groups,plan,tile,D,FF,H):
    ins=[v for g in groups for v in g]
    sd=jax.ShapeDtypeStruct
    shapes=[sd((ins[4*c].shape[0],hi-lo),F32) for c,lo,hi in plan]+[sd((D//n,),F32)]*17+[sd((FF//n,),F32)]*3+[sd((H,256//n),F32),sd((H,),F32)]
    return pl.pallas_call(functools.partial(finish_kernel,n,plan,tile),in_specs=[pl.BlockSpec(v.shape) for v in ins],out_shape=shapes,
        compiler_params=params(0),name="finish",cost_estimate=cost(1000,1000))(*ins)

def swap(x,n,bit):
    return lax.ppermute(x,"dp",[(j,j^(1<<bit)) for j in range(n)])
def after(token,*vals):
    return lax.optimization_barrier(tuple(vals)+tuple(token))[:len(vals)]
class Halving:
    def __init__(self,n,keep,send,order):
        self.n,self.order=n,list(order)
        self.live=list(range(n.bit_length()-2,0,-1))
        self.keep=keep; self.got=swap(send,n,0); self.part=(0,1)
    def split(self,orders):
        chains=[]
        for k,order in enumerate(orders):
            h=object.__new__(Halving)
            h.n,h.order,h.live=self.n,list(order),list(self.live)
            h.keep,h.got,h.part=self.keep,self.got,(k,len(orders))
            chains.append(h)
        return chains
def step(token,index,*chains):
    bits=[];work=[]
    flat=after(token,*[v for c in chains for v in (c.keep,c.got)])
    for k,c in enumerate(chains):
        b=c.order.pop(0)
        axis=c.live.index(b)
        c.live.remove(b)
        keep,got=flat[2*k:2*k+2]
        shape=(2**axis,2,2**(len(c.live)-axis))+keep.shape[-2:]
        bits.append((b,(index>>b)&1))
        work.append((keep.reshape(shape),got.reshape(shape))+c.part)
    outs=halve(jnp.stack([v for _,v in bits]).astype(jnp.int32),work)
    for k,c in enumerate(chains):
        c.keep,c.part=outs[2*k],(0,1)
        c.got=swap(outs[2*k+1],c.n,bits[k][0])
    return [outs[2*k+1] for k in range(len(chains))]
def last_step(token,index,zs,*chains):
    flat=after(token,*[v for c in chains for v in (c.keep,c.got)])
    z=((index>>zs[0])&3).reshape(1).astype(jnp.int32)
    cut=lambda v: v.reshape((4,)+v.shape[-2:])
    own,*sends=deal(z,[(cut(flat[2*k]),cut(flat[2*k+1])) for k in range(len(chains))])
    n=chains[0].n
    return [own]+[lax.ppermute(s,"dp",[(j,j^((m+1)<<zs[0])) for j in range(n)]) for m,s in enumerate(sends)]

def shards(n,tokens,memory,out_grad,dec_len,mem_len,group_bounds,
           self_norm_gain,self_norm_bias,self_query,self_query_bias,self_key,self_value,self_value_bias,self_output,self_output_bias,
           position_bias,head_scale,self_post_gain,self_post_bias,cross_norm_gain,cross_norm_bias,cross_query,cross_query_bias,
           cross_key,cross_value,cross_value_bias,cross_output,cross_output_bias,cross_post_gain,cross_post_bias,
           feed_norm_gain,feed_norm_bias,feed_inner,feed_inner_bias,feed_mid_gain,feed_mid_bias,feed_outer,feed_outer_bias):
    bits=n.bit_length()-1
    xs,ys,zs=([1],[2],[3,4]) if bits==5 else ([1,2],[3,4],list(range(5,bits)))
    order_a=xs+ys; order_b=ys+xs
    index=lax.axis_index("dp")
    idx=index.reshape(1).astype(jnp.int32)
    core=idx&1
    x=tokens[0]; m=memory[0]; og=out_grad[0]
    S,D=x.shape
    H=head_scale.shape[0]; pairs=H//2
    all_dec=lax.all_to_all(jnp.broadcast_to(dec_len.astype(F32).reshape(1,1,1),(n,8,128)),"dp",0,0,tiled=True)
    q1,k1,v1,k2,v2=pre(x,m,self_norm_gain,self_norm_bias,self_query,self_query_bias,self_key,self_value,self_value_bias,cross_key,cross_value,cross_value_bias)
    a1,lse1=attn_fwd(True,dec_len,head_scale,position_bias,q1,k1,v1)
    x1,q2,nb1,ib1=post(a1,x,self_output,self_output_bias,self_post_gain,self_post_bias,cross_norm_gain,cross_norm_bias,cross_query,cross_query_bias)
    a2,lse2=attn_fwd(False,mem_len,head_scale,position_bias,q2,k2,v2)
    lo,gx2,go2,u,gf,h3,g3,gb2,va,vf,fac=mid(n,dec_len,group_bounds,idx,all_dec,a2,x1,og,cross_output,feed_inner,feed_outer,cross_output_bias,cross_post_gain,cross_post_bias,feed_norm_gain,feed_norm_bias,feed_inner_bias,feed_mid_gain,feed_mid_bias,feed_outer_bias)
    keep,send=wgrad_cols(core,fac,[(h3,gf),(a2,gb2)],n)
    fi=Halving(n,keep,send,order_b)
    u,=after([send],u)
    keep,send=wgrad_rows(core,fac,u,g3,n)
    fo=Halving(n,keep,send,order_a)
    t=step([send],index,fi)
    t=step(t,index,fo)
    go2,=after(t,go2)
    gq2,gk2,gv2,_=attn_bwd(False,mem_len,head_scale,position_bias,q2,k2,v2,go2,a2,lse2,0,pairs)
    gx1,go1,h2,gqs2,gb1,vb=cross_back(head_scale,gq2,x1,gx2,nb1,ib1,gv2,cross_query,self_output,cross_norm_gain,cross_norm_bias,self_post_gain)
    t=step([vb],index,fo)
    h2,=after(t,h2)
    keep,send=wgrad_cols(core,fac,[(h2,gqs2),(m,gv2),(m,gk2),(a1,gb1)],n)
    g2=Halving(n,keep,send,[])
    t=step([send],index,fi)
    go1,=after(t,go1)
    half=pairs//2
    back=attn_bwd(True,dec_len,head_scale,position_bias,q1,k1,v1,go1,a1,lse1,0,half)
    t=[back[3]]
    while fo.order: t=step(t,index,fo)
    r_fo=last_step(t,index,zs,fo)
    ga,gb_=g2.split([order_a,order_b])
    t=step([r_fo[0]],index,ga,gb_)
    go1,=after(t,go1)
    gq1,gk1,gv1,ds,gb=attn_bwd(True,dec_len,head_scale,position_bias,q1,k1,v1,go1,a1,lse1,half,pairs-half,back)
    t=[ds]
    while fi.order: t=step(t,index,fi)
    r_fi=last_step(t,index,zs,fi)
    gx1,=after([r_fi[0]],gx1)
    gt,h1,gqs1,keep,send=tail(n,core,fac,head_scale,x,gx1,gq1,gk1,gv1,self_query,self_key,self_value,self_norm_gain,self_norm_bias,va,vb,vf,gb,ds)
    sv=Halving(n,keep,send,order_a)
    h1,=after([send,ga.got,gb_.got]+r_fo[1:],h1)
    keep,send=wgrad_cols(core,fac,[(h1,gqs1),(h1,gv1),(h1,gk1)],n)
    g3_=Halving(n,keep,send,[])
    t=[send]
    while ga.order: t=step(t,index,ga,gb_)
    sa,sb=g3_.split([order_a,order_b])
    t=step(t,index,sa,sb,sv)
    gk2,=after(t+r_fi[1:],gk2)
    gm=memory_grad(gk2,gv2,cross_key,cross_value)
    r_g2=last_step([gm],index,zs,ga,gb_)
    t=r_g2[:1]
    while sa.order: t=step(t,index,sa,sb,sv)
    t=t+r_g2[1:]
    FF=feed_inner.shape[1]
    if sv.keep.shape[-2]==sa.keep.shape[-2]:
        groups=[last_step(t,index,zs,sa,sb,sv)]
        tile=(3,3*D,3*D+128)
    else:
        groups=[last_step(t,index,zs,sa,sb),last_step(t,index,zs,sv)]
        tile=(4,0,128)
    g_fo,g_fi,g_co,g_cq,g_cv,g_ck,g_so,g_sq,g_sv,g_sk,*small=finish(n,[r_fo,r_fi,r_g2]+groups,[
        (0,0,D),(1,0,FF),(1,FF,FF+D),(2,0,D),(2,D,2*D),(2,2*D,3*D),(2,3*D,4*D),(3,0,D),(3,D,2*D),(3,2*D,3*D)],tile,D,FF,H)
    (sng,snb,sqb,svb,sob,spg,spb,cng,cnb,cqb,cvb,cob,cpg,cpb,fng,fnb,fob,fmg,fmb,fib,gpos,ghs)=small
    fo_b=fob
    return (lo[None],gt[None],gm[None],
        sng,snb,g_sq,sqb,g_sk,g_sv,svb,g_so,sob,gpos,ghs,spg,spb,cng,cnb,g_cq,cqb,g_ck,g_cv,cvb,g_co,cob,cpg,cpb,
        fng,fnb,g_fi,fib,fmg,fmb,g_fo,fo_b)

def solution(mesh):
    n=mesh.shape["dp"]
    vec=P("dp"); mat=P("dp",None); cube=P("dp",None,None)
    return jax.shard_map(functools.partial(shards,n),mesh=mesh,in_specs=(cube,cube,cube,vec,vec)+(P(),)*33,
        out_specs=(cube,cube,cube,vec,vec,mat,vec,mat,mat,vec,mat,vec,P(None,"dp"),P(),vec,vec,vec,vec,mat,vec,
                   mat,mat,vec,mat,vec,vec,vec,vec,vec,mat,vec,vec,vec,mat,vec),check_vma=False)
```
